32 devices in a mesh: shard: 8 (over z, x), seq: 4 (over y, core).
Axes of the slice: x: 2, y: 2, z: 4, core: 2. Of those that a mesh axis runs over, the one named last changes fastest.
Arguments:
- inputs: bfloat16 [16, 512, 768], P('shard', 'seq'), may hold values from -6 to 6
- lengths: int32 [16], P('shard'), may hold values from 128 to 512, as said below
- w_query: bfloat16 [768, 768], P('shard'), may hold values from -0.21875 to 0.21875
- b_query: bfloat16 [768], P('shard'), may hold values from -3 to 3
- w_key: bfloat16 [768, 768], P('shard'), may hold values from -0.21875 to 0.21875
- w_value: bfloat16 [768, 768], P('shard'), may hold values from -0.21875 to 0.21875
- b_value: bfloat16 [768], P('shard'), may hold values from -2 to 2
- w_output: bfloat16 [768, 768], P('shard'), may hold values from -0.875 to 0.875
- b_output: bfloat16 [768], P('shard'), may hold values from -2 to 2
- gain_one: bfloat16 [768], P('shard'), may hold values from 0.25 to 1.75
- shift_one: bfloat16 [768], P('shard'), may hold values from -2 to 2
- w_inner: bfloat16 [768, 3072], P('shard'), may hold values from -0.21875 to 0.21875
- b_inner: bfloat16 [3072], P('shard'), may hold values from -2 to 2
- w_outer: bfloat16 [3072, 768], P('shard'), may hold values from -0.109375 to 0.109375
- b_outer: bfloat16 [768], P('shard'), may hold values from -2 to 2
- gain_two: bfloat16 [768], P('shard'), may hold values from 0.25 to 1.75
- shift_two: bfloat16 [768], P('shard'), may hold values from -2 to 2
- cotangent: bfloat16 [16, 512, 768], P('shard', 'seq'), may hold values from -6 to 6
Outputs:
- output: bfloat16 [16, 512, 768], P('shard', 'seq')
- grad_inputs: float32 [16, 512, 768], P('shard', 'seq')
- grad_w_query: float32 [768, 768], P('shard')
- grad_b_query: float32 [768], P('shard')
- grad_w_key: float32 [768, 768], P('shard')
- grad_w_value: float32 [768, 768], P('shard')
- grad_b_value: float32 [768], P('shard')
- grad_w_output: float32 [768, 768], P('shard')
- grad_b_output: float32 [768], P('shard')
- grad_gain_one: float32 [768], P('shard')
- grad_shift_one: float32 [768], P('shard')
- grad_w_inner: float32 [768, 3072], P('shard')
- grad_b_inner: float32 [3072], P('shard')
- grad_w_outer: float32 [3072, 768], P('shard')
- grad_b_outer: float32 [768], P('shard')
- grad_gain_two: float32 [768], P('shard')
- grad_shift_two: float32 [768], P('shard')
The draws below stay inside these ranges and needn't reach their ends.
Inputs may be any that keep to these rules, and one draw needn't show every extreme that they name: `lengths`: every draw has a slot of 512 valid tokens and a slot of 128.
All inputs are finite; a program needn't handle non-finite values.
Results may differ from the reference program's by a relative error of at most 0.017.
Values may be sent and summed in bfloat16 or wider, within the bound.
A program may use at most 128 MiB of HBM per device.

```python
import jax
import jax.numpy as jnp
from jax import lax

D = 768
H = 12
FF = 3072
HEAD_DIM = 64
SEQ = 512
SLOTS = 16


def draw_lengths(key, part):
    key_one, key_two, key_three = jax.random.split(key, 3)
    lowest = SEQ // 4
    lengths_drawn = jax.random.randint(key_one, (SLOTS,), lowest, SEQ + 1)
    longest = jax.random.randint(key_two, (), 0, SLOTS)
    offset = jax.random.randint(key_three, (), 1, max(SLOTS, 2))
    shortest = (longest + offset) % SLOTS
    lengths_drawn = lengths_drawn.at[longest].set(SEQ)
    lengths_drawn = lengths_drawn.at[shortest].set(lowest)
    return lengths_drawn.astype(jnp.int32)


def with_spikes(values, key, source, target, blocks, factor):
    def block_of(dim):
        return (jnp.arange(values.shape[dim]) // (values.shape[dim] // blocks)).reshape((-1,) + (1,) * (values.ndim - 1 - dim))

    near = jax.random.permutation(key, blocks)[block_of(target)]
    far = (block_of(target) + blocks // 2) % blocks
    return jnp.where((block_of(source) == near) | (block_of(source) == far), factor * values, values)


def level_of(key, shape, pieces, smallest, largest):
    def one(dim, shards_of):
        draws = jax.random.uniform(jax.random.fold_in(jax.random.fold_in(key, 6), dim), (shards_of,), jnp.float32, smallest / len(pieces), largest / len(pieces))
        return jnp.repeat(jnp.exp(draws), shape[dim] // shards_of).reshape((-1,) + (1,) * (len(shape) - dim - 1))

    level = one(*pieces[0])
    for cut in pieces[1:]:
        level = level * one(*cut)
    return level


def scatter_about(key, shape, scale, bound, shards=(), held_as=jnp.bfloat16):
    loudness = level_of(key, shape, shards, -0.22, 0.18) if shards else 1.0
    array = jax.random.normal(key, shape, jnp.float32) * scale * loudness
    return jnp.minimum(jnp.maximum(array, -bound), bound).astype(held_as)


def heavy_noise(key, dims, spread, bound, cuts, heavy, held_as=jnp.bfloat16):
    drawn = spread * jax.random.normal(key, dims, jnp.float32)
    if cuts:
        drawn = drawn * level_of(key, dims, cuts, -0.22, 0.18)
    return jnp.clip(with_spikes(drawn, jax.random.fold_in(key, 3), *heavy), -bound, bound).astype(held_as)


def setup_inputs(seed: int = 0) -> dict:
    key_list = jax.random.split(jax.random.key(seed), 19)
    return {
        "inputs": scatter_about(key_list[0], (SLOTS, SEQ, D), 1.0, 6.0, ((0, 8), (1, 4))),
        "lengths": draw_lengths(jax.random.fold_in(key_list[18], 71), 0),
        "w_query": scatter_about(key_list[2], (D, D), D ** -0.5, 0.21875, ((0, 8),)),
        "b_query": scatter_about(key_list[3], (D,), 0.5, 3.0, ((0, 8),)),
        "w_key": scatter_about(key_list[4], (D, D), D ** -0.5, 0.21875, ((0, 8),)),
        "w_value": scatter_about(key_list[5], (D, D), D ** -0.5, 0.21875, ((0, 8),)),
        "b_value": scatter_about(key_list[6], (D,), 0.3, 2.0, ((0, 8),)),
        "w_output": scatter_about(key_list[7], (D, D), (D // 16) ** -0.5, 0.875, ((0, 8),)),
        "b_output": scatter_about(key_list[8], (D,), 0.3, 2.0, ((0, 8),)),
        "gain_one": jnp.clip(1.0 + 0.15 * jax.random.normal(key_list[9], (D,), jnp.float32), 0.25, 1.75).astype(jnp.bfloat16),
        "shift_one": scatter_about(key_list[10], (D,), 0.3, 2.0, ((0, 8),)),
        "w_inner": scatter_about(key_list[11], (D, FF), D ** -0.5, 0.21875, ((0, 8),)),
        "b_inner": scatter_about(key_list[12], (FF,), 0.3, 2.0, ((0, 8),)),
        "w_outer": scatter_about(key_list[13], (FF, D), FF ** -0.5, 0.109375, ((0, 8),)),
        "b_outer": scatter_about(key_list[14], (D,), 0.3, 2.0, ((0, 8),)),
        "gain_two": jnp.clip(1.0 + 0.15 * jax.random.normal(key_list[15], (D,), jnp.float32), 0.25, 1.75).astype(jnp.bfloat16),
        "shift_two": scatter_about(key_list[16], (D,), 0.3, 2.0, ((0, 8),)),
        "cotangent": heavy_noise(key_list[17], (SLOTS, SEQ, D), 1.0, 6.0, ((0, 8), (1, 4)), (0, 2, 8, 2.0)),
    }


@jax.custom_vjp
def low(v):
    return lax.optimization_barrier(v.astype(jnp.bfloat16)).astype(jnp.float32)

@jax.custom_vjp
def low_back(v):
    return v

def low_keep(v):
    return (low(v), None)

def low_pass(kept, grad):
    return (grad,)

def back_keep(v):
    return (v, None)

def back_low(kept, grad):
    return (low(grad),)
low.defvjp(low_keep, low_pass)
low_back.defvjp(back_keep, back_low)
highest = lax.Precision.HIGHEST
epsilon = 1e-12

def layer_norm(tensor, norm_gain, norm_shift):
    average = lax.optimization_barrier(jnp.mean(tensor, axis=-1, keepdims=True))
    centred = tensor - average
    variance = lax.optimization_barrier(jnp.mean(centred * centred, axis=-1, keepdims=True))
    return centred * lax.rsqrt(variance + epsilon) * norm_gain + norm_shift

def product(operand, weight):
    return jnp.dot(operand, weight, precision=highest)

def sequence_layer(rows, length, params):
    query_w, query_b, key_w, value_w, value_b, output_w, output_b, gain_a, shift_a, inner_w, inner_b, outer_w, outer_b, gain_b, shift_b = params
    queries = low_back(low(product(rows, query_w) + query_b))
    key_rows = low_back(low(product(rows, key_w)))
    values = low_back(low(product(rows, value_w) + value_b))
    split = (SEQ, H, HEAD_DIM)
    raw_scores = jnp.einsum('qhd,khd->hqk', queries.reshape(split), key_rows.reshape(split), precision=highest) * HEAD_DIM ** (-0.5)
    scores = low_back(raw_scores)
    visible = jnp.arange(SEQ) < length
    logits = jnp.where(visible[None, None, :], scores, -1000000000.0)
    attn_probs = jax.nn.softmax(logits, axis=-1)
    context = jnp.einsum('hqk,khd->qhd', low(attn_probs), values.reshape(split), precision=highest).reshape(SEQ, D)
    context = low_back(low(context))
    branch = low_back(product(context, output_w) + output_b)
    normed = layer_norm(rows + branch, gain_a, shift_a)
    pre_inner = low_back(product(low(normed), inner_w) + inner_b)
    activated = low(jax.nn.gelu(pre_inner, approximate=False))
    ffn_out = low_back(product(activated, outer_w) + outer_b)
    return layer_norm(normed + ffn_out, gain_b, shift_b)

def reference(inputs, lengths, w_query, b_query, w_key, w_value, b_value, w_output, b_output, gain_one, shift_one, w_inner, b_inner, w_outer, b_outer, gain_two, shift_two, cotangent):
    params = (w_query.astype(jnp.float32), b_query.astype(jnp.float32), w_key.astype(jnp.float32), w_value.astype(jnp.float32), b_value.astype(jnp.float32), w_output.astype(jnp.float32), b_output.astype(jnp.float32), gain_one.astype(jnp.float32), shift_one.astype(jnp.float32), w_inner.astype(jnp.float32), b_inner.astype(jnp.float32), w_outer.astype(jnp.float32), b_outer.astype(jnp.float32), gain_two.astype(jnp.float32), shift_two.astype(jnp.float32))

    def whole(rows, weights):

        def per_slot(packed):
            return sequence_layer(packed[0], packed[1], weights)
        return lax.map(jax.checkpoint(per_slot), (rows, lengths))
    result, pullback = jax.vjp(whole, inputs.astype(jnp.float32), params)
    grad_rows, grads = pullback(cotangent.astype(jnp.float32))
    return (result.astype(jnp.bfloat16), grad_rows, grads[0], grads[1], grads[2], grads[3], grads[4], grads[5], grads[6], grads[7], grads[8], grads[9], grads[10], grads[11], grads[12], grads[13], grads[14])
```

```python
from functools import partial
from types import SimpleNamespace

import jax
import jax.numpy as jnp
from jax import lax
from jax.experimental import pallas as pl
from jax.experimental.pallas import tpu as pltpu
from jax.sharding import PartitionSpec as P

HEAD_DIM = 64
BF16, F32 = jnp.bfloat16, jnp.float32
MESH = pl.DeviceIdType.MESH


epsilon = 1e-12


def layer_norm(tensor, norm_gain, norm_shift):
    average = jnp.mean(tensor, axis=-1, keepdims=True)
    centred = tensor - average
    variance = jnp.mean(centred * centred, axis=-1, keepdims=True)
    return centred * lax.rsqrt(variance + epsilon) * norm_gain + norm_shift


def product(operand, weight):
    return jnp.dot(operand, weight, preferred_element_type=jnp.float32)


def row_contract(operand, weight):
    return lax.dot_general(
        operand, weight, (((0,), (0,)), ((), ())), preferred_element_type=jnp.float32
    )


def times_transposed(operand, weight):
    return lax.dot_general(
        operand, weight, (((1,), (1,)), ((), ())), preferred_element_type=jnp.float32
    )


def column_sum(tensor):
    return jnp.sum(tensor.astype(jnp.float32), axis=0)


def place():
    shard, seq = lax.axis_index("shard"), lax.axis_index("seq")
    return shard // 2, lax.rem(shard, 2), seq // 2, lax.rem(seq, 2)


def device(z, x, y, core):
    return (z * 2 + x, y * 2 + core)


def send(src, dst, send_sem, recv_sem, where):
    copy = pltpu.make_async_remote_copy(
        src_ref=src,
        dst_ref=dst,
        send_sem=send_sem,
        recv_sem=recv_sem,
        device_id=where,
        device_id_type=MESH,
    )
    copy.start()
    return copy


def await_bytes(ref, sem):
    pltpu.make_async_copy(ref, ref, sem).wait()


def greet(z, x, y, core):
    barrier = pltpu.get_barrier_semaphore()
    others = [device(lax.rem(z + j, 4), x, y, core) for j in (1, 2, 3)]
    others += [device(z, 1 - x, y, core), device(z, x, 1 - y, core), device(z, x, y, 1 - core)]
    for other in others:
        pl.semaphore_signal(barrier, inc=1, device_id=other, device_id_type=MESH)
    pl.semaphore_wait(barrier, len(others))


def at(start, size):
    return pl.ds(pl.multiple_of(start, size), size)


ITEMS = [(0, 0), (1, 0), (2, 0), (3, 0)] + [(4, i) for i in range(4)] + [(5, i) for i in range(4)]
SIXTH = 16
LEAD = 2
X_STEP = 2
FORWARD_DELAY = (1, 2, 3)
BACKWARD_DELAY = (0, 1, 2, 3, 4, 5)
ROWS = 96


def item_rows(ref, item, shard, start, size):
    which, part = item
    if which < 4:
        return ref.at[at(shard * ROWS + start, size), :]
    if which == 4:
        return ref.at[at(shard * ROWS + start, size), pl.ds(part * 768, 768)]
    return ref.at[at(shard * 4 * ROWS + part * ROWS + start, size), :]


def column(start, width):
    return pl.ds(pl.multiple_of(start, 128), width)


def head_masks():
    lane = lax.broadcasted_iota(jnp.int32, (1, 128), 1)
    low = (lane < HEAD_DIM).astype(F32)
    return (low.astype(BF16), (1.0 - low).astype(BF16))


def vectors(r):
    r.vec[...] = jnp.sum(r.small[...].astype(F32), axis=0)
    for i in range(4):
        r.b_inner[:, i * 768 : i * 768 + 768] = r.vec[5 + i : 6 + i, :]


def project_one(r, name):
    own = at(r.seq * 128, 128)
    for slot in range(2):

        @pl.loop(0, 3)
        def _(c):
            cols = column(c * 256, 256)
            if name == "q":
                r.q[slot, :, cols] = (product(r.x[slot, own, :], r.w_q[:, cols]) + r.vec[0:1, cols]).astype(BF16)
            elif name == "k":
                r.k[slot, :, cols] = product(r.x[slot], r.w_k[:, cols]).astype(BF16)
            else:
                r.v[slot, :, cols] = (product(r.x[slot], r.w_v[:, cols]) + r.vec[1:2, cols]).astype(BF16)


def attend(r, slot, first, last):
    masks = head_masks()
    visible = lax.broadcasted_iota(jnp.int32, (512, 128), 0) < r.lengths[slot]

    @pl.loop(first, last)
    def _(p):
        cols = column(p * 128, 128)
        k, q, v = r.k[slot, :, cols], r.q[slot, :, cols], r.v[slot, :, cols]
        context = None
        for h in range(2):
            scores = times_transposed(k, q * masks[h]) * (HEAD_DIM**-0.5)
            logits = jnp.where(visible, scores, -1000000000.0)
            shifted = jnp.exp(logits - jnp.max(logits, axis=0, keepdims=True))
            probs = shifted * (1.0 / jnp.sum(shifted, axis=0, keepdims=True))
            low = probs.astype(BF16)
            r.p[slot, p * 2 + h] = low
            part = row_contract(low, v * masks[h])
            context = part if context is None else context + part
        r.c[slot, :, cols] = context.astype(BF16)


def norm_stats(rows):
    average = jnp.mean(rows, axis=-1, keepdims=True)
    centred = rows - average
    variance = jnp.mean(centred * centred, axis=-1, keepdims=True)
    scale = lax.rsqrt(variance + epsilon)
    return centred * scale, scale


def norm_back(grad, gain, unit, scale):
    g = grad * gain
    return scale * (
        g - jnp.mean(g, axis=-1, keepdims=True) - unit * jnp.mean(g * unit, axis=-1, keepdims=True)
    )


def first_norm(r):
    for slot in range(2):
        rows = pl.ds(slot * 128, 128)
        h1 = r.x[slot, at(r.seq * 128, 128), :].astype(F32) + product(r.c[slot], r.w_o[...]) + r.vec[2:3, :]
        unit, scale = norm_stats(h1)
        r.unit_one[rows, :] = unit
        r.scale_one[rows, :] = jnp.broadcast_to(scale, (128, 128))
        n1 = unit * r.vec[3:4, :] + r.vec[4:5, :]
        r.n1[rows, :] = n1
        r.n1b[rows, :] = n1.astype(BF16)


def feed_in(r, i):
    @pl.loop(0, 3)
    def _(c):
        cols = column(i * 768 + c * 256, 256)
        u = product(r.n1b[...], r.w_inner[:, cols]) + r.b_inner[:, cols]
        phi = 0.5 * (1.0 + lax.erf(u * 0.7071067811865476))
        r.g[:, cols] = (u * phi).astype(BF16)
        r.slope[:, cols] = (phi + u * (0.3989422804014327 * jnp.exp(-0.5 * u * u))).astype(BF16)


def second_norm(r):
    for slot in range(2):
        rows = pl.ds(slot * 128, 128)
        h2 = r.n1[rows, :] + product(r.g[rows, :], r.w_outer[...]) + r.vec[9:10, :]
        unit, scale = norm_stats(h2)
        r.result[slot] = (unit * r.vec[10:11, :] + r.vec[11:12, :]).astype(BF16)
        grad = r.cot[slot].astype(F32)
        back = norm_back(grad, r.vec[10:11, :], unit, scale)
        low = back.astype(BF16)
        r.dh2[rows, :] = back
        r.df[rows, :] = low
        tally(r, slot, 10, grad * unit)
        tally(r, slot, 11, grad)
        tally(r, slot, 9, low.astype(F32))


def tally(r, slot, row, values):
    total = jnp.sum(values, axis=0, keepdims=True)
    r.sums[row : row + 1, :] = total if slot == 0 else r.sums[row : row + 1, :] + total


KINDS = {
    "place": ((16, 768), F32),
    "small_own": ((16, 768), BF16),
    "small": ((8, 16, 768), BF16),
    "b_inner": ((1, 3072), F32),
    "x": ((2, 512, 768), BF16),
    "q": ((2, 128, 768), BF16),
    "k": ((2, 512, 768), BF16),
    "v": ((2, 512, 768), BF16),
    "p": ((2, 12, 512, 128), BF16),
    "c": ((2, 128, 768), BF16),
    "unit_one": ((256, 768), F32),
    "scale_one": ((256, 128), F32),
    "n1": ((256, 768), F32),
    "n1b": ((256, 768), BF16),
    "g": ((256, 3072), BF16),
    "slope": ((256, 3072), BF16),
    "dh2": ((256, 768), F32),
    "df": ((256, 768), BF16),
    "da": ((2, 128, 768), BF16),
    "dc": ((2, 128, 768), BF16),
    "dq": ((2, 128, 768), BF16),
    "dk": ((2, 512, 768), BF16),
    "dv": ((2, 512, 768), BF16),
    "dx_own": ((2, 128, 768), F32),
    "dx_part": ((2, 512, 768), BF16),
    "sums": ((16, 768), F32),
    "ring": ((4, 768, 768), BF16),
}


def kinds(*names):
    return {name: KINDS[name] for name in names}


VECTOR_ROWS = (0, 1, 2, 3, 4, None, 9, 10, 11)
HANDED = ("x", "q", "k", "v", "p", "c", "unit_one", "scale_one", "n1b", "g", "slope", "dh2", "df")

FORWARD_WORK = kinds(
    "place", "small_own", "small", "b_inner", "x", "q", "k", "v", "p", "c", "unit_one", "scale_one", "n1", "n1b", "g",
    "slope", "dh2", "df",
)

def place_vectors(r, shard):
    r.place[...] = jnp.zeros_like(r.place)
    for row, ref in zip(VECTOR_ROWS, r.vectors):
        if row is not None:
            r.place[row : row + 1, 0:ROWS] = ref[...].astype(F32)
    r.place[...] = pltpu.roll(r.place[...], shard * ROWS, 1)
    r.place[pl.ds(5 + shard // 2, 1), column(lax.rem(shard, 2) * 384, 384)] = r.vectors[5][...].astype(F32)
    r.small_own[...] = r.place[...].astype(BF16)


def forward_kernel(*refs):
    own = refs[0:6]
    r = SimpleNamespace(vectors=refs[6:15])
    x_own, r.cot, r.lengths = refs[15:18]
    kept = refs[18:24]
    r.result, r.sums, r.vec = refs[24:27]
    handed = dict(zip(HANDED, refs[27:40]))
    full = refs[40:46]
    rest = list(refs[46:])
    for name in FORWARD_WORK:
        setattr(r, name, rest.pop(0))
    r.w_q, r.w_k, r.w_v, r.w_o, r.w_inner, r.w_outer = full
    small_own, small_full, x_full = r.small_own, r.small, r.x
    send_sem, z_sem, x_sem, y_sem, c_sem, local_sem, extra_send, extra_recv, keep_sem = rest
    z, x, y, core = place()
    shard = z * 2 + x
    seq = y * 2 + core
    r.seq = seq
    place_vectors(r, shard)
    r.sums[...] = jnp.zeros_like(r.sums)
    greet(z, x, y, core)
    to_x = device(z, 1 - x, y, core)
    to_y = device(z, x, 1 - y, core)
    to_c = device(z, x, y, 1 - core)
    offsets = (y * 64 + core * 16, 32 + core * 16)
    far = (1 - y) * 64 + core * 16

    def shard_at(back, side):
        return lax.rem(z + 4 - back, 4) * 2 + side

    def own_rows(item, off, size):
        which, part = item
        if which < 4:
            return own[which].at[at(off, size), :]
        if which == 4:
            return own[which].at[at(off, size), pl.ds(part * 768, 768)]
        return own[which].at[at(part * ROWS + off, size), :]

    mine = x_full.at[:, at(seq * 128, 128), :]
    x_local = pltpu.make_async_copy(x_own, mine, local_sem.at[6])
    x_local.start()
    s_local = pltpu.make_async_copy(small_own, small_full.at[shard], local_sem.at[7])
    s_local.start()

    def start(n):
        item = ITEMS[n]
        w = full[item[0]]
        for piece, off in enumerate(offsets):
            src = own_rows(item, off, SIXTH)
            dst = item_rows(w, item, shard, off, SIXTH)
            for j in (2, 1, 3):
                send(src, dst, send_sem.at[n], z_sem.at[n, j - 1, piece], device(lax.rem(z + j, 4), x, y, core))
            send(src, dst, send_sem.at[n], x_sem.at[n, 0, piece], to_x)

    start(0)
    send(x_own, mine, extra_send.at[0], extra_recv.at[0], to_y)
    send(x_own, mine, extra_send.at[0], extra_recv.at[1], to_c)
    for j in (1, 2, 3):
        there = device(lax.rem(z + j, 4), x, y, core)
        send(small_own, small_full.at[shard], extra_send.at[1], extra_recv.at[1 + j], there)
    send(small_own, small_full.at[shard], extra_send.at[1], extra_recv.at[5], to_x)
    for n in range(1, LEAD):
        start(n)
    locals_ = []
    for w in range(6):
        rows = own[w].shape[0]
        copy = pltpu.make_async_copy(own[w], full[w].at[at(shard * rows, rows), :], local_sem.at[w])
        copy.start()
        locals_.append(copy)

    def from_z(n):
        item = ITEMS[n]
        w = full[item[0]]
        for j in (1, 2, 3):
            for piece, off in enumerate(offsets):
                got = item_rows(w, item, shard_at(j, x), off, SIXTH)
                await_bytes(got, z_sem.at[n, j - 1, piece])
                send(got, got, send_sem.at[n], x_sem.at[n, j, piece], to_x)
                if piece == 0:
                    send(got, got, send_sem.at[n], y_sem.at[n, j - 1], to_y)
                send(got, got, send_sem.at[n], c_sem.at[n], to_c)

    def from_x(n):
        item = ITEMS[n]
        w = full[item[0]]
        for j in range(4):
            for piece, off in enumerate(offsets):
                got = item_rows(w, item, shard_at(j, 1 - x), off, SIXTH)
                await_bytes(got, x_sem.at[n, j, piece])
                if piece == 0:
                    send(got, got, send_sem.at[n], y_sem.at[n, 3 + j], to_y)
                send(got, got, send_sem.at[n], c_sem.at[n], to_c)

    def from_y(n):
        item = ITEMS[n]
        w = full[item[0]]
        for m in range(7):
            owner = shard_at(m + 1, x) if m < 3 else shard_at(m - 3, 1 - x)
            got = item_rows(w, item, owner, far, SIXTH)
            await_bytes(got, y_sem.at[n, m])
            send(got, got, send_sem.at[n], c_sem.at[n], to_c)

    def from_c(n):
        await_bytes(full[0].at[pl.ds(0, 7 * ROWS // 2), :], c_sem.at[n])

    def small_relay():
        for j in (1, 2, 3):
            there = small_full.at[shard_at(j, x)]
            await_bytes(there, extra_recv.at[1 + j])
            send(there, there, extra_send.at[1], extra_recv.at[5 + j], to_x)

    def x_relay():
        theirs = x_full.at[:, at(((1 - y) * 2 + core) * 128, 128), :]
        await_bytes(theirs, extra_recv.at[0])
        send(theirs, theirs, extra_send.at[0], extra_recv.at[1], to_c)

    keeps = []

    def keep(src, dst):
        copy = pltpu.make_async_copy(src, dst, keep_sem.at[len(keeps)])
        copy.start()
        keeps.append(copy)

    def hand(*names):
        for name in names:
            keep(getattr(r, name), handed[name])

    def arrive():
        for j in range(4):
            await_bytes(small_full.at[shard_at(j, 1 - x)], extra_recv.at[5 + j])
        await_bytes(x_full.at[:, pl.ds(0, 256), :], extra_recv.at[1])
        for copy in locals_:
            copy.wait()
        x_local.wait()
        s_local.wait()
        vectors(r)
        hand("x")

    def after(n):
        if n == 0:
            arrive()
            project_one(r, "q")
            hand("q")
        elif n == 1:
            project_one(r, "k")
            hand("k")
        elif n == 2:
            project_one(r, "v")
            hand("v")
        if 2 <= n <= 5:
            attend(r, (n - 2) // 2, (n % 2) * 3, (n % 2) * 3 + 3)
        if n == 5:
            hand("p", "c")
            first_norm(r)
            hand("unit_one", "scale_one", "n1b")
            feed_in(r, 0)
        if n == 6:
            feed_in(r, 1)
            feed_in(r, 2)
        if n == 7:
            feed_in(r, 3)
            hand("g", "slope")
        if n in (0, 1, 2, 3, 7, 11):
            which = ITEMS[n][0]
            keep(full[which], kept[which])

    delay = FORWARD_DELAY
    stages = ((0, from_z), (delay[0], from_x), (delay[1], from_y), (delay[2], from_c))
    for step in range(len(ITEMS) + delay[2]):
        if step + LEAD < len(ITEMS):
            start(step + LEAD)
        if step == 1:
            small_relay()
        if step == X_STEP:
            x_relay()
        for depth, stage in stages:
            n = step - depth
            if 0 <= n < len(ITEMS):
                stage(n)
        n = step - delay[2]
        if 0 <= n < len(ITEMS):
            after(n)

    second_norm(r)
    hand("dh2", "df")
    await_bytes(x_full.at[:, pl.ds(0, 384), :], extra_send.at[0])
    await_bytes(small_full.at[pl.ds(0, 7)], extra_send.at[1])
    for n in range(len(ITEMS)):
        await_bytes(full[0].at[pl.ds(0, 7 * ROWS), :], send_sem.at[n])
    for copy in keeps:
        copy.wait()


def forward(weights, vectors_in, inputs, cotangent, lengths):
    count = len(ITEMS)
    wholes = [(8 * w.shape[0], w.shape[1]) for w in weights]
    outs = [jax.ShapeDtypeStruct(shape, BF16) for shape in wholes]
    outs += [
        jax.ShapeDtypeStruct(cotangent.shape, BF16),
        jax.ShapeDtypeStruct((16, 768), F32),
        jax.ShapeDtypeStruct((16, 768), F32),
    ]
    outs += [jax.ShapeDtypeStruct(*FORWARD_WORK[name]) for name in HANDED]
    vmem, anywhere = pl.BlockSpec(memory_space=pltpu.VMEM), pl.BlockSpec(memory_space=pl.ANY)
    return pl.pallas_call(
        forward_kernel,
        out_shape=outs,
        in_specs=[vmem] * 17 + [pl.BlockSpec(memory_space=pltpu.SMEM)],
        out_specs=[anywhere] * 6 + [vmem] * 3 + [anywhere] * len(HANDED),
        scratch_shapes=[pltpu.VMEM(shape, BF16) for shape in wholes]
        + [pltpu.VMEM(*kind) for kind in FORWARD_WORK.values()]
        + [
            pltpu.SemaphoreType.DMA((count,)),
            pltpu.SemaphoreType.DMA((count, 3, 2)),
            pltpu.SemaphoreType.DMA((count, 4, 2)),
            pltpu.SemaphoreType.DMA((count, 7)),
            pltpu.SemaphoreType.DMA((count,)),
            pltpu.SemaphoreType.DMA((8,)),
            pltpu.SemaphoreType.DMA((2,)),
            pltpu.SemaphoreType.DMA((9,)),
            pltpu.SemaphoreType.DMA((6 + len(HANDED),)),
        ],
        compiler_params=pltpu.CompilerParams(
            collective_id=0, has_side_effects=True, vmem_limit_bytes=60 * 2**20
        ),
        name="forward",
    )(*weights, *vectors_in, inputs, cotangent, lengths)


ORDER = (8, 9, 10, 11, 4, 5, 6, 7, 3, 0, 1, 2)
RING = 4
TAKE_ORDER = ("g", "df", "slope", "n1b", "dh2", "unit_one", "scale_one", "c", "k", "q", "v", "p", "x")
GRAD_SHAPES = [(768, 768)] * 4 + [(768, 3072), (3072, 768)]

BACKWARD_WORK = kinds(
    "x", "q", "k", "v", "p", "c", "unit_one", "scale_one", "n1b", "g", "slope", "dh2", "df", "da", "dc", "dq", "dk", "dv",
    "dx_own", "dx_part", "sums", "ring",
)

def ring_load(r, j):
    if j < 4:
        src = r.w_outer.at[pl.ds(j * 768, 768), :]
    elif j < 8:
        src = r.w_inner.at[:, pl.ds((j - 4) * 768, 768)]
    else:
        src = (r.w_o, r.w_q, r.w_k, r.w_v)[j - 8]
    copy = pltpu.make_async_copy(src, r.ring.at[j % RING], r.ring_sem.at[j])
    copy.start()
    return copy


def outer_grads(r):
    @pl.loop(0, 12)
    def _(c):
        cols = column(c * 256, 256)
        r.grads[5][at(c * 256, 256), :] = row_contract(r.g[:, cols], r.df[...]).astype(BF16)


def inner_part(r, i, weight):
    @pl.loop(0, 3)
    def _(c):
        cols = column(i * 768 + c * 256, 256)
        low = (times_transposed(r.df[...], weight[at(c * 256, 256), :]) * r.slope[:, cols].astype(F32)).astype(BF16)
        r.slope[:, cols] = low
        r.sums[5 + i : 6 + i, column(c * 256, 256)] = jnp.sum(low.astype(F32), axis=0, keepdims=True)
        r.grads[4][:, cols] = row_contract(r.n1b[...], low).astype(BF16)


def normed_part(r, i, weight):
    r.dh2[...] = r.dh2[...] + times_transposed(r.slope[:, i * 768 : i * 768 + 768], weight[...])


def first_norm_back(r):
    for slot in range(2):
        rows = pl.ds(slot * 128, 128)
        dn1 = r.dh2[rows, :]
        unit = r.unit_one[rows, :]
        back = norm_back(dn1, r.vec[3:4, :], unit, r.scale_one[rows, 0:1])
        low = back.astype(BF16)
        r.da[slot] = low
        tally(r, slot, 3, dn1 * unit)
        tally(r, slot, 4, dn1)
        tally(r, slot, 2, low.astype(F32))
        r.dx_own[slot] = back


def output_back(r, weight):
    for slot in range(2):
        r.dc[slot] = times_transposed(r.da[slot], weight[...]).astype(BF16)


def attend_back(r, slot, first, last):
    masks = head_masks()
    factor = HEAD_DIM**-0.5

    @pl.loop(first, last)
    def _(p):
        cols = column(p * 128, 128)
        k, q, v, dc = r.k[slot, :, cols], r.q[slot, :, cols], r.v[slot, :, cols], r.dc[slot, :, cols]
        dq = dk = dv = None
        for h in range(2):
            low = r.p[slot, p * 2 + h]
            probs = low.astype(F32)
            dch = dc * masks[h]
            dp = times_transposed(v, dch)
            inner = jnp.sum(dp * probs, axis=0, keepdims=True)
            ds = (probs * (dp - inner)).astype(BF16)
            parts = (row_contract(ds, k * masks[h]), product(ds, q * masks[h]), product(low, dch))
            dq, dk, dv = parts if dq is None else (dq + parts[0], dk + parts[1], dv + parts[2])
        dq = (dq * factor).astype(BF16)
        dv = dv.astype(BF16)
        r.dq[slot, :, cols] = dq
        r.dk[slot, :, cols] = (dk * factor).astype(BF16)
        r.dv[slot, :, cols] = dv
        dq_sum = jnp.sum(dq.astype(F32), axis=0, keepdims=True)
        dv_sum = jnp.sum(dv.astype(F32), axis=0, keepdims=True)
        if slot == 0:
            r.sums[0:1, cols] = dq_sum
            r.sums[1:2, cols] = dv_sum
        else:
            r.sums[0:1, cols] = r.sums[0:1, cols] + dq_sum
            r.sums[1:2, cols] = r.sums[1:2, cols] + dv_sum


def square_grad(r, which):
    own = at(r.seq * 128, 128)

    @pl.loop(0, 3)
    def _(c):
        cols = column(c * 256, 256)
        value = None
        for s in range(2):
            left, right = (
                (r.x[s, own, cols], r.dq[s]),
                (r.x[s, :, cols], r.dk[s]),
                (r.x[s, :, cols], r.dv[s]),
                (r.c[s, :, cols], r.da[s]),
            )[which]
            piece = row_contract(left, right)
            value = piece if value is None else value + piece
        r.grads[which][at(c * 256, 256), :] = value.astype(BF16)


def input_grads(r, w_q, w_k, w_v):
    for slot in range(2):
        r.dx_own[slot] = r.dx_own[slot] + times_transposed(r.dq[slot], w_q[...])

        @pl.loop(0, 3)
        def _(c):
            rows = at(c * 256, 256)
            r.dx_part[slot, :, column(c * 256, 256)] = (
                times_transposed(r.dk[slot], w_k[rows, :]) + times_transposed(r.dv[slot], w_v[rows, :])
            ).astype(BF16)


def backward_kernel(*refs):
    r = SimpleNamespace()
    r.w_q, r.w_k, r.w_v, r.w_o, r.w_inner, r.w_outer = refs[0:6]
    taken = dict(zip(HANDED, refs[6:19]))
    r.vec, sums_in = refs[19:21]
    out = refs[21:27]
    small_out, dx_out = refs[27:29]
    r.grads = refs[29:35]
    rest = list(refs[35:])
    for name in BACKWARD_WORK:
        setattr(r, name, rest.pop(0))
    (from_core, from_y, from_x, from_z, total, both, back_y, back_c) = rest[0:8]
    (small_c, small_y, small_x, small_z, small_1, small_2, small_3, dx_c, dx_sum, dx_y) = rest[8:18]
    send_sem, c_sem, y_sem, x_sem, z_sem, fy_sem, fc_sem, s_send, s_recv, d_send, d_recv = rest[18:29]
    r.take_sem, r.ring_sem = rest[29:31]
    f32 = F32
    small = r.sums
    z, x, y, core = place()
    seq = y * 2 + core
    r.seq = seq
    takes = {}
    for i, name in enumerate(TAKE_ORDER):
        if name == "slope":
            loads = [ring_load(r, j) for j in range(RING)]
        takes[name] = pltpu.make_async_copy(taken[name], getattr(r, name), r.take_sem.at[i])
        takes[name].start()
    r.sums[...] = sums_in[...]
    greet(z, x, y, core)
    to_x = device(z, 1 - x, y, core)
    to_y = device(z, x, 1 - y, core)
    to_c = device(z, x, y, 1 - core)
    mine = (y * 64 + core * 16, 32 + core * 16, (1 - y) * 64 + core * 16)
    theirs = (y * 64 + (1 - core) * 16, 32 + (1 - core) * 16, (1 - y) * 64 + (1 - core) * 16)

    def grad(n, start, shard):
        item = ITEMS[ORDER[n]]
        return item_rows(r.grads[item[0]], item, shard, start, SIXTH)

    def to_partner(n):
        for p in range(3):
            for shard in range(8):
                send(
                    grad(n, theirs[p], shard),
                    from_core.at[n, shard, pl.ds(p * 16, 16), :],
                    send_sem.at[n],
                    c_sem.at[n],
                    to_c,
                )

    def stage_core(n):
        await_bytes(from_core.at[n], c_sem.at[n])
        for p in (2, 1):
            for shard in range(8):
                own = grad(n, mine[p], shard)
                own[...] = (
                    own[...].astype(f32) + from_core[n, shard, p * 16 : p * 16 + 16, :].astype(f32)
                ).astype(BF16)
                if p == 2:
                    send(own, from_y.at[n, shard], send_sem.at[n], y_sem.at[n], to_y)

    def stage_y(n):
        await_bytes(from_y.at[n], y_sem.at[n])
        for shard in range(8):
            own = grad(n, mine[0], shard)
            own[...] = (
                own[...].astype(f32)
                + from_core[n, shard, 0:16, :].astype(f32)
                + from_y[n, shard].astype(f32)
            ).astype(BF16)
        for row in range(4):
            for p in range(2):
                send(
                    grad(n, mine[p], row * 2 + 1 - x),
                    from_x.at[n, row, pl.ds(p * 16, 16), :],
                    send_sem.at[n],
                    x_sem.at[n],
                    to_x,
                )

    def stage_x(n):
        await_bytes(from_x.at[n], x_sem.at[n])
        for row in range(4):
            for p in range(2):
                own = grad(n, mine[p], row * 2 + x)
                own[...] = (own[...].astype(f32) + from_x[n, row, p * 16 : p * 16 + 16, :].astype(f32)).astype(BF16)
        for j in (2, 1, 3):
            there = lax.rem(z + j, 4)
            for p in range(2):
                send(
                    grad(n, mine[p], there * 2 + x),
                    from_z.at[n, j - 1, pl.ds(p * 16, 16), :],
                    send_sem.at[n],
                    z_sem.at[n, j - 1],
                    device(there, x, y, core),
                )

    def stage_z(n):
        for j in range(3):
            await_bytes(from_z.at[n, j], z_sem.at[n, j])
        for p in range(2):
            rows = pl.ds(p * 16, 16)
            total[n, rows, :] = (
                grad(n, mine[p], z * 2 + x)[...].astype(f32)
                + from_z[n, 0, rows, :].astype(f32)
                + from_z[n, 1, rows, :].astype(f32)
                + from_z[n, 2, rows, :].astype(f32)
            ).astype(BF16)
        send(total.at[n], back_y.at[n], send_sem.at[n], fy_sem.at[n], to_y)
        send(total.at[n, pl.ds(0, 16), :], back_c.at[n, pl.ds(0, 16), :], send_sem.at[n], fc_sem.at[n], to_c)

    def put(n, start, value):
        which, part = ITEMS[ORDER[n]]
        rows = at(start + (part * ROWS if which == 5 else 0), SIXTH)
        if which == 4:
            out[which][rows, part * 768 : part * 768 + 768] = value
        else:
            out[which][rows, :] = value

    def stage_back(n):
        await_bytes(back_y.at[n], fy_sem.at[n])
        both[n] = (total[n, 16:32, :].astype(f32) + back_y[n, 16:32, :].astype(f32)).astype(BF16)
        send(both.at[n], back_c.at[n, pl.ds(16, 16), :], send_sem.at[n], fc_sem.at[n], to_c)
        send(back_y.at[n, pl.ds(0, 16), :], back_c.at[n, pl.ds(32, 16), :], send_sem.at[n], fc_sem.at[n], to_c)
        put(n, mine[0], total[n, 0:16, :])
        put(n, mine[1], both[n])
        put(n, mine[2], back_y[n, 0:16, :])

    def stage_end(n):
        await_bytes(back_c.at[n], fc_sem.at[n])
        for p in range(3):
            put(n, theirs[p], back_c[n, p * 16 : p * 16 + 16, :])

    def dx_rows(who):
        return r.dx_part.at[:, at(who * 128, 128), :]

    def dx_0():
        send(dx_rows((1 - y) * 2 + 1 - core), dx_c.at[1], d_send, d_recv.at[0], to_c)
        send(dx_rows(y * 2 + 1 - core), dx_c.at[0], d_send, d_recv.at[0], to_c)

    def dx_1():
        await_bytes(dx_c, d_recv.at[0])
        dx_sum[...] = (dx_rows((1 - y) * 2 + core)[...].astype(f32) + dx_c[1].astype(f32)).astype(BF16)
        send(dx_sum, dx_y, d_send, d_recv.at[1], to_y)

    def dx_end():
        await_bytes(dx_y, d_recv.at[1])
        dx_out[...] = (
            r.dx_own[...] + dx_rows(seq)[...].astype(f32) + dx_c[0].astype(f32) + dx_y[...].astype(f32)
        )

    def small_0():
        send(small, small_c, s_send.at[0], s_recv.at[0], to_c)

    def small_1st():
        await_bytes(small_c, s_recv.at[0])
        small_1[...] = small[...] + small_c[...]
        send(small_1, small_y, s_send.at[1], s_recv.at[1], to_y)

    def small_2nd():
        await_bytes(small_y, s_recv.at[1])
        small_2[...] = small_1[...] + small_y[...]
        send(small_2, small_x, s_send.at[2], s_recv.at[2], to_x)

    def small_3rd():
        await_bytes(small_x, s_recv.at[2])
        small_3[...] = small_2[...] + small_x[...]
        for j in (1, 2, 3):
            send(small_3, small_z.at[z], s_send.at[3], s_recv.at[2 + j], device(lax.rem(z + j, 4), x, y, core))

    def small_4th():
        for j in (1, 2, 3):
            await_bytes(small_z.at[lax.rem(z + 4 - j, 4)], s_recv.at[2 + j])
        await_bytes(small_z.at[pl.ds(0, 3)], s_send.at[3])
        small_z[z] = small_3[...]
        small_out[...] = ((small_z[0] + small_z[1]) + small_z[2]) + small_z[3]

    def block(j):
        loads[j].wait()
        return r.ring.at[j % RING]

    def refill(j):
        loads.append(ring_load(r, j))

    def task(k):
        if k == 0:
            takes["g"].wait()
            takes["df"].wait()
            outer_grads(r)
            for n in range(4):
                to_partner(n)
            takes["slope"].wait()
            takes["n1b"].wait()
        if k < 4:
            inner_part(r, k, block(k))
            refill(k + RING)
            to_partner(4 + k)
        if k == 4:
            takes["dh2"].wait()
            for i in range(4):
                normed_part(r, i, block(4 + i))
                refill(8 + i)
            for name in ("unit_one", "scale_one", "c"):
                takes[name].wait()
            first_norm_back(r)
            square_grad(r, 3)
            to_partner(8)
        if k == 5:
            output_back(r, block(8))
            for name in ("k", "q", "v", "p"):
                takes[name].wait()
        if 5 <= k <= 8:
            attend_back(r, (k - 5) // 2, ((k - 5) % 2) * 3, ((k - 5) % 2) * 3 + 3)
        if k == 9:
            takes["x"].wait()
            small_0()
            for i in range(3):
                square_grad(r, i)
                to_partner(9 + i)
        if k == 10:
            input_grads(r, block(9), block(10), block(11))
            dx_0()

    extra = {10: small_1st, 11: small_2nd, 12: small_3rd, 14: small_4th}
    count = len(ITEMS)
    depths = BACKWARD_DELAY
    stages = tuple(zip(depths, (stage_core, stage_y, stage_x, stage_z, stage_back, stage_end)))
    for step in range(count + depths[-1]):
        task(step)
        for depth, stage in stages:
            n = step - depth
            if 0 <= n < count:
                stage(n)
        if step in extra:
            extra[step]()
        if step == 11:
            dx_1()
        if step == count + depths[-1] - 2:
            dx_end()

    for n in range(count):
        await_bytes(from_core.at[n], send_sem.at[n])
        await_bytes(from_y.at[n], send_sem.at[n])
        await_bytes(from_x.at[n], send_sem.at[n])
        await_bytes(from_z.at[n], send_sem.at[n])
        await_bytes(back_y.at[n], send_sem.at[n])
        await_bytes(back_c.at[n], send_sem.at[n])
    for j in range(3):
        await_bytes(small, s_send.at[j])
    await_bytes(dx_c, d_send)
    await_bytes(dx_sum, d_send)


def backward(weights, handed, vec, sums, dx_like):
    count = len(ITEMS)
    outs = [jax.ShapeDtypeStruct((s[0] // 8, s[1]), BF16) for s in GRAD_SHAPES]
    outs += [jax.ShapeDtypeStruct((16, 768), F32), jax.ShapeDtypeStruct(dx_like.shape, F32)]
    vmem, anywhere = pl.BlockSpec(memory_space=pltpu.VMEM), pl.BlockSpec(memory_space=pl.ANY)
    shape = (16, 768)
    return pl.pallas_call(
        backward_kernel,
        out_shape=outs,
        in_specs=[anywhere] * (6 + len(HANDED)) + [vmem] * 2,
        out_specs=[vmem] * 8,
        scratch_shapes=[pltpu.VMEM(s, BF16) for s in GRAD_SHAPES]
        + [pltpu.VMEM(*kind) for kind in BACKWARD_WORK.values()]
        + [
            pltpu.VMEM((count, 8, 48, 768), BF16),
            pltpu.VMEM((count, 8, 16, 768), BF16),
            pltpu.VMEM((count, 4, 32, 768), BF16),
            pltpu.VMEM((count, 3, 32, 768), BF16),
            pltpu.VMEM((count, 32, 768), BF16),
            pltpu.VMEM((count, 16, 768), BF16),
            pltpu.VMEM((count, 32, 768), BF16),
            pltpu.VMEM((count, 48, 768), BF16),
        ]
        + [pltpu.VMEM(shape, F32)] * 3
        + [pltpu.VMEM((4,) + shape, F32)]
        + [pltpu.VMEM(shape, F32)] * 3
        + [
            pltpu.VMEM((2,) + dx_like.shape, BF16),
            pltpu.VMEM(dx_like.shape, BF16),
            pltpu.VMEM(dx_like.shape, BF16),
            pltpu.SemaphoreType.DMA((count,)),
            pltpu.SemaphoreType.DMA((count,)),
            pltpu.SemaphoreType.DMA((count,)),
            pltpu.SemaphoreType.DMA((count,)),
            pltpu.SemaphoreType.DMA((count, 3)),
            pltpu.SemaphoreType.DMA((count,)),
            pltpu.SemaphoreType.DMA((count,)),
            pltpu.SemaphoreType.DMA((4,)),
            pltpu.SemaphoreType.DMA((6,)),
            pltpu.SemaphoreType.DMA,
            pltpu.SemaphoreType.DMA((2,)),
            pltpu.SemaphoreType.DMA((len(HANDED),)),
            pltpu.SemaphoreType.DMA((12,)),
        ],
        compiler_params=pltpu.CompilerParams(
            collective_id=1, has_side_effects=True, vmem_limit_bytes=67043328
        ),
        name="backward",
    )(*weights, *handed, vec, sums)


def finish_kernel(*refs):
    shares, totals, dx, result = refs[0:6], refs[6], refs[7], refs[8]
    outs = refs[9:15]
    vectors_out = refs[15:24]
    dx_out, result_out, turned = refs[24:27]
    shard = lax.axis_index("shard")
    for share, out in zip(shares, outs):
        out[...] = share[...].astype(F32)
    dx_out[...] = dx[...]
    result_out[...] = result[...]
    turned[...] = pltpu.roll(totals[...], lax.rem(8 - shard, 8) * ROWS, 1)
    for row, out in zip(VECTOR_ROWS, vectors_out):
        if row is not None:
            out[...] = turned[row : row + 1, 0:ROWS]
    vectors_out[5][...] = totals[pl.ds(5 + shard // 2, 1), column(lax.rem(shard, 2) * 384, 384)]


def finish(shares, totals, dx, result):
    outs = [jax.ShapeDtypeStruct(s.shape, F32) for s in shares]
    outs += [jax.ShapeDtypeStruct((1, 384 if row is None else ROWS), F32) for row in VECTOR_ROWS]
    outs += [jax.ShapeDtypeStruct(dx.shape, F32), jax.ShapeDtypeStruct(result.shape, BF16)]
    vmem = pl.BlockSpec(memory_space=pltpu.VMEM)
    return pl.pallas_call(
        finish_kernel,
        out_shape=outs,
        in_specs=[vmem] * 9,
        out_specs=[vmem] * len(outs),
        scratch_shapes=[pltpu.VMEM((16, 768), F32)],
        compiler_params=pltpu.CompilerParams(vmem_limit_bytes=32 * 2**20),
        name="finish",
    )(*shares, totals, dx, result)


def per_device(
    inputs,
    lengths,
    w_query,
    b_query,
    w_key,
    w_value,
    b_value,
    w_output,
    b_output,
    gain_one,
    shift_one,
    w_inner,
    b_inner,
    w_outer,
    b_outer,
    gain_two,
    shift_two,
    cotangent,
):
    vectors_in = (b_query, b_value, b_output, gain_one, shift_one, b_inner, b_outer, gain_two, shift_two)
    weights = (w_query, w_key, w_value, w_output, w_inner, w_outer)
    first = forward(weights, [v.reshape(1, -1) for v in vectors_in], inputs, cotangent, lengths)
    wholes, (result, sums, vec), handed = first[0:6], first[6:9], first[9:]
    *shares, totals, dx = backward(wholes, handed, vec, sums, inputs)
    done = finish(shares, totals, dx, result)
    g_q, g_k, g_v, g_o, g_inner, g_outer = done[0:6]
    g_bq, g_bv, g_bo, g_g1, g_s1, g_bi, g_bouter, g_g2, g_s2 = [v.reshape(-1) for v in done[6:15]]
    return (
        done[16],
        done[15],
        g_q,
        g_bq,
        g_k,
        g_v,
        g_bv,
        g_o,
        g_bo,
        g_g1,
        g_s1,
        g_inner,
        g_bi,
        g_outer,
        g_bouter,
        g_g2,
        g_s2,
    )


def head_logits(query_seq, key_seq, length, factor):
    scores = (
        jnp.einsum("qhd,khd->hqk", query_seq, key_seq, preferred_element_type=jnp.float32) * factor
    )
    visible = jnp.arange(key_seq.shape[0]) < length
    return jnp.where(visible[None, None, :], scores, -1000000000.0)


def per_device_plain(
    inputs,
    lengths,
    w_query,
    b_query,
    w_key,
    w_value,
    b_value,
    w_output,
    b_output,
    gain_one,
    shift_one,
    w_inner,
    b_inner,
    w_outer,
    b_outer,
    gain_two,
    shift_two,
    cotangent,
):
    local_seqs, tok_dev, model_width = inputs.shape
    groups = lax.axis_size("seq")
    head_width = model_width // groups
    local_heads = head_width // HEAD_DIM
    factor = HEAD_DIM ** (-0.5)
    gathered = (
        lax.all_gather(w_query, "shard", axis=0, tiled=True),
        lax.all_gather(b_query, "shard", axis=0, tiled=True),
        lax.all_gather(w_key, "shard", axis=0, tiled=True),
        lax.all_gather(w_value, "shard", axis=0, tiled=True),
        lax.all_gather(b_value, "shard", axis=0, tiled=True),
        lax.all_gather(w_output, "shard", axis=0, tiled=True),
        lax.all_gather(b_output, "shard", axis=0, tiled=True),
        lax.all_gather(gain_one, "shard", axis=0, tiled=True),
        lax.all_gather(shift_one, "shard", axis=0, tiled=True),
        lax.all_gather(w_inner, "shard", axis=0, tiled=True),
        lax.all_gather(b_inner, "shard", axis=0, tiled=True),
        lax.all_gather(w_outer, "shard", axis=0, tiled=True),
        lax.all_gather(b_outer, "shard", axis=0, tiled=True),
        lax.all_gather(gain_two, "shard", axis=0, tiled=True),
        lax.all_gather(shift_two, "shard", axis=0, tiled=True),
    )
    (
        query_w,
        query_b,
        key_w,
        value_w,
        value_b,
        output_w,
        output_b,
        gain_a,
        shift_a,
        inner_w,
        inner_b,
        outer_w,
        outer_b,
        gain_b,
        shift_b,
    ) = gathered
    gain_first = gain_a.astype(jnp.float32)
    shift_first = shift_a.astype(jnp.float32)
    gain_second = gain_b.astype(jnp.float32)
    shift_second = shift_b.astype(jnp.float32)
    flat_rows = inputs.reshape(local_seqs * tok_dev, model_width)
    queries = (product(flat_rows, query_w) + query_b.astype(jnp.float32)).astype(jnp.bfloat16)
    key_rows = product(flat_rows, key_w).astype(jnp.bfloat16)
    values = (product(flat_rows, value_w) + value_b.astype(jnp.float32)).astype(jnp.bfloat16)
    shape_seq = (local_seqs, tok_dev, model_width)
    head_q, head_k, head_v = (
        lax.all_to_all(queries.reshape(shape_seq), "seq", split_axis=2, concat_axis=1, tiled=True),
        lax.all_to_all(key_rows.reshape(shape_seq), "seq", split_axis=2, concat_axis=1, tiled=True),
        lax.all_to_all(values.reshape(shape_seq), "seq", split_axis=2, concat_axis=1, tiled=True),
    )
    seq_len = head_q.shape[1]
    split = (local_seqs, seq_len, local_heads, HEAD_DIM)
    head_q = head_q.reshape(split)
    head_k = head_k.reshape(split)
    head_v = head_v.reshape(split)

    def attend(packed):
        query_seq, key_seq, value_seq, length = packed
        logits = head_logits(query_seq, key_seq, length, factor)
        row_max = jnp.max(logits, axis=-1, keepdims=True)
        shifted = jnp.exp(logits - row_max)
        row_total = jnp.sum(shifted, axis=-1, keepdims=True)
        weights = (shifted / row_total).astype(jnp.bfloat16)
        context = jnp.einsum("hqk,khd->qhd", weights, value_seq, preferred_element_type=jnp.float32)
        return (context.astype(jnp.bfloat16), (row_max + jnp.log(row_total))[..., 0])

    head_context, log_total = lax.map(attend, (head_q, head_k, head_v, lengths))
    back_shape = (local_seqs, seq_len, head_width)
    context = lax.all_to_all(
        head_context.reshape(back_shape), "seq", split_axis=1, concat_axis=2, tiled=True
    ).reshape(-1, model_width)
    branch = product(context, output_w) + output_b.astype(jnp.float32)
    summed = flat_rows.astype(jnp.float32) + branch
    normed = layer_norm(summed, gain_first, shift_first)
    normed_low = normed.astype(jnp.bfloat16)
    pre_inner = product(normed_low, inner_w) + inner_b.astype(jnp.float32)
    activated = jax.nn.gelu(pre_inner, approximate=False).astype(jnp.bfloat16)
    final_sum = normed + product(activated, outer_w) + outer_b.astype(jnp.float32)
    result = layer_norm(final_sum, gain_second, shift_second)
    grad_out = cotangent.reshape(-1, model_width).astype(jnp.float32)
    second_back = jax.vjp(layer_norm, final_sum, gain_second, shift_second)[1]
    grad_final, grad_gain_two, grad_shift_two = second_back(grad_out)
    grad_ffn = grad_final.astype(jnp.bfloat16)
    grad_w_outer = row_contract(activated, grad_ffn)
    grad_b_outer = column_sum(grad_ffn)
    grad_active = times_transposed(grad_ffn, outer_w)
    gelu_back = jax.vjp(partial(jax.nn.gelu, approximate=False), pre_inner)[1]
    grad_pre = gelu_back(grad_active)[0].astype(jnp.bfloat16)
    grad_w_inner = row_contract(normed_low, grad_pre)
    grad_b_inner = column_sum(grad_pre)
    grad_normed = grad_final + times_transposed(grad_pre, inner_w)
    first_back = jax.vjp(layer_norm, summed, gain_first, shift_first)[1]
    grad_summed, grad_gain_one, grad_shift_one = first_back(grad_normed)
    grad_branch = grad_summed.astype(jnp.bfloat16)
    grad_w_output = row_contract(context, grad_branch)
    grad_b_output = column_sum(grad_branch)
    grad_context = times_transposed(grad_branch, output_w).astype(jnp.bfloat16)
    grad_head_context = lax.all_to_all(
        grad_context.reshape(shape_seq), "seq", split_axis=2, concat_axis=1, tiled=True
    ).reshape(split)

    def attend_back(packed):
        query_seq, key_seq, value_seq, log_sum, grad_seq, length = packed
        logits = head_logits(query_seq, key_seq, length, factor)
        attn_probs = jnp.exp(logits - log_sum[..., None])
        weights = attn_probs.astype(jnp.bfloat16)
        grad_value = jnp.einsum(
            "hqk,qhd->khd", weights, grad_seq, preferred_element_type=jnp.float32
        )
        grad_probs = jnp.einsum(
            "qhd,khd->hqk", grad_seq, value_seq, preferred_element_type=jnp.float32
        )
        inner_sum = jnp.sum(grad_probs * attn_probs, axis=-1, keepdims=True)
        grad_scores = (attn_probs * (grad_probs - inner_sum)).astype(jnp.bfloat16)
        grad_query = (
            jnp.einsum("hqk,khd->qhd", grad_scores, key_seq, preferred_element_type=jnp.float32)
            * factor
        )
        grad_key = (
            jnp.einsum("hqk,qhd->khd", grad_scores, query_seq, preferred_element_type=jnp.float32)
            * factor
        )
        return (
            grad_query.astype(jnp.bfloat16),
            grad_key.astype(jnp.bfloat16),
            grad_value.astype(jnp.bfloat16),
        )

    head_gq, head_gk, head_gv = lax.map(
        attend_back, (head_q, head_k, head_v, log_total, grad_head_context, lengths)
    )
    tok_gq, tok_gk, tok_gv = (
        lax.all_to_all(head_gq.reshape(back_shape), "seq", split_axis=1, concat_axis=2, tiled=True),
        lax.all_to_all(head_gk.reshape(back_shape), "seq", split_axis=1, concat_axis=2, tiled=True),
        lax.all_to_all(head_gv.reshape(back_shape), "seq", split_axis=1, concat_axis=2, tiled=True),
    )
    grad_query = tok_gq.reshape(-1, model_width)
    grad_key = tok_gk.reshape(-1, model_width)
    grad_value = tok_gv.reshape(-1, model_width)
    grad_w_query = row_contract(flat_rows, grad_query)
    grad_b_query = column_sum(grad_query)
    grad_w_key = row_contract(flat_rows, grad_key)
    grad_w_value = row_contract(flat_rows, grad_value)
    grad_b_value = column_sum(grad_value)
    grad_rows = (
        grad_summed
        + times_transposed(grad_query, query_w)
        + times_transposed(grad_key, key_w)
        + times_transposed(grad_value, value_w)
    )
    local_grads = (
        grad_w_query,
        grad_b_query,
        grad_w_key,
        grad_w_value,
        grad_b_value,
        grad_w_output,
        grad_b_output,
        grad_gain_one,
        grad_shift_one,
        grad_w_inner,
        grad_b_inner,
        grad_w_outer,
        grad_b_outer,
        grad_gain_two,
        grad_shift_two,
    )
    shares = (
        lax.psum_scatter(local_grads[0], "shard", scatter_dimension=0, tiled=True),
        lax.psum_scatter(local_grads[1], "shard", scatter_dimension=0, tiled=True),
        lax.psum_scatter(local_grads[2], "shard", scatter_dimension=0, tiled=True),
        lax.psum_scatter(local_grads[3], "shard", scatter_dimension=0, tiled=True),
        lax.psum_scatter(local_grads[4], "shard", scatter_dimension=0, tiled=True),
        lax.psum_scatter(local_grads[5], "shard", scatter_dimension=0, tiled=True),
        lax.psum_scatter(local_grads[6], "shard", scatter_dimension=0, tiled=True),
        lax.psum_scatter(local_grads[7], "shard", scatter_dimension=0, tiled=True),
        lax.psum_scatter(local_grads[8], "shard", scatter_dimension=0, tiled=True),
        lax.psum_scatter(local_grads[9], "shard", scatter_dimension=0, tiled=True),
        lax.psum_scatter(local_grads[10], "shard", scatter_dimension=0, tiled=True),
        lax.psum_scatter(local_grads[11], "shard", scatter_dimension=0, tiled=True),
        lax.psum_scatter(local_grads[12], "shard", scatter_dimension=0, tiled=True),
        lax.psum_scatter(local_grads[13], "shard", scatter_dimension=0, tiled=True),
        lax.psum_scatter(local_grads[14], "shard", scatter_dimension=0, tiled=True),
    )
    summed_grads = (
        lax.psum(shares[0].astype(jnp.bfloat16), "seq").astype(jnp.float32),
        lax.psum(shares[1].astype(jnp.bfloat16), "seq").astype(jnp.float32),
        lax.psum(shares[2].astype(jnp.bfloat16), "seq").astype(jnp.float32),
        lax.psum(shares[3].astype(jnp.bfloat16), "seq").astype(jnp.float32),
        lax.psum(shares[4].astype(jnp.bfloat16), "seq").astype(jnp.float32),
        lax.psum(shares[5].astype(jnp.bfloat16), "seq").astype(jnp.float32),
        lax.psum(shares[6].astype(jnp.bfloat16), "seq").astype(jnp.float32),
        lax.psum(shares[7].astype(jnp.bfloat16), "seq").astype(jnp.float32),
        lax.psum(shares[8].astype(jnp.bfloat16), "seq").astype(jnp.float32),
        lax.psum(shares[9].astype(jnp.bfloat16), "seq").astype(jnp.float32),
        lax.psum(shares[10].astype(jnp.bfloat16), "seq").astype(jnp.float32),
        lax.psum(shares[11].astype(jnp.bfloat16), "seq").astype(jnp.float32),
        lax.psum(shares[12].astype(jnp.bfloat16), "seq").astype(jnp.float32),
        lax.psum(shares[13].astype(jnp.bfloat16), "seq").astype(jnp.float32),
        lax.psum(shares[14].astype(jnp.bfloat16), "seq").astype(jnp.float32),
    )
    return (
        result.astype(jnp.bfloat16).reshape(shape_seq),
        grad_rows.reshape(shape_seq),
        summed_grads[0],
        summed_grads[1],
        summed_grads[2],
        summed_grads[3],
        summed_grads[4],
        summed_grads[5],
        summed_grads[6],
        summed_grads[7],
        summed_grads[8],
        summed_grads[9],
        summed_grads[10],
        summed_grads[11],
        summed_grads[12],
        summed_grads[13],
        summed_grads[14],
    )


def solution(mesh):
    tuned = (mesh.shape["shard"], mesh.shape["seq"]) == (8, 4)
    return jax.shard_map(
        per_device if tuned else per_device_plain,
        mesh=mesh,
        in_specs=(
            P("shard", "seq", None),
            P("shard"),
            P("shard", None),
            P("shard"),
            P("shard", None),
            P("shard", None),
            P("shard"),
            P("shard", None),
            P("shard"),
            P("shard"),
            P("shard"),
            P("shard", None),
            P("shard"),
            P("shard", None),
            P("shard"),
            P("shard"),
            P("shard"),
            P("shard", "seq", None),
        ),
        out_specs=(
            P("shard", "seq", None),
            P("shard", "seq", None),
            P("shard", None),
            P("shard"),
            P("shard", None),
            P("shard", None),
            P("shard"),
            P("shard", None),
            P("shard"),
            P("shard"),
            P("shard"),
            P("shard", None),
            P("shard"),
            P("shard", None),
            P("shard"),
            P("shard"),
            P("shard"),
        ),
        check_vma=False,
    )
```

```python
from functools import partial
from types import SimpleNamespace

import jax
import jax.numpy as jnp
from jax import lax
from jax.experimental import pallas as pl
from jax.experimental.pallas import tpu as pltpu
from jax.sharding import PartitionSpec as P

HEAD_DIM = 64
BF16, F32 = jnp.bfloat16, jnp.float32
MESH = pl.DeviceIdType.MESH


epsilon = 1e-12


def layer_norm(tensor, norm_gain, norm_shift):
    average = jnp.mean(tensor, axis=-1, keepdims=True)
    centred = tensor - average
    variance = jnp.mean(centred * centred, axis=-1, keepdims=True)
    return centred * lax.rsqrt(variance + epsilon) * norm_gain + norm_shift


def product(operand, weight):
    return jnp.dot(operand, weight, preferred_element_type=jnp.float32)


def row_contract(operand, weight):
    return lax.dot_general(
        operand, weight, (((0,), (0,)), ((), ())), preferred_element_type=jnp.float32
    )


def times_transposed(operand, weight):
    return lax.dot_general(
        operand, weight, (((1,), (1,)), ((), ())), preferred_element_type=jnp.float32
    )


def column_sum(tensor):
    return jnp.sum(tensor.astype(jnp.float32), axis=0)


def place():
    shard, seq = lax.axis_index("shard"), lax.axis_index("seq")
    return shard // 2, lax.rem(shard, 2), seq // 2, lax.rem(seq, 2)


def device(z, x, y, core):
    return (z * 2 + x, y * 2 + core)


def send(src, dst, send_sem, recv_sem, where):
    copy = pltpu.make_async_remote_copy(
        src_ref=src,
        dst_ref=dst,
        send_sem=send_sem,
        recv_sem=recv_sem,
        device_id=where,
        device_id_type=MESH,
    )
    copy.start()
    return copy


def await_bytes(ref, sem):
    pltpu.make_async_copy(ref, ref, sem).wait()


def greet(z, x, y, core):
    barrier = pltpu.get_barrier_semaphore()
    others = [device(lax.rem(z + j, 4), x, y, core) for j in (1, 2, 3)]
    others += [device(z, 1 - x, y, core), device(z, x, 1 - y, core), device(z, x, y, 1 - core)]
    for other in others:
        pl.semaphore_signal(barrier, inc=1, device_id=other, device_id_type=MESH)
    pl.semaphore_wait(barrier, len(others))


def at(start, size):
    return pl.ds(pl.multiple_of(start, 16), size)


ITEMS = [(w, 0, 768) for w in range(4)] + [(4, i * 768, 768) for i in range(4)] + [(5, i * 256, 256) for i in range(3)]
ROWS = 96
SHARD_ROWS = (96, 96, 96, 96, 96, 384)
WIDTHS = (768, 768, 768, 768, 3072, 768)
LEAD = 2
X_STEP = 2
FORWARD_DELAY = (1, 2, 3)
BACKWARD_DELAY = (0, 1, 2, 3, 4, 5)
THIRDS = (3,) * len(ITEMS)


def half(item, core):
    which, first, width = item
    return pl.ds(pl.multiple_of(first + core * (width // 2), 128), width // 2)


def column(start, width):
    return pl.ds(pl.multiple_of(start, 128), width)


def head_masks():
    lane = lax.broadcasted_iota(jnp.int32, (1, 128), 1)
    low = (lane < HEAD_DIM).astype(F32)
    return (low.astype(BF16), (1.0 - low).astype(BF16))


def vectors(r):
    r.vec[...] = jnp.sum(r.small[...].astype(F32), axis=0)
    for i in range(4):
        r.b_inner[:, i * 768 : i * 768 + 768] = r.vec[5 + i : 6 + i, :]


def project_one(r, name):
    own = at(r.seq * 128, 128)
    for slot in range(2):

        @pl.loop(0, 3)
        def _(c):
            cols = column(c * 256, 256)
            if name == "q":
                r.q[slot, :, cols] = (product(r.x[slot, own, :], r.w_q[:, :, cols].reshape(768, 256)) + r.vec[0:1, cols]).astype(BF16)
            elif name == "k":
                r.k[slot, :, cols] = product(r.x[slot], r.w_k[:, :, cols].reshape(768, 256)).astype(BF16)
            else:
                r.v[slot, :, cols] = (product(r.x[slot], r.w_v[:, :, cols].reshape(768, 256)) + r.vec[1:2, cols]).astype(BF16)


def attend(r, slot, first, last):
    masks = head_masks()
    visible = lax.broadcasted_iota(jnp.int32, (512, 128), 0) < r.lengths[slot]

    @pl.loop(first, last)
    def _(p):
        cols = column(p * 128, 128)
        k, q, v = r.k[slot, :, cols], r.q[slot, :, cols], r.v[slot, :, cols]
        context = None
        for h in range(2):
            scores = times_transposed(k, q * masks[h]) * (HEAD_DIM**-0.5)
            logits = jnp.where(visible, scores, -1000000000.0)
            shifted = jnp.exp(logits - jnp.max(logits, axis=0, keepdims=True))
            probs = shifted * (1.0 / jnp.sum(shifted, axis=0, keepdims=True))
            low = probs.astype(BF16)
            r.p[slot, p * 2 + h] = low
            part = row_contract(low, v * masks[h])
            context = part if context is None else context + part
        r.c[slot, :, cols] = context.astype(BF16)


def norm_stats(rows):
    average = jnp.mean(rows, axis=-1, keepdims=True)
    centred = rows - average
    variance = jnp.mean(centred * centred, axis=-1, keepdims=True)
    scale = lax.rsqrt(variance + epsilon)
    return centred * scale, scale


def norm_back(grad, gain, unit, scale):
    g = grad * gain
    return scale * (
        g - jnp.mean(g, axis=-1, keepdims=True) - unit * jnp.mean(g * unit, axis=-1, keepdims=True)
    )


def first_norm(r):
    for slot in range(2):
        rows = pl.ds(slot * 128, 128)
        h1 = r.x[slot, at(r.seq * 128, 128), :].astype(F32) + product(r.c[slot], r.w_o[...].reshape(768, 768)) + r.vec[2:3, :]
        unit, scale = norm_stats(h1)
        r.unit_one[rows, :] = unit
        r.scale_one[rows, :] = jnp.broadcast_to(scale, (128, 128))
        n1 = unit * r.vec[3:4, :] + r.vec[4:5, :]
        r.n1[rows, :] = n1
        r.n1b[rows, :] = n1.astype(BF16)


def feed_in(r, i):
    @pl.loop(0, 3)
    def _(c):
        cols = column(i * 768 + c * 256, 256)
        u = product(r.n1b[...], r.w_inner[:, :, cols].reshape(768, 256)) + r.b_inner[:, cols]
        phi = 0.5 * (1.0 + lax.erf(u * 0.7071067811865476))
        r.g[:, cols] = (u * phi).astype(BF16)
        r.slope[:, cols] = (phi + u * (0.3989422804014327 * jnp.exp(-0.5 * u * u))).astype(BF16)


def feed_out(r, i):
    cols = pl.ds(i * 256, 256)
    r.dh2[:, cols] = r.n1[:, cols] + product(r.g[...], r.w_outer[:, :, cols].reshape(3072, 256)) + r.vec[9:10, cols]


def second_norm(r):
    for slot in range(2):
        rows = pl.ds(slot * 128, 128)
        unit, scale = norm_stats(r.dh2[rows, :])
        r.result[slot] = (unit * r.vec[10:11, :] + r.vec[11:12, :]).astype(BF16)
        grad = r.cot[slot].astype(F32)
        back = norm_back(grad, r.vec[10:11, :], unit, scale)
        low = back.astype(BF16)
        r.dh2[rows, :] = back
        r.df[rows, :] = low
        tally(r, slot, 10, grad * unit)
        tally(r, slot, 11, grad)
        tally(r, slot, 9, low.astype(F32))


def tally(r, slot, row, values):
    total = jnp.sum(values, axis=0, keepdims=True)
    r.sums[row : row + 1, :] = total if slot == 0 else r.sums[row : row + 1, :] + total


KINDS = {
    "place": ((16, 768), F32),
    "small_own": ((16, 768), BF16),
    "small": ((8, 16, 768), BF16),
    "b_inner": ((1, 3072), F32),
    "x": ((2, 512, 768), BF16),
    "q": ((2, 128, 768), BF16),
    "k": ((2, 512, 768), BF16),
    "v": ((2, 512, 768), BF16),
    "p": ((2, 12, 512, 128), BF16),
    "c": ((2, 128, 768), BF16),
    "unit_one": ((256, 768), F32),
    "scale_one": ((256, 128), F32),
    "n1": ((256, 768), F32),
    "n1b": ((256, 768), BF16),
    "g": ((256, 3072), BF16),
    "slope": ((256, 3072), BF16),
    "dh2": ((256, 768), F32),
    "df": ((256, 768), BF16),
    "da": ((2, 128, 768), BF16),
    "dc": ((2, 128, 768), BF16),
    "dq": ((2, 128, 768), BF16),
    "dk": ((2, 512, 768), BF16),
    "dv": ((2, 512, 768), BF16),
    "dx_own": ((2, 128, 768), F32),
    "dx_part": ((2, 512, 768), BF16),
    "sums": ((16, 768), F32),
    "ring": ((4, 768, 768), BF16),
}


def kinds(*names):
    return {name: KINDS[name] for name in names}


VECTOR_ROWS = (0, 1, 2, 3, 4, None, 9, 10, 11)
HANDED = ("x", "q", "k", "v", "p", "c", "unit_one", "scale_one", "n1b", "g", "slope", "dh2", "df")

FORWARD_WORK = kinds(
    "place", "small_own", "small", "b_inner", "x", "q", "k", "v", "p", "c", "unit_one", "scale_one", "n1", "n1b", "g",
    "slope", "dh2", "df",
)

def place_vectors(r, shard):
    r.place[...] = jnp.zeros_like(r.place)
    for row, ref in zip(VECTOR_ROWS, r.vectors):
        if row is not None:
            r.place[row : row + 1, 0:ROWS] = ref[...].astype(F32)
    r.place[...] = pltpu.roll(r.place[...], shard * ROWS, 1)
    r.place[pl.ds(5 + shard // 2, 1), column(lax.rem(shard, 2) * 384, 384)] = r.vectors[5][...].astype(F32)
    r.small_own[...] = r.place[...].astype(BF16)


def forward_kernel(*refs):
    own = refs[0:6]
    r = SimpleNamespace(vectors=refs[6:15])
    x_own, r.cot, r.lengths = refs[15:18]
    kept = refs[18:24]
    r.result, r.sums, r.vec = refs[24:27]
    handed = dict(zip(HANDED, refs[27:40]))
    full = refs[40:46]
    rest = list(refs[46:])
    for name in FORWARD_WORK:
        setattr(r, name, rest.pop(0))
    r.w_q, r.w_k, r.w_v, r.w_o, r.w_inner, r.w_outer = full
    small_own, small_full, x_full = r.small_own, r.small, r.x
    send_sem, z_sem, x_sem, y_sem, c_sem, local_sem, own_sem, extra_send, extra_recv, keep_sem = rest
    z, x, y, core = place()
    shard = z * 2 + x
    seq = y * 2 + core
    r.seq = seq
    place_vectors(r, shard)
    r.sums[...] = jnp.zeros_like(r.sums)
    greet(z, x, y, core)
    to_x = device(z, 1 - x, y, core)
    to_y = device(z, x, 1 - y, core)
    to_c = device(z, x, y, 1 - core)
    def shard_at(back, side):
        return lax.rem(z + 4 - back, 4) * 2 + side

    def kept_rows(n):
        rows = SHARD_ROWS[ITEMS[n][0]]
        return rows, rows // 3

    def block(n, owner, begin, size):
        return full[ITEMS[n][0]].at[owner, at(begin, size), half(ITEMS[n], core)]

    def carried(n, owner):
        rows, third = kept_rows(n)
        return block(n, owner, y * third, rows - third)

    def for_y(n, owner):
        rows, third = kept_rows(n)
        return block(n, owner, y * (rows - third), third)

    mine = x_full.at[:, at(seq * 128, 128), :]
    x_local = pltpu.make_async_copy(x_own, mine, local_sem.at[0])
    x_local.start()
    s_local = pltpu.make_async_copy(small_own, small_full.at[shard], local_sem.at[1])
    s_local.start()

    def start(n):
        rows, third = kept_rows(n)
        src = own[ITEMS[n][0]].at[at(y * third, rows - third), half(ITEMS[n], core)]
        for j in (2, 1, 3):
            there = device(lax.rem(z + j, 4), x, y, core)
            send(src, carried(n, shard), send_sem.at[n], z_sem.at[n, j - 1], there)
        send(src, carried(n, shard), send_sem.at[n], x_sem.at[n, 0], to_x)

    start(0)
    send(x_own, mine, extra_send.at[0], extra_recv.at[0], to_y)
    send(x_own, mine, extra_send.at[0], extra_recv.at[1], to_c)
    for j in (1, 2, 3):
        there = device(lax.rem(z + j, 4), x, y, core)
        send(small_own, small_full.at[shard], extra_send.at[1], extra_recv.at[1 + j], there)
    send(small_own, small_full.at[shard], extra_send.at[1], extra_recv.at[5], to_x)
    for n in range(1, LEAD):
        start(n)
    locals_ = []
    for n, item in enumerate(ITEMS):
        rows = SHARD_ROWS[item[0]]
        copy = pltpu.make_async_copy(own[item[0]].at[:, half(item, core)], block(n, shard, 0, rows), own_sem.at[n])
        copy.start()
        locals_.append(copy)

    def from_z(n):
        for j in (1, 2, 3):
            owner = shard_at(j, x)
            got = carried(n, owner)
            await_bytes(got, z_sem.at[n, j - 1])
            send(got, got, send_sem.at[n], x_sem.at[n, j], to_x)
            send(for_y(n, owner), for_y(n, owner), send_sem.at[n], y_sem.at[n], to_y)

    def from_x(n):
        for j in range(4):
            owner = shard_at(j, 1 - x)
            await_bytes(carried(n, owner), x_sem.at[n, j])
            send(for_y(n, owner), for_y(n, owner), send_sem.at[n], y_sem.at[n], to_y)

    def some(n, owners, rows):
        return full[ITEMS[n][0]].at[pl.ds(0, owners), pl.ds(0, rows), half(ITEMS[n], core)]

    def from_y(n):
        rows, third = kept_rows(n)
        await_bytes(some(n, 7, third), y_sem.at[n])
        locals_[n].wait()
        whole = some(n, 8, rows)
        send(whole, whole, send_sem.at[n], c_sem.at[n], to_c)

    def from_c(n):
        await_bytes(some(n, 8, SHARD_ROWS[ITEMS[n][0]]), c_sem.at[n])

    def sent(n):
        rows, third = kept_rows(n)
        await_bytes(some(n, 7, rows - third), send_sem.at[n])
        await_bytes(some(n, 7, third), send_sem.at[n])
        await_bytes(some(n, 8, rows), send_sem.at[n])

    def small_relay():
        for j in (1, 2, 3):
            there = small_full.at[shard_at(j, x)]
            await_bytes(there, extra_recv.at[1 + j])
            send(there, there, extra_send.at[1], extra_recv.at[5 + j], to_x)

    def x_relay():
        theirs = x_full.at[:, at(((1 - y) * 2 + core) * 128, 128), :]
        await_bytes(theirs, extra_recv.at[0])
        send(theirs, theirs, extra_send.at[0], extra_recv.at[1], to_c)

    keeps = []

    def keep(src, dst):
        copy = pltpu.make_async_copy(src, dst, keep_sem.at[len(keeps)])
        copy.start()
        keeps.append(copy)

    def hand(*names):
        for name in names:
            keep(getattr(r, name), handed[name])

    def arrive():
        for j in range(4):
            await_bytes(small_full.at[shard_at(j, 1 - x)], extra_recv.at[5 + j])
        await_bytes(x_full.at[:, pl.ds(0, 256), :], extra_recv.at[1])
        x_local.wait()
        s_local.wait()
        vectors(r)
        hand("x")

    def after(n):
        if n == 0:
            arrive()
            project_one(r, "q")
            hand("q")
        elif n == 1:
            project_one(r, "k")
            hand("k")
        elif n == 2:
            project_one(r, "v")
            hand("v")
        if 2 <= n <= 5:
            attend(r, (n - 2) // 2, (n % 2) * 3, (n % 2) * 3 + 3)
        if n == 5:
            hand("p", "c")
            first_norm(r)
            hand("unit_one", "scale_one", "n1b")
            feed_in(r, 0)
        if n == 6:
            feed_in(r, 1)
            feed_in(r, 2)
        if n == 7:
            feed_in(r, 3)
            hand("g", "slope")
        if n >= 8:
            feed_out(r, n - 8)
        if n in (0, 1, 2, 3, 7, 10):
            which = ITEMS[n][0]
            keep(full[which], kept[which])

    delay = FORWARD_DELAY
    stages = ((0, from_z), (delay[0], from_x), (delay[1], from_y), (delay[2], from_c))
    for step in range(len(ITEMS) + delay[2]):
        if step + LEAD < len(ITEMS):
            start(step + LEAD)
        if step == 1:
            small_relay()
        if step == X_STEP:
            x_relay()
        for depth, stage in stages:
            n = step - depth
            if 0 <= n < len(ITEMS):
                stage(n)
        n = step - delay[2]
        if 0 <= n < len(ITEMS):
            after(n)

    second_norm(r)
    hand("dh2", "df")
    await_bytes(x_full.at[:, pl.ds(0, 384), :], extra_send.at[0])
    await_bytes(small_full.at[pl.ds(0, 7)], extra_send.at[1])
    for n in range(len(ITEMS)):
        sent(n)
    for copy in keeps:
        copy.wait()


def forward(weights, vectors_in, inputs, cotangent, lengths):
    count = len(ITEMS)
    wholes = [(8,) + w.shape for w in weights]
    outs = [jax.ShapeDtypeStruct(shape, BF16) for shape in wholes]
    outs += [
        jax.ShapeDtypeStruct(cotangent.shape, BF16),
        jax.ShapeDtypeStruct((16, 768), F32),
        jax.ShapeDtypeStruct((16, 768), F32),
    ]
    outs += [jax.ShapeDtypeStruct(*FORWARD_WORK[name]) for name in HANDED]
    vmem, anywhere = pl.BlockSpec(memory_space=pltpu.VMEM), pl.BlockSpec(memory_space=pl.ANY)
    return pl.pallas_call(
        forward_kernel,
        out_shape=outs,
        in_specs=[vmem] * 17 + [pl.BlockSpec(memory_space=pltpu.SMEM)],
        out_specs=[anywhere] * 6 + [vmem] * 3 + [anywhere] * len(HANDED),
        scratch_shapes=[pltpu.VMEM(shape, BF16) for shape in wholes]
        + [pltpu.VMEM(*kind) for kind in FORWARD_WORK.values()]
        + [
            pltpu.SemaphoreType.DMA((count,)),
            pltpu.SemaphoreType.DMA((count, 3)),
            pltpu.SemaphoreType.DMA((count, 4)),
            pltpu.SemaphoreType.DMA((count,)),
            pltpu.SemaphoreType.DMA((count,)),
            pltpu.SemaphoreType.DMA((2,)),
            pltpu.SemaphoreType.DMA((count,)),
            pltpu.SemaphoreType.DMA((2,)),
            pltpu.SemaphoreType.DMA((9,)),
            pltpu.SemaphoreType.DMA((6 + len(HANDED),)),
        ],
        compiler_params=pltpu.CompilerParams(
            collective_id=0, has_side_effects=True, vmem_limit_bytes=60 * 2**20
        ),
        name="forward",
    )(*weights, *vectors_in, inputs, cotangent, lengths)


ORDER = (8, 9, 10, 4, 5, 6, 7, 3, 0, 1, 2)
RING = 4
TAKE_ORDER = ("g", "df", "slope", "n1b", "dh2", "unit_one", "scale_one", "c", "k", "q", "v", "p", "x")
GRAD_SHAPES = [(4, 2, rows, width) for rows, width in zip(SHARD_ROWS, WIDTHS)]

BACKWARD_WORK = kinds(
    "x", "q", "k", "v", "p", "c", "unit_one", "scale_one", "n1b", "g", "slope", "dh2", "df", "da", "dc", "dq", "dk", "dv",
    "dx_own", "dx_part", "sums", "ring",
)

def ring_load(r, j):
    if j < 4:
        src = r.w_outer.at[pl.ds(j * 768, 768), :]
    elif j < 8:
        src = r.w_inner.at[:, pl.ds((j - 4) * 768, 768)]
    else:
        src = (r.w_o, r.w_q, r.w_k, r.w_v)[j - 8]
    copy = pltpu.make_async_copy(src, r.ring.at[j % RING], r.ring_sem.at[j])
    copy.start()
    return copy


def outer_grad(r, i):
    cols = pl.ds(i * 256, 256)
    for c in range(8):
        left = r.g[:, c * 384 : c * 384 + 384]
        r.grads[5][c // 2, c % 2, :, cols] = row_contract(left, r.df[:, cols]).astype(BF16)


def inner_part(r, i, weight):
    @pl.loop(0, 3)
    def _(c):
        cols = column(i * 768 + c * 256, 256)
        low = (times_transposed(r.df[...], weight[at(c * 256, 256), :]) * r.slope[:, cols].astype(F32)).astype(BF16)
        r.slope[:, cols] = low
        r.sums[5 + i : 6 + i, column(c * 256, 256)] = jnp.sum(low.astype(F32), axis=0, keepdims=True)
        r.grads[4][:, :, :, cols] = row_contract(r.n1b[...], low).astype(BF16).reshape(4, 2, ROWS, 256)


def normed_part(r, i, weight):
    r.dh2[...] = r.dh2[...] + times_transposed(r.slope[:, i * 768 : i * 768 + 768], weight[...])


def first_norm_back(r):
    for slot in range(2):
        rows = pl.ds(slot * 128, 128)
        dn1 = r.dh2[rows, :]
        unit = r.unit_one[rows, :]
        back = norm_back(dn1, r.vec[3:4, :], unit, r.scale_one[rows, 0:1])
        low = back.astype(BF16)
        r.da[slot] = low
        tally(r, slot, 3, dn1 * unit)
        tally(r, slot, 4, dn1)
        tally(r, slot, 2, low.astype(F32))
        r.dx_own[slot] = back


def output_back(r, weight):
    for slot in range(2):
        r.dc[slot] = times_transposed(r.da[slot], weight[...]).astype(BF16)


def attend_back(r, slot, first, last):
    masks = head_masks()
    factor = HEAD_DIM**-0.5

    @pl.loop(first, last)
    def _(p):
        cols = column(p * 128, 128)
        k, q, v, dc = r.k[slot, :, cols], r.q[slot, :, cols], r.v[slot, :, cols], r.dc[slot, :, cols]
        dq = dk = dv = None
        for h in range(2):
            low = r.p[slot, p * 2 + h]
            probs = low.astype(F32)
            dch = dc * masks[h]
            dp = times_transposed(v, dch)
            inner = jnp.sum(dp * probs, axis=0, keepdims=True)
            ds = (probs * (dp - inner)).astype(BF16)
            parts = (row_contract(ds, k * masks[h]), product(ds, q * masks[h]), product(low, dch))
            dq, dk, dv = parts if dq is None else (dq + parts[0], dk + parts[1], dv + parts[2])
        dq = (dq * factor).astype(BF16)
        dv = dv.astype(BF16)
        r.dq[slot, :, cols] = dq
        r.dk[slot, :, cols] = (dk * factor).astype(BF16)
        r.dv[slot, :, cols] = dv
        dq_sum = jnp.sum(dq.astype(F32), axis=0, keepdims=True)
        dv_sum = jnp.sum(dv.astype(F32), axis=0, keepdims=True)
        if slot == 0:
            r.sums[0:1, cols] = dq_sum
            r.sums[1:2, cols] = dv_sum
        else:
            r.sums[0:1, cols] = r.sums[0:1, cols] + dq_sum
            r.sums[1:2, cols] = r.sums[1:2, cols] + dv_sum


def square_grad(r, which):
    own = at(r.seq * 128, 128)

    @pl.loop(0, 2)
    def _(c):
        cols = column(c * 384, 384)
        value = None
        for s in range(2):
            left, right = (
                (r.x[s, own, cols], r.dq[s]),
                (r.x[s, :, cols], r.dk[s]),
                (r.x[s, :, cols], r.dv[s]),
                (r.c[s, :, cols], r.da[s]),
            )[which]
            piece = row_contract(left, right)
            value = piece if value is None else value + piece
        r.grads[which][pl.ds(c * 2, 2)] = value.astype(BF16).reshape(2, 2, ROWS, 768)


def input_grads(r, w_q, w_k, w_v):
    for slot in range(2):
        r.dx_own[slot] = r.dx_own[slot] + times_transposed(r.dq[slot], w_q[...])

        @pl.loop(0, 3)
        def _(c):
            rows = at(c * 256, 256)
            r.dx_part[slot, :, column(c * 256, 256)] = (
                times_transposed(r.dk[slot], w_k[rows, :]) + times_transposed(r.dv[slot], w_v[rows, :])
            ).astype(BF16)


def backward_kernel(*refs):
    r = SimpleNamespace()
    r.w_q, r.w_k, r.w_v, r.w_o, r.w_inner, r.w_outer = refs[0:6]
    taken = dict(zip(HANDED, refs[6:19]))
    r.vec, sums_in = refs[19:21]
    out = refs[21:27]
    small_out, dx_out = refs[27:29]
    r.grads = refs[29:35]
    rest = list(refs[35:])
    for name in BACKWARD_WORK:
        setattr(r, name, rest.pop(0))
    count = len(ITEMS)
    from_core, from_y, from_x, from_z, total, back_y = [rest[i * count : i * count + count] for i in range(6)]
    rest = rest[6 * count :]
    (small_c, small_y, small_x, small_z, small_1, small_2, small_3, dx_c, dx_sum, dx_y) = rest[0:10]
    send_sem, c_sem, y_sem, x_sem, z_sem, fy_sem, fc_sem, s_send, s_recv, d_send, d_recv = rest[10:21]
    r.take_sem, r.ring_sem = rest[21:23]
    f32 = F32
    small = r.sums
    z, x, y, core = place()
    seq = y * 2 + core
    r.seq = seq
    takes = {}
    for i, name in enumerate(TAKE_ORDER):
        if name == "slope":
            loads = [ring_load(r, j) for j in range(RING)]
        takes[name] = pltpu.make_async_copy(taken[name], getattr(r, name), r.take_sem.at[i])
        takes[name].start()
    r.sums[...] = sums_in[...]
    greet(z, x, y, core)
    to_x = device(z, 1 - x, y, core)
    to_y = device(z, x, 1 - y, core)
    to_c = device(z, x, y, 1 - core)

    def parts(n):
        rows = SHARD_ROWS[ITEMS[ORDER[n]][0]]
        return rows, rows // THIRDS[n]

    def grad(n, side=core):
        item = ITEMS[ORDER[n]]
        return r.grads[item[0]].at[:, :, :, half(item, side)]

    def to_partner(n):
        send(grad(n, 1 - core), from_core[n], send_sem.at[n], c_sem.at[n], to_c)

    def add(ref, *others):
        value = ref[...].astype(f32)
        for other in others:
            value = value + other[...].astype(f32)
        ref[...] = value.astype(BF16)

    def stage_core(n):
        rows, part = parts(n)
        await_bytes(from_core[n], c_sem.at[n])
        far = at((1 - y) * (rows - part), part)
        add(grad(n).at[:, :, far, :], from_core[n].at[:, :, far, :])
        send(grad(n).at[:, :, far, :], from_y[n], send_sem.at[n], y_sem.at[n], to_y)
        middle = pl.ds(part, rows - 2 * part)
        add(grad(n).at[:, :, middle, :], from_core[n].at[:, :, middle, :])

    def stage_y(n):
        rows, part = parts(n)
        await_bytes(from_y[n], y_sem.at[n])
        near = at(y * (rows - part), part)
        add(grad(n).at[:, :, near, :], from_core[n].at[:, :, near, :], from_y[n])
        carried = at(y * part, rows - part)
        send(grad(n).at[:, 1 - x, carried, :], from_x[n], send_sem.at[n], x_sem.at[n], to_x)

    def stage_x(n):
        rows, part = parts(n)
        await_bytes(from_x[n], x_sem.at[n])
        carried = at(y * part, rows - part)
        add(grad(n).at[:, x, carried, :], from_x[n])
        for j in (2, 1, 3):
            there = lax.rem(z + j, 4)
            send(
                grad(n).at[there, x, carried, :],
                from_z[n].at[j - 1],
                send_sem.at[n],
                z_sem.at[n, j - 1],
                device(there, x, y, core),
            )

    def stage_z(n):
        rows, part = parts(n)
        for j in range(3):
            await_bytes(from_z[n].at[j], z_sem.at[n, j])
        value = grad(n).at[z, x, at(y * part, rows - part), :][...].astype(f32)
        for j in range(3):
            value = value + from_z[n][j].astype(f32)
        total[n][...] = value.astype(BF16)
        send(total[n], back_y[n], send_sem.at[n], fy_sem.at[n], to_y)

    def shares(n):
        item = ITEMS[ORDER[n]]
        return out[item[0]].at[:, half(item, core)]

    def stage_back(n):
        rows, part = parts(n)
        await_bytes(back_y[n], fy_sem.at[n])
        middle = rows - 2 * part
        place_ = shares(n)
        place_[at(y * (rows - part), part), :] = total[n][at(y * middle, part), :]
        place_[at((1 - y) * (rows - part), part), :] = back_y[n][at((1 - y) * middle, part), :]
        place_[pl.ds(part, middle), :] = (
            total[n][at((1 - y) * part, middle), :].astype(f32) + back_y[n][at(y * part, middle), :].astype(f32)
        ).astype(BF16)
        send(place_, place_, send_sem.at[n], fc_sem.at[n], to_c)

    def stage_end(n):
        await_bytes(shares(n), fc_sem.at[n])

    def sent(n):
        for ref in (from_core[n], from_y[n], from_x[n], from_z[n], total[n], shares(n)):
            await_bytes(ref, send_sem.at[n])

    def dx_rows(who):
        return r.dx_part.at[:, at(who * 128, 128), :]

    def dx_0():
        send(dx_rows((1 - y) * 2 + 1 - core), dx_c.at[1], d_send, d_recv.at[0], to_c)
        send(dx_rows(y * 2 + 1 - core), dx_c.at[0], d_send, d_recv.at[0], to_c)

    def dx_1():
        await_bytes(dx_c, d_recv.at[0])
        dx_sum[...] = (dx_rows((1 - y) * 2 + core)[...].astype(f32) + dx_c[1].astype(f32)).astype(BF16)
        send(dx_sum, dx_y, d_send, d_recv.at[1], to_y)

    def dx_end():
        await_bytes(dx_y, d_recv.at[1])
        dx_out[...] = (
            r.dx_own[...] + dx_rows(seq)[...].astype(f32) + dx_c[0].astype(f32) + dx_y[...].astype(f32)
        )

    def small_0():
        send(small, small_c, s_send.at[0], s_recv.at[0], to_c)

    def small_1st():
        await_bytes(small_c, s_recv.at[0])
        small_1[...] = small[...] + small_c[...]
        send(small_1, small_y, s_send.at[1], s_recv.at[1], to_y)

    def small_2nd():
        await_bytes(small_y, s_recv.at[1])
        small_2[...] = small_1[...] + small_y[...]
        send(small_2, small_x, s_send.at[2], s_recv.at[2], to_x)

    def small_3rd():
        await_bytes(small_x, s_recv.at[2])
        small_3[...] = small_2[...] + small_x[...]
        for j in (1, 2, 3):
            send(small_3, small_z.at[z], s_send.at[3], s_recv.at[2 + j], device(lax.rem(z + j, 4), x, y, core))

    def small_4th():
        for j in (1, 2, 3):
            await_bytes(small_z.at[lax.rem(z + 4 - j, 4)], s_recv.at[2 + j])
        await_bytes(small_z.at[pl.ds(0, 3)], s_send.at[3])
        small_z[z] = small_3[...]
        small_out[...] = ((small_z[0] + small_z[1]) + small_z[2]) + small_z[3]

    def block(j):
        loads[j].wait()
        return r.ring.at[j % RING]

    def refill(j):
        loads.append(ring_load(r, j))

    def task(k):
        if k == 0:
            takes["g"].wait()
            takes["df"].wait()
            for i in range(2):
                outer_grad(r, i)
                to_partner(i)
        if k == 1:
            outer_grad(r, 2)
            to_partner(2)
            takes["slope"].wait()
            takes["n1b"].wait()
        for i in ((), (0,), (1,), (2, 3))[k] if k < 4 else ():
            inner_part(r, i, block(i))
            refill(i + RING)
            to_partner(3 + i)
        if k == 4:
            takes["dh2"].wait()
            for i in range(4):
                normed_part(r, i, block(4 + i))
                refill(8 + i)
            for name in ("unit_one", "scale_one", "c"):
                takes[name].wait()
            first_norm_back(r)
            square_grad(r, 3)
            to_partner(7)
        if k == 5:
            output_back(r, block(8))
            for name in ("k", "q", "v", "p"):
                takes[name].wait()
        for i in {5: (0,), 6: (1,), 7: (2, 3)}.get(k, ()):
            attend_back(r, i // 2, (i % 2) * 3, (i % 2) * 3 + 3)
        if k == 8:
            takes["x"].wait()
            small_0()
            for i in range(3):
                square_grad(r, i)
                to_partner(8 + i)
        if k == 9:
            input_grads(r, block(9), block(10), block(11))
            dx_0()

    extra = {9: small_1st, 10: small_2nd, 11: small_3rd, 13: small_4th}
    depths = BACKWARD_DELAY
    stages = tuple(zip(depths, (stage_core, stage_y, stage_x, stage_z, stage_back, stage_end)))
    for step in range(count + depths[-1]):
        task(step)
        for depth, stage in stages:
            n = step - depth
            if 0 <= n < count:
                stage(n)
        if step in extra:
            extra[step]()
        if step == 10:
            dx_1()
        if step == count + depths[-1] - 2:
            dx_end()

    for n in range(count):
        sent(n)
    for j in range(3):
        await_bytes(small, s_send.at[j])
    await_bytes(dx_c, d_send)
    await_bytes(dx_sum, d_send)


def reduce_shapes():
    stages = [[] for _ in range(6)]
    for n, number in enumerate(ORDER):
        which, _, width = ITEMS[number]
        rows = SHARD_ROWS[which]
        part, width = rows // THIRDS[n], width // 2
        left = rows - part
        shapes = ((4, 2, rows, width), (4, 2, part, width), (4, left, width), (3, left, width), (left, width), (left, width))
        for stage, shape in zip(stages, shapes):
            stage.append(shape)
    return stages


def backward(weights, handed, vec, sums, dx_like):
    count = len(ITEMS)
    outs = [jax.ShapeDtypeStruct(s[2:], BF16) for s in GRAD_SHAPES]
    outs += [jax.ShapeDtypeStruct((16, 768), F32), jax.ShapeDtypeStruct(dx_like.shape, F32)]
    vmem, anywhere = pl.BlockSpec(memory_space=pltpu.VMEM), pl.BlockSpec(memory_space=pl.ANY)
    shape = (16, 768)
    return pl.pallas_call(
        backward_kernel,
        out_shape=outs,
        in_specs=[anywhere] * (6 + len(HANDED)) + [vmem] * 2,
        out_specs=[vmem] * 8,
        scratch_shapes=[pltpu.VMEM(s, BF16) for s in GRAD_SHAPES]
        + [pltpu.VMEM(*kind) for kind in BACKWARD_WORK.values()]
        + [pltpu.VMEM(shape_, BF16) for stage in reduce_shapes() for shape_ in stage]
        + [pltpu.VMEM(shape, F32)] * 3
        + [pltpu.VMEM((4,) + shape, F32)]
        + [pltpu.VMEM(shape, F32)] * 3
        + [
            pltpu.VMEM((2,) + dx_like.shape, BF16),
            pltpu.VMEM(dx_like.shape, BF16),
            pltpu.VMEM(dx_like.shape, BF16),
            pltpu.SemaphoreType.DMA((count,)),
            pltpu.SemaphoreType.DMA((count,)),
            pltpu.SemaphoreType.DMA((count,)),
            pltpu.SemaphoreType.DMA((count,)),
            pltpu.SemaphoreType.DMA((count, 3)),
            pltpu.SemaphoreType.DMA((count,)),
            pltpu.SemaphoreType.DMA((count,)),
            pltpu.SemaphoreType.DMA((4,)),
            pltpu.SemaphoreType.DMA((6,)),
            pltpu.SemaphoreType.DMA,
            pltpu.SemaphoreType.DMA((2,)),
            pltpu.SemaphoreType.DMA((len(HANDED),)),
            pltpu.SemaphoreType.DMA((12,)),
        ],
        compiler_params=pltpu.CompilerParams(
            collective_id=1, has_side_effects=True, vmem_limit_bytes=67043328
        ),
        name="backward",
    )(*weights, *handed, vec, sums)


def finish_kernel(*refs):
    shares, totals, dx, result = refs[0:6], refs[6], refs[7], refs[8]
    outs = refs[9:15]
    vectors_out = refs[15:24]
    dx_out, result_out, turned = refs[24:27]
    shard = lax.axis_index("shard")
    for share, out in zip(shares, outs):
        out[...] = share[...].astype(F32)
    dx_out[...] = dx[...]
    result_out[...] = result[...]
    turned[...] = pltpu.roll(totals[...], lax.rem(8 - shard, 8) * ROWS, 1)
    for row, out in zip(VECTOR_ROWS, vectors_out):
        if row is not None:
            out[...] = turned[row : row + 1, 0:ROWS]
    vectors_out[5][...] = totals[pl.ds(5 + shard // 2, 1), column(lax.rem(shard, 2) * 384, 384)]


def finish(shares, totals, dx, result):
    outs = [jax.ShapeDtypeStruct(s.shape, F32) for s in shares]
    outs += [jax.ShapeDtypeStruct((1, 384 if row is None else ROWS), F32) for row in VECTOR_ROWS]
    outs += [jax.ShapeDtypeStruct(dx.shape, F32), jax.ShapeDtypeStruct(result.shape, BF16)]
    vmem = pl.BlockSpec(memory_space=pltpu.VMEM)
    return pl.pallas_call(
        finish_kernel,
        out_shape=outs,
        in_specs=[vmem] * 9,
        out_specs=[vmem] * len(outs),
        scratch_shapes=[pltpu.VMEM((16, 768), F32)],
        compiler_params=pltpu.CompilerParams(vmem_limit_bytes=67043328),
        name="finish",
    )(*shares, totals, dx, result)


def per_device(
    inputs,
    lengths,
    w_query,
    b_query,
    w_key,
    w_value,
    b_value,
    w_output,
    b_output,
    gain_one,
    shift_one,
    w_inner,
    b_inner,
    w_outer,
    b_outer,
    gain_two,
    shift_two,
    cotangent,
):
    vectors_in = (b_query, b_value, b_output, gain_one, shift_one, b_inner, b_outer, gain_two, shift_two)
    weights = (w_query, w_key, w_value, w_output, w_inner, w_outer)
    first = forward(weights, [v.reshape(1, -1) for v in vectors_in], inputs, cotangent, lengths)
    wholes = [w.reshape(-1, w.shape[2]) for w in first[0:6]]
    (result, sums, vec), handed = first[6:9], first[9:]
    *shares, totals, dx = backward(wholes, handed, vec, sums, inputs)
    done = finish(shares, totals, dx, result)
    g_q, g_k, g_v, g_o, g_inner, g_outer = done[0:6]
    g_bq, g_bv, g_bo, g_g1, g_s1, g_bi, g_bouter, g_g2, g_s2 = [v.reshape(-1) for v in done[6:15]]
    return (
        done[16],
        done[15],
        g_q,
        g_bq,
        g_k,
        g_v,
        g_bv,
        g_o,
        g_bo,
        g_g1,
        g_s1,
        g_inner,
        g_bi,
        g_outer,
        g_bouter,
        g_g2,
        g_s2,
    )


def head_logits(query_seq, key_seq, length, factor):
    scores = (
        jnp.einsum("qhd,khd->hqk", query_seq, key_seq, preferred_element_type=jnp.float32) * factor
    )
    visible = jnp.arange(key_seq.shape[0]) < length
    return jnp.where(visible[None, None, :], scores, -1000000000.0)


def per_device_plain(
    inputs,
    lengths,
    w_query,
    b_query,
    w_key,
    w_value,
    b_value,
    w_output,
    b_output,
    gain_one,
    shift_one,
    w_inner,
    b_inner,
    w_outer,
    b_outer,
    gain_two,
    shift_two,
    cotangent,
):
    local_seqs, tok_dev, model_width = inputs.shape
    groups = lax.axis_size("seq")
    head_width = model_width // groups
    local_heads = head_width // HEAD_DIM
    factor = HEAD_DIM ** (-0.5)
    gathered = (
        lax.all_gather(w_query, "shard", axis=0, tiled=True),
        lax.all_gather(b_query, "shard", axis=0, tiled=True),
        lax.all_gather(w_key, "shard", axis=0, tiled=True),
        lax.all_gather(w_value, "shard", axis=0, tiled=True),
        lax.all_gather(b_value, "shard", axis=0, tiled=True),
        lax.all_gather(w_output, "shard", axis=0, tiled=True),
        lax.all_gather(b_output, "shard", axis=0, tiled=True),
        lax.all_gather(gain_one, "shard", axis=0, tiled=True),
        lax.all_gather(shift_one, "shard", axis=0, tiled=True),
        lax.all_gather(w_inner, "shard", axis=0, tiled=True),
        lax.all_gather(b_inner, "shard", axis=0, tiled=True),
        lax.all_gather(w_outer, "shard", axis=0, tiled=True),
        lax.all_gather(b_outer, "shard", axis=0, tiled=True),
        lax.all_gather(gain_two, "shard", axis=0, tiled=True),
        lax.all_gather(shift_two, "shard", axis=0, tiled=True),
    )
    (
        query_w,
        query_b,
        key_w,
        value_w,
        value_b,
        output_w,
        output_b,
        gain_a,
        shift_a,
        inner_w,
        inner_b,
        outer_w,
        outer_b,
        gain_b,
        shift_b,
    ) = gathered
    gain_first = gain_a.astype(jnp.float32)
    shift_first = shift_a.astype(jnp.float32)
    gain_second = gain_b.astype(jnp.float32)
    shift_second = shift_b.astype(jnp.float32)
    flat_rows = inputs.reshape(local_seqs * tok_dev, model_width)
    queries = (product(flat_rows, query_w) + query_b.astype(jnp.float32)).astype(jnp.bfloat16)
    key_rows = product(flat_rows, key_w).astype(jnp.bfloat16)
    values = (product(flat_rows, value_w) + value_b.astype(jnp.float32)).astype(jnp.bfloat16)
    shape_seq = (local_seqs, tok_dev, model_width)
    head_q, head_k, head_v = (
        lax.all_to_all(queries.reshape(shape_seq), "seq", split_axis=2, concat_axis=1, tiled=True),
        lax.all_to_all(key_rows.reshape(shape_seq), "seq", split_axis=2, concat_axis=1, tiled=True),
        lax.all_to_all(values.reshape(shape_seq), "seq", split_axis=2, concat_axis=1, tiled=True),
    )
    seq_len = head_q.shape[1]
    split = (local_seqs, seq_len, local_heads, HEAD_DIM)
    head_q = head_q.reshape(split)
    head_k = head_k.reshape(split)
    head_v = head_v.reshape(split)

    def attend(packed):
        query_seq, key_seq, value_seq, length = packed
        logits = head_logits(query_seq, key_seq, length, factor)
        row_max = jnp.max(logits, axis=-1, keepdims=True)
        shifted = jnp.exp(logits - row_max)
        row_total = jnp.sum(shifted, axis=-1, keepdims=True)
        weights = (shifted / row_total).astype(jnp.bfloat16)
        context = jnp.einsum("hqk,khd->qhd", weights, value_seq, preferred_element_type=jnp.float32)
        return (context.astype(jnp.bfloat16), (row_max + jnp.log(row_total))[..., 0])

    head_context, log_total = lax.map(attend, (head_q, head_k, head_v, lengths))
    back_shape = (local_seqs, seq_len, head_width)
    context = lax.all_to_all(
        head_context.reshape(back_shape), "seq", split_axis=1, concat_axis=2, tiled=True
    ).reshape(-1, model_width)
    branch = product(context, output_w) + output_b.astype(jnp.float32)
    summed = flat_rows.astype(jnp.float32) + branch
    normed = layer_norm(summed, gain_first, shift_first)
    normed_low = normed.astype(jnp.bfloat16)
    pre_inner = product(normed_low, inner_w) + inner_b.astype(jnp.float32)
    activated = jax.nn.gelu(pre_inner, approximate=False).astype(jnp.bfloat16)
    final_sum = normed + product(activated, outer_w) + outer_b.astype(jnp.float32)
    result = layer_norm(final_sum, gain_second, shift_second)
    grad_out = cotangent.reshape(-1, model_width).astype(jnp.float32)
    second_back = jax.vjp(layer_norm, final_sum, gain_second, shift_second)[1]
    grad_final, grad_gain_two, grad_shift_two = second_back(grad_out)
    grad_ffn = grad_final.astype(jnp.bfloat16)
    grad_w_outer = row_contract(activated, grad_ffn)
    grad_b_outer = column_sum(grad_ffn)
    grad_active = times_transposed(grad_ffn, outer_w)
    gelu_back = jax.vjp(partial(jax.nn.gelu, approximate=False), pre_inner)[1]
    grad_pre = gelu_back(grad_active)[0].astype(jnp.bfloat16)
    grad_w_inner = row_contract(normed_low, grad_pre)
    grad_b_inner = column_sum(grad_pre)
    grad_normed = grad_final + times_transposed(grad_pre, inner_w)
    first_back = jax.vjp(layer_norm, summed, gain_first, shift_first)[1]
    grad_summed, grad_gain_one, grad_shift_one = first_back(grad_normed)
    grad_branch = grad_summed.astype(jnp.bfloat16)
    grad_w_output = row_contract(context, grad_branch)
    grad_b_output = column_sum(grad_branch)
    grad_context = times_transposed(grad_branch, output_w).astype(jnp.bfloat16)
    grad_head_context = lax.all_to_all(
        grad_context.reshape(shape_seq), "seq", split_axis=2, concat_axis=1, tiled=True
    ).reshape(split)

    def attend_back(packed):
        query_seq, key_seq, value_seq, log_sum, grad_seq, length = packed
        logits = head_logits(query_seq, key_seq, length, factor)
        attn_probs = jnp.exp(logits - log_sum[..., None])
        weights = attn_probs.astype(jnp.bfloat16)
        grad_value = jnp.einsum(
            "hqk,qhd->khd", weights, grad_seq, preferred_element_type=jnp.float32
        )
        grad_probs = jnp.einsum(
            "qhd,khd->hqk", grad_seq, value_seq, preferred_element_type=jnp.float32
        )
        inner_sum = jnp.sum(grad_probs * attn_probs, axis=-1, keepdims=True)
        grad_scores = (attn_probs * (grad_probs - inner_sum)).astype(jnp.bfloat16)
        grad_query = (
            jnp.einsum("hqk,khd->qhd", grad_scores, key_seq, preferred_element_type=jnp.float32)
            * factor
        )
        grad_key = (
            jnp.einsum("hqk,qhd->khd", grad_scores, query_seq, preferred_element_type=jnp.float32)
            * factor
        )
        return (
            grad_query.astype(jnp.bfloat16),
            grad_key.astype(jnp.bfloat16),
            grad_value.astype(jnp.bfloat16),
        )

    head_gq, head_gk, head_gv = lax.map(
        attend_back, (head_q, head_k, head_v, log_total, grad_head_context, lengths)
    )
    tok_gq, tok_gk, tok_gv = (
        lax.all_to_all(head_gq.reshape(back_shape), "seq", split_axis=1, concat_axis=2, tiled=True),
        lax.all_to_all(head_gk.reshape(back_shape), "seq", split_axis=1, concat_axis=2, tiled=True),
        lax.all_to_all(head_gv.reshape(back_shape), "seq", split_axis=1, concat_axis=2, tiled=True),
    )
    grad_query = tok_gq.reshape(-1, model_width)
    grad_key = tok_gk.reshape(-1, model_width)
    grad_value = tok_gv.reshape(-1, model_width)
    grad_w_query = row_contract(flat_rows, grad_query)
    grad_b_query = column_sum(grad_query)
    grad_w_key = row_contract(flat_rows, grad_key)
    grad_w_value = row_contract(flat_rows, grad_value)
    grad_b_value = column_sum(grad_value)
    grad_rows = (
        grad_summed
        + times_transposed(grad_query, query_w)
        + times_transposed(grad_key, key_w)
        + times_transposed(grad_value, value_w)
    )
    local_grads = (
        grad_w_query,
        grad_b_query,
        grad_w_key,
        grad_w_value,
        grad_b_value,
        grad_w_output,
        grad_b_output,
        grad_gain_one,
        grad_shift_one,
        grad_w_inner,
        grad_b_inner,
        grad_w_outer,
        grad_b_outer,
        grad_gain_two,
        grad_shift_two,
    )
    shares = (
        lax.psum_scatter(local_grads[0], "shard", scatter_dimension=0, tiled=True),
        lax.psum_scatter(local_grads[1], "shard", scatter_dimension=0, tiled=True),
        lax.psum_scatter(local_grads[2], "shard", scatter_dimension=0, tiled=True),
        lax.psum_scatter(local_grads[3], "shard", scatter_dimension=0, tiled=True),
        lax.psum_scatter(local_grads[4], "shard", scatter_dimension=0, tiled=True),
        lax.psum_scatter(local_grads[5], "shard", scatter_dimension=0, tiled=True),
        lax.psum_scatter(local_grads[6], "shard", scatter_dimension=0, tiled=True),
        lax.psum_scatter(local_grads[7], "shard", scatter_dimension=0, tiled=True),
        lax.psum_scatter(local_grads[8], "shard", scatter_dimension=0, tiled=True),
        lax.psum_scatter(local_grads[9], "shard", scatter_dimension=0, tiled=True),
        lax.psum_scatter(local_grads[10], "shard", scatter_dimension=0, tiled=True),
        lax.psum_scatter(local_grads[11], "shard", scatter_dimension=0, tiled=True),
        lax.psum_scatter(local_grads[12], "shard", scatter_dimension=0, tiled=True),
        lax.psum_scatter(local_grads[13], "shard", scatter_dimension=0, tiled=True),
        lax.psum_scatter(local_grads[14], "shard", scatter_dimension=0, tiled=True),
    )
    summed_grads = (
        lax.psum(shares[0].astype(jnp.bfloat16), "seq").astype(jnp.float32),
        lax.psum(shares[1].astype(jnp.bfloat16), "seq").astype(jnp.float32),
        lax.psum(shares[2].astype(jnp.bfloat16), "seq").astype(jnp.float32),
        lax.psum(shares[3].astype(jnp.bfloat16), "seq").astype(jnp.float32),
        lax.psum(shares[4].astype(jnp.bfloat16), "seq").astype(jnp.float32),
        lax.psum(shares[5].astype(jnp.bfloat16), "seq").astype(jnp.float32),
        lax.psum(shares[6].astype(jnp.bfloat16), "seq").astype(jnp.float32),
        lax.psum(shares[7].astype(jnp.bfloat16), "seq").astype(jnp.float32),
        lax.psum(shares[8].astype(jnp.bfloat16), "seq").astype(jnp.float32),
        lax.psum(shares[9].astype(jnp.bfloat16), "seq").astype(jnp.float32),
        lax.psum(shares[10].astype(jnp.bfloat16), "seq").astype(jnp.float32),
        lax.psum(shares[11].astype(jnp.bfloat16), "seq").astype(jnp.float32),
        lax.psum(shares[12].astype(jnp.bfloat16), "seq").astype(jnp.float32),
        lax.psum(shares[13].astype(jnp.bfloat16), "seq").astype(jnp.float32),
        lax.psum(shares[14].astype(jnp.bfloat16), "seq").astype(jnp.float32),
    )
    return (
        result.astype(jnp.bfloat16).reshape(shape_seq),
        grad_rows.reshape(shape_seq),
        summed_grads[0],
        summed_grads[1],
        summed_grads[2],
        summed_grads[3],
        summed_grads[4],
        summed_grads[5],
        summed_grads[6],
        summed_grads[7],
        summed_grads[8],
        summed_grads[9],
        summed_grads[10],
        summed_grads[11],
        summed_grads[12],
        summed_grads[13],
        summed_grads[14],
    )


def solution(mesh):
    tuned = (mesh.shape["shard"], mesh.shape["seq"]) == (8, 4)
    return jax.shard_map(
        per_device if tuned else per_device_plain,
        mesh=mesh,
        in_specs=(
            P("shard", "seq", None),
            P("shard"),
            P("shard", None),
            P("shard"),
            P("shard", None),
            P("shard", None),
            P("shard"),
            P("shard", None),
            P("shard"),
            P("shard"),
            P("shard"),
            P("shard", None),
            P("shard"),
            P("shard", None),
            P("shard"),
            P("shard"),
            P("shard"),
            P("shard", "seq", None),
        ),
        out_specs=(
            P("shard", "seq", None),
            P("shard", "seq", None),
            P("shard", None),
            P("shard"),
            P("shard", None),
            P("shard", None),
            P("shard"),
            P("shard", None),
            P("shard"),
            P("shard"),
            P("shard"),
            P("shard", None),
            P("shard"),
            P("shard", None),
            P("shard"),
            P("shard"),
            P("shard"),
        ),
        check_vma=False,
    )
```

```python
from functools import partial
from types import SimpleNamespace

import jax
import jax.numpy as jnp
from jax import lax
from jax.experimental import pallas as pl
from jax.experimental.pallas import tpu as pltpu
from jax.sharding import PartitionSpec as P

HEAD_DIM = 64
BF16, F32 = jnp.bfloat16, jnp.float32
MESH = pl.DeviceIdType.MESH


epsilon = 1e-12


def layer_norm(tensor, norm_gain, norm_shift):
    average = jnp.mean(tensor, axis=-1, keepdims=True)
    centred = tensor - average
    variance = jnp.mean(centred * centred, axis=-1, keepdims=True)
    return centred * lax.rsqrt(variance + epsilon) * norm_gain + norm_shift


def product(operand, weight):
    return jnp.dot(operand, weight, preferred_element_type=jnp.float32)


def row_contract(operand, weight):
    return lax.dot_general(
        operand, weight, (((0,), (0,)), ((), ())), preferred_element_type=jnp.float32
    )


def times_transposed(operand, weight):
    return lax.dot_general(
        operand, weight, (((1,), (1,)), ((), ())), preferred_element_type=jnp.float32
    )


def column_sum(tensor):
    return jnp.sum(tensor.astype(jnp.float32), axis=0)


def place():
    shard, seq = lax.axis_index("shard"), lax.axis_index("seq")
    return shard // 2, lax.rem(shard, 2), seq // 2, lax.rem(seq, 2)


def device(z, x, y, core):
    return (z * 2 + x, y * 2 + core)


def send(src, dst, send_sem, recv_sem, where):
    copy = pltpu.make_async_remote_copy(
        src_ref=src,
        dst_ref=dst,
        send_sem=send_sem,
        recv_sem=recv_sem,
        device_id=where,
        device_id_type=MESH,
    )
    copy.start()
    return copy


def await_bytes(ref, sem):
    pltpu.make_async_copy(ref, ref, sem).wait()


def along_z(z):
    return (z + 1 - 2 * lax.rem(z, 2), lax.rem(z + 2, 4), 3 - z)


def greet(z, x, y, core):
    barrier = pltpu.get_barrier_semaphore()
    others = [device(lax.rem(z + j, 4), x, y, core) for j in (1, 2, 3)]
    others += [device(z, 1 - x, y, core), device(z, x, 1 - y, core), device(z, x, y, 1 - core)]
    for other in others:
        pl.semaphore_signal(barrier, inc=1, device_id=other, device_id_type=MESH)
    pl.semaphore_wait(barrier, len(others))


def at(start, size):
    return pl.ds(pl.multiple_of(start, 16), size)


ITEMS = [(w, 0, 768) for w in range(4)] + [(4, i * 768, 768) for i in range(4)] + [(5, i * 256, 256) for i in range(3)]
ROWS = 96
SHARD_ROWS = (96, 96, 96, 96, 96, 384)
WIDTHS = (768, 768, 768, 768, 3072, 768)
LEAD = 2
X_STEP = 2
FORWARD_DELAY = (1, 2, 4, 5)
BACKWARD_DELAY = (0, 1, 2, 4, 5, 6)
THIRDS = (3,) * len(ITEMS)


def half(item, core):
    which, first, width = item
    return pl.ds(pl.multiple_of(first + core * (width // 2), 128), width // 2)


def column(start, width):
    return pl.ds(pl.multiple_of(start, 128), width)


def head_masks():
    lane = lax.broadcasted_iota(jnp.int32, (1, 128), 1)
    low = (lane < HEAD_DIM).astype(F32)
    return (low.astype(BF16), (1.0 - low).astype(BF16))


def vectors(r):
    r.vec[...] = jnp.sum(r.small[...].astype(F32), axis=0)
    for i in range(4):
        r.b_inner[:, i * 768 : i * 768 + 768] = r.vec[5 + i : 6 + i, :]


def project_one(r, name):
    own = at(r.seq * 128, 128)
    for slot in range(2):

        @pl.loop(0, 3)
        def _(c):
            cols = column(c * 256, 256)
            if name == "q":
                r.q[slot, :, cols] = (product(r.x[slot, own, :], r.w_q[:, :, cols].reshape(768, 256)) + r.vec[0:1, cols]).astype(BF16)
            elif name == "k":
                r.k[slot, :, cols] = product(r.x[slot], r.w_k[:, :, cols].reshape(768, 256)).astype(BF16)
            else:
                r.v[slot, :, cols] = (product(r.x[slot], r.w_v[:, :, cols].reshape(768, 256)) + r.vec[1:2, cols]).astype(BF16)


def attend(r, slot, first, last):
    masks = head_masks()
    visible = lax.broadcasted_iota(jnp.int32, (512, 128), 0) < r.lengths[slot]

    @pl.loop(first, last)
    def _(p):
        cols = column(p * 128, 128)
        k, q, v = r.k[slot, :, cols], r.q[slot, :, cols], r.v[slot, :, cols]
        context = None
        for h in range(2):
            scores = times_transposed(k, q * masks[h]) * (HEAD_DIM**-0.5)
            logits = jnp.where(visible, scores, -1000000000.0)
            shifted = jnp.exp(logits - jnp.max(logits, axis=0, keepdims=True))
            probs = shifted * (1.0 / jnp.sum(shifted, axis=0, keepdims=True))
            low = probs.astype(BF16)
            r.p[slot, p * 2 + h] = low
            part = row_contract(low, v * masks[h])
            context = part if context is None else context + part
        r.c[slot, :, cols] = context.astype(BF16)


def norm_stats(rows):
    average = jnp.mean(rows, axis=-1, keepdims=True)
    centred = rows - average
    variance = jnp.mean(centred * centred, axis=-1, keepdims=True)
    scale = lax.rsqrt(variance + epsilon)
    return centred * scale, scale


def norm_back(grad, gain, unit, scale):
    g = grad * gain
    return scale * (
        g - jnp.mean(g, axis=-1, keepdims=True) - unit * jnp.mean(g * unit, axis=-1, keepdims=True)
    )


def first_norm(r):
    for slot in range(2):
        rows = pl.ds(slot * 128, 128)
        h1 = r.x[slot, at(r.seq * 128, 128), :].astype(F32) + product(r.c[slot], r.w_o[...].reshape(768, 768)) + r.vec[2:3, :]
        unit, scale = norm_stats(h1)
        r.unit_one[rows, :] = unit
        r.scale_one[rows, :] = jnp.broadcast_to(scale, (128, 128))
        n1 = unit * r.vec[3:4, :] + r.vec[4:5, :]
        r.n1[rows, :] = n1
        r.n1b[rows, :] = n1.astype(BF16)


def feed_in(r, i):
    @pl.loop(0, 3)
    def _(c):
        cols = column(i * 768 + c * 256, 256)
        u = product(r.n1b[...], r.w_inner[:, :, cols].reshape(768, 256)) + r.b_inner[:, cols]
        phi = 0.5 * (1.0 + lax.erf(u * 0.7071067811865476))
        r.g[:, cols] = (u * phi).astype(BF16)
        r.slope[:, cols] = (phi + u * (0.3989422804014327 * jnp.exp(-0.5 * u * u))).astype(BF16)


def feed_out(r, i):
    cols = pl.ds(i * 256, 256)
    r.dh2[:, cols] = r.n1[:, cols] + product(r.g[...], r.w_outer[:, :, cols].reshape(3072, 256)) + r.vec[9:10, cols]


def second_norm(r):
    for slot in range(2):
        rows = pl.ds(slot * 128, 128)
        unit, scale = norm_stats(r.dh2[rows, :])
        r.result[slot] = (unit * r.vec[10:11, :] + r.vec[11:12, :]).astype(BF16)
        grad = r.cot[slot].astype(F32)
        back = norm_back(grad, r.vec[10:11, :], unit, scale)
        low = back.astype(BF16)
        r.dh2[rows, :] = back
        r.df[rows, :] = low
        tally(r, slot, 10, grad * unit)
        tally(r, slot, 11, grad)
        tally(r, slot, 9, low.astype(F32))


def tally(r, slot, row, values):
    total = jnp.sum(values, axis=0, keepdims=True)
    r.sums[row : row + 1, :] = total if slot == 0 else r.sums[row : row + 1, :] + total


KINDS = {
    "place": ((16, 768), F32),
    "small_own": ((16, 768), BF16),
    "small": ((8, 16, 768), BF16),
    "b_inner": ((1, 3072), F32),
    "x": ((2, 512, 768), BF16),
    "q": ((2, 128, 768), BF16),
    "k": ((2, 512, 768), BF16),
    "v": ((2, 512, 768), BF16),
    "p": ((2, 12, 512, 128), BF16),
    "c": ((2, 128, 768), BF16),
    "unit_one": ((256, 768), F32),
    "scale_one": ((256, 128), F32),
    "n1": ((256, 768), F32),
    "n1b": ((256, 768), BF16),
    "g": ((256, 3072), BF16),
    "slope": ((256, 3072), BF16),
    "dh2": ((256, 768), F32),
    "df": ((256, 768), BF16),
    "da": ((2, 128, 768), BF16),
    "dc": ((2, 128, 768), BF16),
    "dq": ((2, 128, 768), BF16),
    "dk": ((2, 512, 768), BF16),
    "dv": ((2, 512, 768), BF16),
    "dx_own": ((2, 128, 768), F32),
    "dx_part": ((2, 512, 768), BF16),
    "sums": ((16, 768), F32),
    "ring": ((4, 768, 768), BF16),
}


def kinds(*names):
    return {name: KINDS[name] for name in names}


VECTOR_ROWS = (0, 1, 2, 3, 4, None, 9, 10, 11)
HANDED = ("x", "q", "k", "v", "p", "c", "unit_one", "scale_one", "n1b", "g", "slope", "dh2", "df")

FORWARD_WORK = kinds(
    "place", "small_own", "small", "b_inner", "x", "q", "k", "v", "p", "c", "unit_one", "scale_one", "n1", "n1b", "g",
    "slope", "dh2", "df",
)

def place_vectors(r, shard):
    r.place[...] = jnp.zeros_like(r.place)
    for row, ref in zip(VECTOR_ROWS, r.vectors):
        if row is not None:
            r.place[row : row + 1, 0:ROWS] = ref[...].astype(F32)
    r.place[...] = pltpu.roll(r.place[...], shard * ROWS, 1)
    r.place[pl.ds(5 + shard // 2, 1), column(lax.rem(shard, 2) * 384, 384)] = r.vectors[5][...].astype(F32).reshape(1, 384)
    r.small_own[...] = r.place[...].astype(BF16)


def forward_kernel(*refs):
    own = refs[0:6]
    r = SimpleNamespace(vectors=refs[6:15])
    x_own, r.cot, r.lengths = refs[15:18]
    kept = refs[18:24]
    r.result, r.sums, r.vec = refs[24:27]
    handed = dict(zip(HANDED, refs[27:40]))
    full = refs[40:46]
    rest = list(refs[46:])
    for name in FORWARD_WORK:
        setattr(r, name, rest.pop(0))
    r.w_q, r.w_k, r.w_v, r.w_o, r.w_inner, r.w_outer = full
    small_own, small_full, x_full = r.small_own, r.small, r.x
    send_sem, z_sem, x_sem, y_sem, c_sem, local_sem, own_sem, extra_send, extra_recv, keep_sem = rest
    z, x, y, core = place()
    shard = z * 2 + x
    seq = y * 2 + core
    r.seq = seq
    place_vectors(r, shard)
    r.sums[...] = jnp.zeros_like(r.sums)
    greet(z, x, y, core)
    to_x = device(z, 1 - x, y, core)
    to_y = device(z, x, 1 - y, core)
    to_c = device(z, x, y, 1 - core)
    others = along_z(z)

    def shard_at(back, side):
        return lax.rem(z + 4 - back, 4) * 2 + side

    def kept_rows(n):
        rows = SHARD_ROWS[ITEMS[n][0]]
        return rows, rows // 3

    def block(n, owner, begin, size):
        return full[ITEMS[n][0]].at[owner, at(begin, size), half(ITEMS[n], core)]

    def carried(n, owner):
        rows, third = kept_rows(n)
        return block(n, owner, y * third, rows - third)

    def for_y(n, owner):
        rows, third = kept_rows(n)
        return block(n, owner, y * (rows - third), third)

    mine = x_full.at[:, at(seq * 128, 128), :]
    x_local = pltpu.make_async_copy(x_own, mine, local_sem.at[0])
    x_local.start()
    s_local = pltpu.make_async_copy(small_own, small_full.at[shard], local_sem.at[1])
    s_local.start()

    def start(n):
        rows, third = kept_rows(n)
        src = own[ITEMS[n][0]].at[at(y * third, rows - third), half(ITEMS[n], core)]
        for m in (1, 0):
            send(src, carried(n, shard), send_sem.at[n], z_sem.at[n, m], device(others[m], x, y, core))
        send(src, carried(n, shard), send_sem.at[n], x_sem.at[n, 0], to_x)

    start(0)
    send(x_own, mine, extra_send.at[0], extra_recv.at[0], to_y)
    send(x_own, mine, extra_send.at[0], extra_recv.at[1], to_c)
    for j in (1, 2, 3):
        there = device(lax.rem(z + j, 4), x, y, core)
        send(small_own, small_full.at[shard], extra_send.at[1], extra_recv.at[1 + j], there)
    send(small_own, small_full.at[shard], extra_send.at[1], extra_recv.at[5], to_x)
    for n in range(1, LEAD):
        start(n)
    locals_ = []
    for n, item in enumerate(ITEMS):
        rows = SHARD_ROWS[item[0]]
        copy = pltpu.make_async_copy(own[item[0]].at[:, half(item, core)], block(n, shard, 0, rows), own_sem.at[n])
        copy.start()
        locals_.append(copy)

    def pass_on(n, m):
        owner = others[m] * 2 + x
        got = carried(n, owner)
        await_bytes(got, z_sem.at[n, m])
        if m == 1:
            send(got, got, send_sem.at[n], z_sem.at[n, 2], device(others[0], x, y, core))
        send(got, got, send_sem.at[n], x_sem.at[n, 1 + m], to_x)
        send(for_y(n, owner), for_y(n, owner), send_sem.at[n], y_sem.at[n], to_y)

    def from_z(n):
        pass_on(n, 0)
        pass_on(n, 1)

    def from_far_z(n):
        pass_on(n, 2)

    def from_x(n):
        for j in range(4):
            owner = (z if j == 0 else others[j - 1]) * 2 + 1 - x
            await_bytes(carried(n, owner), x_sem.at[n, j])
            send(for_y(n, owner), for_y(n, owner), send_sem.at[n], y_sem.at[n], to_y)

    def some(n, owners, rows):
        return full[ITEMS[n][0]].at[pl.ds(0, owners), pl.ds(0, rows), half(ITEMS[n], core)]

    def from_y(n):
        rows, third = kept_rows(n)
        await_bytes(some(n, 7, third), y_sem.at[n])
        locals_[n].wait()
        whole = some(n, 8, rows)
        send(whole, whole, send_sem.at[n], c_sem.at[n], to_c)

    def from_c(n):
        await_bytes(some(n, 8, SHARD_ROWS[ITEMS[n][0]]), c_sem.at[n])

    def sent(n):
        rows, third = kept_rows(n)
        await_bytes(some(n, 7, rows - third), send_sem.at[n])
        await_bytes(some(n, 7, third), send_sem.at[n])
        await_bytes(some(n, 8, rows), send_sem.at[n])

    def small_relay():
        for j in (1, 2, 3):
            there = small_full.at[shard_at(j, x)]
            await_bytes(there, extra_recv.at[1 + j])
            send(there, there, extra_send.at[1], extra_recv.at[5 + j], to_x)

    def x_relay():
        theirs = x_full.at[:, at(((1 - y) * 2 + core) * 128, 128), :]
        await_bytes(theirs, extra_recv.at[0])
        send(theirs, theirs, extra_send.at[0], extra_recv.at[1], to_c)

    keeps = []

    def keep(src, dst):
        copy = pltpu.make_async_copy(src, dst, keep_sem.at[len(keeps)])
        copy.start()
        keeps.append(copy)

    def hand(*names):
        for name in names:
            keep(getattr(r, name), handed[name])

    def arrive():
        for j in range(4):
            await_bytes(small_full.at[shard_at(j, 1 - x)], extra_recv.at[5 + j])
        await_bytes(x_full.at[:, pl.ds(0, 256), :], extra_recv.at[1])
        x_local.wait()
        s_local.wait()
        vectors(r)
        hand("x")

    def after(n):
        if n == 0:
            arrive()
            project_one(r, "q")
            hand("q")
        elif n == 1:
            project_one(r, "k")
            hand("k")
        elif n == 2:
            project_one(r, "v")
            hand("v")
        if 2 <= n <= 5:
            attend(r, (n - 2) // 2, (n % 2) * 3, (n % 2) * 3 + 3)
        if n == 5:
            hand("p", "c")
            first_norm(r)
            hand("unit_one", "scale_one", "n1b")
            feed_in(r, 0)
        if n == 6:
            feed_in(r, 1)
            feed_in(r, 2)
        if n == 7:
            feed_in(r, 3)
            hand("g", "slope")
        if n >= 8:
            feed_out(r, n - 8)
        if n in (0, 1, 2, 3, 7, 10):
            which = ITEMS[n][0]
            keep(full[which], kept[which])

    delay = FORWARD_DELAY
    stages = ((0, from_z),) + tuple(zip(delay, (from_far_z, from_x, from_y, from_c)))
    for step in range(len(ITEMS) + delay[-1]):
        if step + LEAD < len(ITEMS):
            start(step + LEAD)
        if step == 1:
            small_relay()
        if step == X_STEP:
            x_relay()
        for depth, stage in stages:
            n = step - depth
            if 0 <= n < len(ITEMS):
                stage(n)
        n = step - delay[-1]
        if 0 <= n < len(ITEMS):
            after(n)

    second_norm(r)
    hand("dh2", "df")
    await_bytes(x_full.at[:, pl.ds(0, 384), :], extra_send.at[0])
    await_bytes(small_full.at[pl.ds(0, 7)], extra_send.at[1])
    for n in range(len(ITEMS)):
        sent(n)
    for copy in keeps:
        copy.wait()


def forward(weights, vectors_in, inputs, cotangent, lengths):
    count = len(ITEMS)
    wholes = [(8,) + w.shape for w in weights]
    outs = [jax.ShapeDtypeStruct(shape, BF16) for shape in wholes]
    outs += [
        jax.ShapeDtypeStruct(cotangent.shape, BF16),
        jax.ShapeDtypeStruct((16, 768), F32),
        jax.ShapeDtypeStruct((16, 768), F32),
    ]
    outs += [jax.ShapeDtypeStruct(*FORWARD_WORK[name]) for name in HANDED]
    vmem, anywhere = pl.BlockSpec(memory_space=pltpu.VMEM), pl.BlockSpec(memory_space=pl.ANY)
    return pl.pallas_call(
        forward_kernel,
        out_shape=outs,
        in_specs=[vmem] * 17 + [pl.BlockSpec(memory_space=pltpu.SMEM)],
        out_specs=[anywhere] * 6 + [vmem] * 3 + [anywhere] * len(HANDED),
        scratch_shapes=[pltpu.VMEM(shape, BF16) for shape in wholes]
        + [pltpu.VMEM(*kind) for kind in FORWARD_WORK.values()]
        + [
            pltpu.SemaphoreType.DMA((count,)),
            pltpu.SemaphoreType.DMA((count, 3)),
            pltpu.SemaphoreType.DMA((count, 4)),
            pltpu.SemaphoreType.DMA((count,)),
            pltpu.SemaphoreType.DMA((count,)),
            pltpu.SemaphoreType.DMA((2,)),
            pltpu.SemaphoreType.DMA((count,)),
            pltpu.SemaphoreType.DMA((2,)),
            pltpu.SemaphoreType.DMA((9,)),
            pltpu.SemaphoreType.DMA((6 + len(HANDED),)),
        ],
        compiler_params=pltpu.CompilerParams(
            collective_id=0, has_side_effects=True, vmem_limit_bytes=60 * 2**20
        ),
        name="forward",
    )(*weights, *vectors_in, inputs, cotangent, lengths)


ORDER = (8, 9, 10, 4, 5, 6, 7, 3, 0, 1, 2)
RING = 4
TAKE_ORDER = ("g", "df", "slope", "n1b", "dh2", "unit_one", "scale_one", "c", "k", "q", "v", "p", "x")
GRAD_SHAPES = [(4, 2, rows, width) for rows, width in zip(SHARD_ROWS, WIDTHS)]

BACKWARD_WORK = kinds(
    "x", "q", "k", "v", "p", "c", "unit_one", "scale_one", "n1b", "g", "slope", "dh2", "df", "da", "dc", "dq", "dk", "dv",
    "dx_own", "dx_part", "sums", "ring",
)

def ring_load(r, j):
    if j < 4:
        src = r.w_outer.at[pl.ds(j * 768, 768), :]
    elif j < 8:
        src = r.w_inner.at[:, pl.ds((j - 4) * 768, 768)]
    else:
        src = (r.w_o, r.w_q, r.w_k, r.w_v)[j - 8]
    copy = pltpu.make_async_copy(src, r.ring.at[j % RING], r.ring_sem.at[j])
    copy.start()
    return copy


def outer_grad(r, i):
    cols = pl.ds(i * 256, 256)
    for c in range(8):
        left = r.g[:, c * 384 : c * 384 + 384]
        r.grads[5][c // 2, c % 2, :, cols] = row_contract(left, r.df[:, cols]).astype(BF16)


def inner_part(r, i, weight):
    @pl.loop(0, 3)
    def _(c):
        cols = column(i * 768 + c * 256, 256)
        low = (times_transposed(r.df[...], weight[at(c * 256, 256), :]) * r.slope[:, cols].astype(F32)).astype(BF16)
        r.slope[:, cols] = low
        r.sums[5 + i : 6 + i, column(c * 256, 256)] = jnp.sum(low.astype(F32), axis=0, keepdims=True)
        r.grads[4][:, :, :, cols] = row_contract(r.n1b[...], low).astype(BF16).reshape(4, 2, ROWS, 256)


def normed_part(r, i, weight):
    r.dh2[...] = r.dh2[...] + times_transposed(r.slope[:, i * 768 : i * 768 + 768], weight[...])


def first_norm_back(r):
    for slot in range(2):
        rows = pl.ds(slot * 128, 128)
        dn1 = r.dh2[rows, :]
        unit = r.unit_one[rows, :]
        back = norm_back(dn1, r.vec[3:4, :], unit, r.scale_one[rows, 0:1])
        low = back.astype(BF16)
        r.da[slot] = low
        tally(r, slot, 3, dn1 * unit)
        tally(r, slot, 4, dn1)
        tally(r, slot, 2, low.astype(F32))
        r.dx_own[slot] = back


def output_back(r, weight):
    for slot in range(2):
        r.dc[slot] = times_transposed(r.da[slot], weight[...]).astype(BF16)


def attend_back(r, slot, first, last):
    masks = head_masks()
    factor = HEAD_DIM**-0.5

    @pl.loop(first, last)
    def _(p):
        cols = column(p * 128, 128)
        k, q, v, dc = r.k[slot, :, cols], r.q[slot, :, cols], r.v[slot, :, cols], r.dc[slot, :, cols]
        dq = dk = dv = None
        for h in range(2):
            low = r.p[slot, p * 2 + h]
            probs = low.astype(F32)
            dch = dc * masks[h]
            dp = times_transposed(v, dch)
            inner = jnp.sum(dp * probs, axis=0, keepdims=True)
            ds = (probs * (dp - inner)).astype(BF16)
            parts = (row_contract(ds, k * masks[h]), product(ds, q * masks[h]), product(low, dch))
            dq, dk, dv = parts if dq is None else (dq + parts[0], dk + parts[1], dv + parts[2])
        dq = (dq * factor).astype(BF16)
        dv = dv.astype(BF16)
        r.dq[slot, :, cols] = dq
        r.dk[slot, :, cols] = (dk * factor).astype(BF16)
        r.dv[slot, :, cols] = dv
        dq_sum = jnp.sum(dq.astype(F32), axis=0, keepdims=True)
        dv_sum = jnp.sum(dv.astype(F32), axis=0, keepdims=True)
        if slot == 0:
            r.sums[0:1, cols] = dq_sum
            r.sums[1:2, cols] = dv_sum
        else:
            r.sums[0:1, cols] = r.sums[0:1, cols] + dq_sum
            r.sums[1:2, cols] = r.sums[1:2, cols] + dv_sum


def square_grad(r, which):
    own = at(r.seq * 128, 128)

    @pl.loop(0, 2)
    def _(c):
        cols = column(c * 384, 384)
        value = None
        for s in range(2):
            left, right = (
                (r.x[s, own, cols], r.dq[s]),
                (r.x[s, :, cols], r.dk[s]),
                (r.x[s, :, cols], r.dv[s]),
                (r.c[s, :, cols], r.da[s]),
            )[which]
            piece = row_contract(left, right)
            value = piece if value is None else value + piece
        r.grads[which][pl.ds(c * 2, 2)] = value.astype(BF16).reshape(2, 2, ROWS, 768)


def input_grads(r, w_q, w_k, w_v):
    for slot in range(2):
        r.dx_own[slot] = r.dx_own[slot] + times_transposed(r.dq[slot], w_q[...])

        @pl.loop(0, 3)
        def _(c):
            rows = at(c * 256, 256)
            r.dx_part[slot, :, column(c * 256, 256)] = (
                times_transposed(r.dk[slot], w_k[rows, :]) + times_transposed(r.dv[slot], w_v[rows, :])
            ).astype(BF16)


def backward_kernel(*refs):
    r = SimpleNamespace()
    r.w_q, r.w_k, r.w_v, r.w_o, r.w_inner, r.w_outer = refs[0:6]
    taken = dict(zip(HANDED, refs[6:19]))
    r.vec, sums_in = refs[19:21]
    out = refs[21:27]
    small_out, dx_out = refs[27:29]
    r.grads = refs[29:35]
    rest = list(refs[35:])
    for name in BACKWARD_WORK:
        setattr(r, name, rest.pop(0))
    count = len(ITEMS)
    from_core, from_y, from_x, from_z, total, back_y = [rest[i * count : i * count + count] for i in range(6)]
    rest = rest[6 * count :]
    (small_c, small_y, small_x, small_z, small_1, small_2, small_3, dx_c, dx_sum, dx_y) = rest[0:10]
    send_sem, c_sem, y_sem, x_sem, z_sem, fy_sem, fc_sem, s_send, s_recv, d_send, d_recv = rest[10:21]
    r.take_sem, r.ring_sem = rest[21:23]
    f32 = F32
    small = r.sums
    z, x, y, core = place()
    seq = y * 2 + core
    r.seq = seq
    takes = {}
    for i, name in enumerate(TAKE_ORDER):
        if name == "slope":
            loads = [ring_load(r, j) for j in range(RING)]
        takes[name] = pltpu.make_async_copy(taken[name], getattr(r, name), r.take_sem.at[i])
        takes[name].start()
    r.sums[...] = sums_in[...]
    greet(z, x, y, core)
    to_x = device(z, 1 - x, y, core)
    to_y = device(z, x, 1 - y, core)
    to_c = device(z, x, y, 1 - core)

    def parts(n):
        rows = SHARD_ROWS[ITEMS[ORDER[n]][0]]
        return rows, rows // THIRDS[n]

    def grad(n, side=core):
        item = ITEMS[ORDER[n]]
        return r.grads[item[0]].at[:, :, :, half(item, side)]

    def to_partner(n):
        send(grad(n, 1 - core), from_core[n], send_sem.at[n], c_sem.at[n], to_c)

    def add(ref, *others):
        value = ref[...].astype(f32)
        for other in others:
            value = value + other[...].astype(f32)
        ref[...] = value.astype(BF16)

    def stage_core(n):
        rows, part = parts(n)
        await_bytes(from_core[n], c_sem.at[n])
        far = at((1 - y) * (rows - part), part)
        add(grad(n).at[:, :, far, :], from_core[n].at[:, :, far, :])
        send(grad(n).at[:, :, far, :], from_y[n], send_sem.at[n], y_sem.at[n], to_y)
        middle = pl.ds(part, rows - 2 * part)
        add(grad(n).at[:, :, middle, :], from_core[n].at[:, :, middle, :])

    def stage_y(n):
        rows, part = parts(n)
        await_bytes(from_y[n], y_sem.at[n])
        near = at(y * (rows - part), part)
        add(grad(n).at[:, :, near, :], from_core[n].at[:, :, near, :], from_y[n])
        carried = at(y * part, rows - part)
        send(grad(n).at[:, 1 - x, carried, :], from_x[n], send_sem.at[n], x_sem.at[n], to_x)

    def stage_x(n):
        rows, part = parts(n)
        await_bytes(from_x[n], x_sem.at[n])
        carried = at(y * part, rows - part)
        add(grad(n).at[:, x, carried, :], from_x[n])
        for j in (2, 1, 3):
            there = lax.rem(z + j, 4)
            send(
                grad(n).at[there, x, carried, :],
                from_z[n].at[j - 1],
                send_sem.at[n],
                z_sem.at[n, j - 1],
                device(there, x, y, core),
            )

    def stage_z(n):
        rows, part = parts(n)
        for j in range(3):
            await_bytes(from_z[n].at[j], z_sem.at[n, j])
        value = grad(n).at[z, x, at(y * part, rows - part), :][...].astype(f32)
        for j in range(3):
            value = value + from_z[n][j].astype(f32)
        total[n][...] = value.astype(BF16)
        send(total[n], back_y[n], send_sem.at[n], fy_sem.at[n], to_y)

    def shares(n):
        item = ITEMS[ORDER[n]]
        return out[item[0]].at[:, half(item, core)]

    def stage_back(n):
        rows, part = parts(n)
        await_bytes(back_y[n], fy_sem.at[n])
        middle = rows - 2 * part
        place_ = shares(n)
        place_[at(y * (rows - part), part), :] = total[n][at(y * middle, part), :]
        place_[at((1 - y) * (rows - part), part), :] = back_y[n][at((1 - y) * middle, part), :]
        place_[pl.ds(part, middle), :] = (
            total[n][at((1 - y) * part, middle), :].astype(f32) + back_y[n][at(y * part, middle), :].astype(f32)
        ).astype(BF16)
        send(place_, place_, send_sem.at[n], fc_sem.at[n], to_c)

    def stage_end(n):
        await_bytes(shares(n), fc_sem.at[n])

    def sent(n):
        for ref in (from_core[n], from_y[n], from_x[n], from_z[n], total[n], shares(n)):
            await_bytes(ref, send_sem.at[n])

    def dx_rows(who):
        return r.dx_part.at[:, at(who * 128, 128), :]

    def dx_0():
        send(dx_rows((1 - y) * 2 + 1 - core), dx_c.at[1], d_send, d_recv.at[0], to_c)
        send(dx_rows(y * 2 + 1 - core), dx_c.at[0], d_send, d_recv.at[0], to_c)

    def dx_1():
        await_bytes(dx_c, d_recv.at[0])
        dx_sum[...] = (dx_rows((1 - y) * 2 + core)[...].astype(f32) + dx_c[1].astype(f32)).astype(BF16)
        send(dx_sum, dx_y, d_send, d_recv.at[1], to_y)

    def dx_end():
        await_bytes(dx_y, d_recv.at[1])
        dx_out[...] = (
            r.dx_own[...] + dx_rows(seq)[...].astype(f32) + dx_c[0].astype(f32) + dx_y[...].astype(f32)
        )

    def small_0():
        send(small, small_c, s_send.at[0], s_recv.at[0], to_c)

    def small_1st():
        await_bytes(small_c, s_recv.at[0])
        small_1[...] = small[...] + small_c[...]
        send(small_1, small_y, s_send.at[1], s_recv.at[1], to_y)

    def small_2nd():
        await_bytes(small_y, s_recv.at[1])
        small_2[...] = small_1[...] + small_y[...]
        send(small_2, small_x, s_send.at[2], s_recv.at[2], to_x)

    def small_3rd():
        await_bytes(small_x, s_recv.at[2])
        small_3[...] = small_2[...] + small_x[...]
        for j in (1, 2, 3):
            send(small_3, small_z.at[z], s_send.at[3], s_recv.at[2 + j], device(lax.rem(z + j, 4), x, y, core))

    def small_4th():
        for j in (1, 2, 3):
            await_bytes(small_z.at[lax.rem(z + 4 - j, 4)], s_recv.at[2 + j])
        await_bytes(small_z.at[pl.ds(0, 3)], s_send.at[3])
        small_z[z] = small_3[...]
        small_out[...] = ((small_z[0] + small_z[1]) + small_z[2]) + small_z[3]

    def block(j):
        loads[j].wait()
        return r.ring.at[j % RING]

    def refill(j):
        loads.append(ring_load(r, j))

    def task(k):
        if k == 0:
            takes["g"].wait()
            takes["df"].wait()
            for i in range(2):
                outer_grad(r, i)
                to_partner(i)
        if k == 1:
            outer_grad(r, 2)
            to_partner(2)
            takes["slope"].wait()
            takes["n1b"].wait()
        for i in ((), (0,), (1,), (2, 3))[k] if k < 4 else ():
            inner_part(r, i, block(i))
            refill(i + RING)
            to_partner(3 + i)
        if k == 4:
            takes["dh2"].wait()
            for i in range(4):
                normed_part(r, i, block(4 + i))
                refill(8 + i)
            for name in ("unit_one", "scale_one", "c"):
                takes[name].wait()
            first_norm_back(r)
            square_grad(r, 3)
            to_partner(7)
        if k == 5:
            output_back(r, block(8))
            for name in ("k", "q", "v", "p"):
                takes[name].wait()
        for i in {5: (0,), 6: (1,), 7: (2, 3)}.get(k, ()):
            attend_back(r, i // 2, (i % 2) * 3, (i % 2) * 3 + 3)
        if k == 8:
            takes["x"].wait()
            small_0()
            for i in range(3):
                square_grad(r, i)
                to_partner(8 + i)
        if k == 9:
            input_grads(r, block(9), block(10), block(11))
            dx_0()

    extra = {9: small_1st, 10: small_2nd, 11: small_3rd, 13: small_4th}
    depths = BACKWARD_DELAY
    stages = tuple(zip(depths, (stage_core, stage_y, stage_x, stage_z, stage_back, stage_end)))
    for step in range(count + depths[-1]):
        task(step)
        for depth, stage in stages:
            n = step - depth
            if 0 <= n < count:
                stage(n)
        if step in extra:
            extra[step]()
        if step == 10:
            dx_1()
        if step == count + depths[-1] - 2:
            dx_end()

    for n in range(count):
        sent(n)
    for j in range(3):
        await_bytes(small, s_send.at[j])
    await_bytes(dx_c, d_send)
    await_bytes(dx_sum, d_send)


def reduce_shapes():
    stages = [[] for _ in range(6)]
    for n, number in enumerate(ORDER):
        which, _, width = ITEMS[number]
        rows = SHARD_ROWS[which]
        part, width = rows // THIRDS[n], width // 2
        left = rows - part
        shapes = ((4, 2, rows, width), (4, 2, part, width), (4, left, width), (3, left, width), (left, width), (left, width))
        for stage, shape in zip(stages, shapes):
            stage.append(shape)
    return stages


def backward(weights, handed, vec, sums, dx_like):
    count = len(ITEMS)
    outs = [jax.ShapeDtypeStruct(s[2:], BF16) for s in GRAD_SHAPES]
    outs += [jax.ShapeDtypeStruct((16, 768), F32), jax.ShapeDtypeStruct(dx_like.shape, F32)]
    vmem, anywhere = pl.BlockSpec(memory_space=pltpu.VMEM), pl.BlockSpec(memory_space=pl.ANY)
    shape = (16, 768)
    return pl.pallas_call(
        backward_kernel,
        out_shape=outs,
        in_specs=[anywhere] * (6 + len(HANDED)) + [vmem] * 2,
        out_specs=[vmem] * 8,
        scratch_shapes=[pltpu.VMEM(s, BF16) for s in GRAD_SHAPES]
        + [pltpu.VMEM(*kind) for kind in BACKWARD_WORK.values()]
        + [pltpu.VMEM(shape_, BF16) for stage in reduce_shapes() for shape_ in stage]
        + [pltpu.VMEM(shape, F32)] * 3
        + [pltpu.VMEM((4,) + shape, F32)]
        + [pltpu.VMEM(shape, F32)] * 3
        + [
            pltpu.VMEM((2,) + dx_like.shape, BF16),
            pltpu.VMEM(dx_like.shape, BF16),
            pltpu.VMEM(dx_like.shape, BF16),
            pltpu.SemaphoreType.DMA((count,)),
            pltpu.SemaphoreType.DMA((count,)),
            pltpu.SemaphoreType.DMA((count,)),
            pltpu.SemaphoreType.DMA((count,)),
            pltpu.SemaphoreType.DMA((count, 3)),
            pltpu.SemaphoreType.DMA((count,)),
            pltpu.SemaphoreType.DMA((count,)),
            pltpu.SemaphoreType.DMA((4,)),
            pltpu.SemaphoreType.DMA((6,)),
            pltpu.SemaphoreType.DMA,
            pltpu.SemaphoreType.DMA((2,)),
            pltpu.SemaphoreType.DMA((len(HANDED),)),
            pltpu.SemaphoreType.DMA((12,)),
        ],
        compiler_params=pltpu.CompilerParams(
            collective_id=1, has_side_effects=True, vmem_limit_bytes=67043328
        ),
        name="backward",
    )(*weights, *handed, vec, sums)


def finish_kernel(*refs):
    shares, totals, dx, result = refs[0:6], refs[6], refs[7], refs[8]
    outs = refs[9:15]
    vectors_out = refs[15:24]
    dx_out, result_out, turned = refs[24:27]
    shard = lax.axis_index("shard")
    for share, out in zip(shares, outs):
        out[...] = share[...].astype(F32)
    dx_out[...] = dx[...]
    result_out[...] = result[...]
    turned[...] = pltpu.roll(totals[...], lax.rem(8 - shard, 8) * ROWS, 1)
    for row, out in zip(VECTOR_ROWS, vectors_out):
        if row is not None:
            out[...] = turned[row : row + 1, 0:ROWS]
    vectors_out[5][...] = totals[pl.ds(5 + shard // 2, 1), column(lax.rem(shard, 2) * 384, 384)].reshape(384)


def finish(shares, totals, dx, result):
    outs = [jax.ShapeDtypeStruct(s.shape, F32) for s in shares]
    outs += [jax.ShapeDtypeStruct((384,) if row is None else (1, ROWS), F32) for row in VECTOR_ROWS]
    outs += [jax.ShapeDtypeStruct(dx.shape, F32), jax.ShapeDtypeStruct(result.shape, BF16)]
    vmem = pl.BlockSpec(memory_space=pltpu.VMEM)
    return pl.pallas_call(
        finish_kernel,
        out_shape=outs,
        in_specs=[vmem] * 9,
        out_specs=[vmem] * len(outs),
        scratch_shapes=[pltpu.VMEM((16, 768), F32)],
        compiler_params=pltpu.CompilerParams(vmem_limit_bytes=67043328),
        name="finish",
    )(*shares, totals, dx, result)


def per_device(
    inputs,
    lengths,
    w_query,
    b_query,
    w_key,
    w_value,
    b_value,
    w_output,
    b_output,
    gain_one,
    shift_one,
    w_inner,
    b_inner,
    w_outer,
    b_outer,
    gain_two,
    shift_two,
    cotangent,
):
    vectors_in = (b_query, b_value, b_output, gain_one, shift_one, b_inner, b_outer, gain_two, shift_two)
    weights = (w_query, w_key, w_value, w_output, w_inner, w_outer)
    first = forward(weights, [v if v is b_inner else v.reshape(1, -1) for v in vectors_in], inputs, cotangent, lengths)
    wholes = [w.reshape(-1, w.shape[2]) for w in first[0:6]]
    (result, sums, vec), handed = first[6:9], first[9:]
    *shares, totals, dx = backward(wholes, handed, vec, sums, inputs)
    done = finish(shares, totals, dx, result)
    g_q, g_k, g_v, g_o, g_inner, g_outer = done[0:6]
    g_bq, g_bv, g_bo, g_g1, g_s1, g_bi, g_bouter, g_g2, g_s2 = [v.reshape(-1) for v in done[6:15]]
    return (
        done[16],
        done[15],
        g_q,
        g_bq,
        g_k,
        g_v,
        g_bv,
        g_o,
        g_bo,
        g_g1,
        g_s1,
        g_inner,
        g_bi,
        g_outer,
        g_bouter,
        g_g2,
        g_s2,
    )


def head_logits(query_seq, key_seq, length, factor):
    scores = (
        jnp.einsum("qhd,khd->hqk", query_seq, key_seq, preferred_element_type=jnp.float32) * factor
    )
    visible = jnp.arange(key_seq.shape[0]) < length
    return jnp.where(visible[None, None, :], scores, -1000000000.0)


def per_device_plain(
    inputs,
    lengths,
    w_query,
    b_query,
    w_key,
    w_value,
    b_value,
    w_output,
    b_output,
    gain_one,
    shift_one,
    w_inner,
    b_inner,
    w_outer,
    b_outer,
    gain_two,
    shift_two,
    cotangent,
):
    local_seqs, tok_dev, model_width = inputs.shape
    groups = lax.axis_size("seq")
    head_width = model_width // groups
    local_heads = head_width // HEAD_DIM
    factor = HEAD_DIM ** (-0.5)
    gathered = (
        lax.all_gather(w_query, "shard", axis=0, tiled=True),
        lax.all_gather(b_query, "shard", axis=0, tiled=True),
        lax.all_gather(w_key, "shard", axis=0, tiled=True),
        lax.all_gather(w_value, "shard", axis=0, tiled=True),
        lax.all_gather(b_value, "shard", axis=0, tiled=True),
        lax.all_gather(w_output, "shard", axis=0, tiled=True),
        lax.all_gather(b_output, "shard", axis=0, tiled=True),
        lax.all_gather(gain_one, "shard", axis=0, tiled=True),
        lax.all_gather(shift_one, "shard", axis=0, tiled=True),
        lax.all_gather(w_inner, "shard", axis=0, tiled=True),
        lax.all_gather(b_inner, "shard", axis=0, tiled=True),
        lax.all_gather(w_outer, "shard", axis=0, tiled=True),
        lax.all_gather(b_outer, "shard", axis=0, tiled=True),
        lax.all_gather(gain_two, "shard", axis=0, tiled=True),
        lax.all_gather(shift_two, "shard", axis=0, tiled=True),
    )
    (
        query_w,
        query_b,
        key_w,
        value_w,
        value_b,
        output_w,
        output_b,
        gain_a,
        shift_a,
        inner_w,
        inner_b,
        outer_w,
        outer_b,
        gain_b,
        shift_b,
    ) = gathered
    gain_first = gain_a.astype(jnp.float32)
    shift_first = shift_a.astype(jnp.float32)
    gain_second = gain_b.astype(jnp.float32)
    shift_second = shift_b.astype(jnp.float32)
    flat_rows = inputs.reshape(local_seqs * tok_dev, model_width)
    queries = (product(flat_rows, query_w) + query_b.astype(jnp.float32)).astype(jnp.bfloat16)
    key_rows = product(flat_rows, key_w).astype(jnp.bfloat16)
    values = (product(flat_rows, value_w) + value_b.astype(jnp.float32)).astype(jnp.bfloat16)
    shape_seq = (local_seqs, tok_dev, model_width)
    head_q, head_k, head_v = (
        lax.all_to_all(queries.reshape(shape_seq), "seq", split_axis=2, concat_axis=1, tiled=True),
        lax.all_to_all(key_rows.reshape(shape_seq), "seq", split_axis=2, concat_axis=1, tiled=True),
        lax.all_to_all(values.reshape(shape_seq), "seq", split_axis=2, concat_axis=1, tiled=True),
    )
    seq_len = head_q.shape[1]
    split = (local_seqs, seq_len, local_heads, HEAD_DIM)
    head_q = head_q.reshape(split)
    head_k = head_k.reshape(split)
    head_v = head_v.reshape(split)

    def attend(packed):
        query_seq, key_seq, value_seq, length = packed
        logits = head_logits(query_seq, key_seq, length, factor)
        row_max = jnp.max(logits, axis=-1, keepdims=True)
        shifted = jnp.exp(logits - row_max)
        row_total = jnp.sum(shifted, axis=-1, keepdims=True)
        weights = (shifted / row_total).astype(jnp.bfloat16)
        context = jnp.einsum("hqk,khd->qhd", weights, value_seq, preferred_element_type=jnp.float32)
        return (context.astype(jnp.bfloat16), (row_max + jnp.log(row_total))[..., 0])

    head_context, log_total = lax.map(attend, (head_q, head_k, head_v, lengths))
    back_shape = (local_seqs, seq_len, head_width)
    context = lax.all_to_all(
        head_context.reshape(back_shape), "seq", split_axis=1, concat_axis=2, tiled=True
    ).reshape(-1, model_width)
    branch = product(context, output_w) + output_b.astype(jnp.float32)
    summed = flat_rows.astype(jnp.float32) + branch
    normed = layer_norm(summed, gain_first, shift_first)
    normed_low = normed.astype(jnp.bfloat16)
    pre_inner = product(normed_low, inner_w) + inner_b.astype(jnp.float32)
    activated = jax.nn.gelu(pre_inner, approximate=False).astype(jnp.bfloat16)
    final_sum = normed + product(activated, outer_w) + outer_b.astype(jnp.float32)
    result = layer_norm(final_sum, gain_second, shift_second)
    grad_out = cotangent.reshape(-1, model_width).astype(jnp.float32)
    second_back = jax.vjp(layer_norm, final_sum, gain_second, shift_second)[1]
    grad_final, grad_gain_two, grad_shift_two = second_back(grad_out)
    grad_ffn = grad_final.astype(jnp.bfloat16)
    grad_w_outer = row_contract(activated, grad_ffn)
    grad_b_outer = column_sum(grad_ffn)
    grad_active = times_transposed(grad_ffn, outer_w)
    gelu_back = jax.vjp(partial(jax.nn.gelu, approximate=False), pre_inner)[1]
    grad_pre = gelu_back(grad_active)[0].astype(jnp.bfloat16)
    grad_w_inner = row_contract(normed_low, grad_pre)
    grad_b_inner = column_sum(grad_pre)
    grad_normed = grad_final + times_transposed(grad_pre, inner_w)
    first_back = jax.vjp(layer_norm, summed, gain_first, shift_first)[1]
    grad_summed, grad_gain_one, grad_shift_one = first_back(grad_normed)
    grad_branch = grad_summed.astype(jnp.bfloat16)
    grad_w_output = row_contract(context, grad_branch)
    grad_b_output = column_sum(grad_branch)
    grad_context = times_transposed(grad_branch, output_w).astype(jnp.bfloat16)
    grad_head_context = lax.all_to_all(
        grad_context.reshape(shape_seq), "seq", split_axis=2, concat_axis=1, tiled=True
    ).reshape(split)

    def attend_back(packed):
        query_seq, key_seq, value_seq, log_sum, grad_seq, length = packed
        logits = head_logits(query_seq, key_seq, length, factor)
        attn_probs = jnp.exp(logits - log_sum[..., None])
        weights = attn_probs.astype(jnp.bfloat16)
        grad_value = jnp.einsum(
            "hqk,qhd->khd", weights, grad_seq, preferred_element_type=jnp.float32
        )
        grad_probs = jnp.einsum(
            "qhd,khd->hqk", grad_seq, value_seq, preferred_element_type=jnp.float32
        )
        inner_sum = jnp.sum(grad_probs * attn_probs, axis=-1, keepdims=True)
        grad_scores = (attn_probs * (grad_probs - inner_sum)).astype(jnp.bfloat16)
        grad_query = (
            jnp.einsum("hqk,khd->qhd", grad_scores, key_seq, preferred_element_type=jnp.float32)
            * factor
        )
        grad_key = (
            jnp.einsum("hqk,qhd->khd", grad_scores, query_seq, preferred_element_type=jnp.float32)
            * factor
        )
        return (
            grad_query.astype(jnp.bfloat16),
            grad_key.astype(jnp.bfloat16),
            grad_value.astype(jnp.bfloat16),
        )

    head_gq, head_gk, head_gv = lax.map(
        attend_back, (head_q, head_k, head_v, log_total, grad_head_context, lengths)
    )
    tok_gq, tok_gk, tok_gv = (
        lax.all_to_all(head_gq.reshape(back_shape), "seq", split_axis=1, concat_axis=2, tiled=True),
        lax.all_to_all(head_gk.reshape(back_shape), "seq", split_axis=1, concat_axis=2, tiled=True),
        lax.all_to_all(head_gv.reshape(back_shape), "seq", split_axis=1, concat_axis=2, tiled=True),
    )
    grad_query = tok_gq.reshape(-1, model_width)
    grad_key = tok_gk.reshape(-1, model_width)
    grad_value = tok_gv.reshape(-1, model_width)
    grad_w_query = row_contract(flat_rows, grad_query)
    grad_b_query = column_sum(grad_query)
    grad_w_key = row_contract(flat_rows, grad_key)
    grad_w_value = row_contract(flat_rows, grad_value)
    grad_b_value = column_sum(grad_value)
    grad_rows = (
        grad_summed
        + times_transposed(grad_query, query_w)
        + times_transposed(grad_key, key_w)
        + times_transposed(grad_value, value_w)
    )
    local_grads = (
        grad_w_query,
        grad_b_query,
        grad_w_key,
        grad_w_value,
        grad_b_value,
        grad_w_output,
        grad_b_output,
        grad_gain_one,
        grad_shift_one,
        grad_w_inner,
        grad_b_inner,
        grad_w_outer,
        grad_b_outer,
        grad_gain_two,
        grad_shift_two,
    )
    shares = (
        lax.psum_scatter(local_grads[0], "shard", scatter_dimension=0, tiled=True),
        lax.psum_scatter(local_grads[1], "shard", scatter_dimension=0, tiled=True),
        lax.psum_scatter(local_grads[2], "shard", scatter_dimension=0, tiled=True),
        lax.psum_scatter(local_grads[3], "shard", scatter_dimension=0, tiled=True),
        lax.psum_scatter(local_grads[4], "shard", scatter_dimension=0, tiled=True),
        lax.psum_scatter(local_grads[5], "shard", scatter_dimension=0, tiled=True),
        lax.psum_scatter(local_grads[6], "shard", scatter_dimension=0, tiled=True),
        lax.psum_scatter(local_grads[7], "shard", scatter_dimension=0, tiled=True),
        lax.psum_scatter(local_grads[8], "shard", scatter_dimension=0, tiled=True),
        lax.psum_scatter(local_grads[9], "shard", scatter_dimension=0, tiled=True),
        lax.psum_scatter(local_grads[10], "shard", scatter_dimension=0, tiled=True),
        lax.psum_scatter(local_grads[11], "shard", scatter_dimension=0, tiled=True),
        lax.psum_scatter(local_grads[12], "shard", scatter_dimension=0, tiled=True),
        lax.psum_scatter(local_grads[13], "shard", scatter_dimension=0, tiled=True),
        lax.psum_scatter(local_grads[14], "shard", scatter_dimension=0, tiled=True),
    )
    summed_grads = (
        lax.psum(shares[0].astype(jnp.bfloat16), "seq").astype(jnp.float32),
        lax.psum(shares[1].astype(jnp.bfloat16), "seq").astype(jnp.float32),
        lax.psum(shares[2].astype(jnp.bfloat16), "seq").astype(jnp.float32),
        lax.psum(shares[3].astype(jnp.bfloat16), "seq").astype(jnp.float32),
        lax.psum(shares[4].astype(jnp.bfloat16), "seq").astype(jnp.float32),
        lax.psum(shares[5].astype(jnp.bfloat16), "seq").astype(jnp.float32),
        lax.psum(shares[6].astype(jnp.bfloat16), "seq").astype(jnp.float32),
        lax.psum(shares[7].astype(jnp.bfloat16), "seq").astype(jnp.float32),
        lax.psum(shares[8].astype(jnp.bfloat16), "seq").astype(jnp.float32),
        lax.psum(shares[9].astype(jnp.bfloat16), "seq").astype(jnp.float32),
        lax.psum(shares[10].astype(jnp.bfloat16), "seq").astype(jnp.float32),
        lax.psum(shares[11].astype(jnp.bfloat16), "seq").astype(jnp.float32),
        lax.psum(shares[12].astype(jnp.bfloat16), "seq").astype(jnp.float32),
        lax.psum(shares[13].astype(jnp.bfloat16), "seq").astype(jnp.float32),
        lax.psum(shares[14].astype(jnp.bfloat16), "seq").astype(jnp.float32),
    )
    return (
        result.astype(jnp.bfloat16).reshape(shape_seq),
        grad_rows.reshape(shape_seq),
        summed_grads[0],
        summed_grads[1],
        summed_grads[2],
        summed_grads[3],
        summed_grads[4],
        summed_grads[5],
        summed_grads[6],
        summed_grads[7],
        summed_grads[8],
        summed_grads[9],
        summed_grads[10],
        summed_grads[11],
        summed_grads[12],
        summed_grads[13],
        summed_grads[14],
    )


def solution(mesh):
    tuned = (mesh.shape["shard"], mesh.shape["seq"]) == (8, 4)
    return jax.shard_map(
        per_device if tuned else per_device_plain,
        mesh=mesh,
        in_specs=(
            P("shard", "seq", None),
            P("shard"),
            P("shard", None),
            P("shard"),
            P("shard", None),
            P("shard", None),
            P("shard"),
            P("shard", None),
            P("shard"),
            P("shard"),
            P("shard"),
            P("shard", None),
            P("shard"),
            P("shard", None),
            P("shard"),
            P("shard"),
            P("shard"),
            P("shard", "seq", None),
        ),
        out_specs=(
            P("shard", "seq", None),
            P("shard", "seq", None),
            P("shard", None),
            P("shard"),
            P("shard", None),
            P("shard", None),
            P("shard"),
            P("shard", None),
            P("shard"),
            P("shard"),
            P("shard"),
            P("shard", None),
            P("shard"),
            P("shard", None),
            P("shard"),
            P("shard"),
            P("shard"),
        ),
        check_vma=False,
    )
```

```python
from functools import partial
from types import SimpleNamespace

import jax
import jax.numpy as jnp
from jax import lax
from jax.experimental import pallas as pl
from jax.experimental.pallas import tpu as pltpu
from jax.sharding import PartitionSpec as P

HEAD_DIM = 64
BF16, F32 = jnp.bfloat16, jnp.float32
MESH = pl.DeviceIdType.MESH


epsilon = 1e-12


def layer_norm(tensor, norm_gain, norm_shift):
    average = jnp.mean(tensor, axis=-1, keepdims=True)
    centred = tensor - average
    variance = jnp.mean(centred * centred, axis=-1, keepdims=True)
    return centred * lax.rsqrt(variance + epsilon) * norm_gain + norm_shift


def product(operand, weight):
    return jnp.dot(operand, weight, preferred_element_type=jnp.float32)


def row_contract(operand, weight):
    return lax.dot_general(
        operand, weight, (((0,), (0,)), ((), ())), preferred_element_type=jnp.float32
    )


def times_transposed(operand, weight):
    return lax.dot_general(
        operand, weight, (((1,), (1,)), ((), ())), preferred_element_type=jnp.float32
    )


def column_sum(tensor):
    return jnp.sum(tensor.astype(jnp.float32), axis=0)


def place():
    shard, seq = lax.axis_index("shard"), lax.axis_index("seq")
    return shard // 2, lax.rem(shard, 2), seq // 2, lax.rem(seq, 2)


def device(z, x, y, core):
    return (z * 2 + x, y * 2 + core)


def send(src, dst, send_sem, recv_sem, where):
    copy = pltpu.make_async_remote_copy(
        src_ref=src,
        dst_ref=dst,
        send_sem=send_sem,
        recv_sem=recv_sem,
        device_id=where,
        device_id_type=MESH,
    )
    copy.start()
    return copy


def await_bytes(ref, sem):
    pltpu.make_async_copy(ref, ref, sem).wait()


def along_z(z):
    return (z + 1 - 2 * lax.rem(z, 2), lax.rem(z + 2, 4), 3 - z)


def greet(z, x, y, core):
    barrier = pltpu.get_barrier_semaphore()
    others = [device(lax.rem(z + j, 4), x, y, core) for j in (1, 2, 3)]
    others += [device(z, 1 - x, y, core), device(z, x, 1 - y, core), device(z, x, y, 1 - core)]
    for other in others:
        pl.semaphore_signal(barrier, inc=1, device_id=other, device_id_type=MESH)
    pl.semaphore_wait(barrier, len(others))


def at(start, size):
    return pl.ds(pl.multiple_of(start, 16), size)


ITEMS = [(w, 0, 768) for w in range(4)] + [(4, i * 768, 768) for i in range(4)] + [(5, i * 256, 256) for i in range(3)]
ROWS = 96
SHARD_ROWS = (96, 96, 96, 96, 96, 384)
WIDTHS = (768, 768, 768, 768, 3072, 768)
LEAD = 2
X_STEP = 2
FORWARD_DELAY = (1, 3, 5, 6)
BACKWARD_DELAY = (0, 2, 3, 5, 8, 9)
THIRDS = (3,) * len(ITEMS)


def half(item, core):
    which, first, width = item
    return pl.ds(pl.multiple_of(first + core * (width // 2), 128), width // 2)


def column(start, width):
    return pl.ds(pl.multiple_of(start, 128), width)


def head_masks():
    lane = lax.broadcasted_iota(jnp.int32, (1, 128), 1)
    low = (lane < HEAD_DIM).astype(F32)
    return (low.astype(BF16), (1.0 - low).astype(BF16))


def vectors(r):
    r.vec[...] = jnp.sum(r.small[...].astype(F32), axis=0)
    for i in range(4):
        r.b_inner[:, i * 768 : i * 768 + 768] = r.vec[5 + i : 6 + i, :]


def project_one(r, name):
    own = at(r.seq * 128, 128)
    for slot in range(2):

        @pl.loop(0, 3)
        def _(c):
            cols = column(c * 256, 256)
            if name == "q":
                r.q[slot, :, cols] = (product(r.x[slot, own, :], r.w_q[:, :, cols].reshape(768, 256)) + r.vec[0:1, cols]).astype(BF16)
            elif name == "k":
                r.k[slot, :, cols] = product(r.x[slot], r.w_k[:, :, cols].reshape(768, 256)).astype(BF16)
            else:
                r.v[slot, :, cols] = (product(r.x[slot], r.w_v[:, :, cols].reshape(768, 256)) + r.vec[1:2, cols]).astype(BF16)


def attend(r, slot, first, last):
    masks = head_masks()
    visible = lax.broadcasted_iota(jnp.int32, (512, 128), 0) < r.lengths[slot]

    @pl.loop(first, last)
    def _(p):
        cols = column(p * 128, 128)
        k, q, v = r.k[slot, :, cols], r.q[slot, :, cols], r.v[slot, :, cols]
        context = None
        for h in range(2):
            scores = times_transposed(k, q * masks[h]) * (HEAD_DIM**-0.5)
            logits = jnp.where(visible, scores, -1000000000.0)
            shifted = jnp.exp(logits - jnp.max(logits, axis=0, keepdims=True))
            probs = shifted * (1.0 / jnp.sum(shifted, axis=0, keepdims=True))
            low = probs.astype(BF16)
            r.p[slot, p * 2 + h] = low
            part = row_contract(low, v * masks[h])
            context = part if context is None else context + part
        r.c[slot, :, cols] = context.astype(BF16)


def norm_stats(rows):
    average = jnp.mean(rows, axis=-1, keepdims=True)
    centred = rows - average
    variance = jnp.mean(centred * centred, axis=-1, keepdims=True)
    scale = lax.rsqrt(variance + epsilon)
    return centred * scale, scale


def norm_back(grad, gain, unit, scale):
    g = grad * gain
    return scale * (
        g - jnp.mean(g, axis=-1, keepdims=True) - unit * jnp.mean(g * unit, axis=-1, keepdims=True)
    )


def first_norm(r):
    for slot in range(2):
        rows = pl.ds(slot * 128, 128)
        h1 = r.x[slot, at(r.seq * 128, 128), :].astype(F32) + product(r.c[slot], r.w_o[...].reshape(768, 768)) + r.vec[2:3, :]
        unit, scale = norm_stats(h1)
        r.unit_one[rows, :] = unit
        r.scale_one[rows, :] = jnp.broadcast_to(scale, (128, 128))
        n1 = unit * r.vec[3:4, :] + r.vec[4:5, :]
        r.n1[rows, :] = n1
        r.n1b[rows, :] = n1.astype(BF16)


def feed_in(r, i):
    @pl.loop(0, 3)
    def _(c):
        cols = column(i * 768 + c * 256, 256)
        u = product(r.n1b[...], r.w_inner[:, :, cols].reshape(768, 256)) + r.b_inner[:, cols]
        phi = 0.5 * (1.0 + lax.erf(u * 0.7071067811865476))
        r.g[:, cols] = (u * phi).astype(BF16)
        r.slope[:, cols] = (phi + u * (0.3989422804014327 * jnp.exp(-0.5 * u * u))).astype(BF16)


def feed_out(r, i):
    cols = pl.ds(i * 256, 256)
    r.dh2[:, cols] = r.n1[:, cols] + product(r.g[...], r.w_outer[:, :, cols].reshape(3072, 256)) + r.vec[9:10, cols]


def second_norm(r):
    for slot in range(2):
        rows = pl.ds(slot * 128, 128)
        unit, scale = norm_stats(r.dh2[rows, :])
        r.result[slot] = (unit * r.vec[10:11, :] + r.vec[11:12, :]).astype(BF16)
        grad = r.cot[slot].astype(F32)
        back = norm_back(grad, r.vec[10:11, :], unit, scale)
        low = back.astype(BF16)
        r.dh2[rows, :] = back
        r.df[rows, :] = low
        tally(r, slot, 10, grad * unit)
        tally(r, slot, 11, grad)
        tally(r, slot, 9, low.astype(F32))


def tally(r, slot, row, values):
    total = jnp.sum(values, axis=0, keepdims=True)
    r.sums[row : row + 1, :] = total if slot == 0 else r.sums[row : row + 1, :] + total


KINDS = {
    "place": ((16, 768), F32),
    "small_own": ((16, 768), BF16),
    "small": ((8, 16, 768), BF16),
    "b_inner": ((1, 3072), F32),
    "x": ((2, 512, 768), BF16),
    "q": ((2, 128, 768), BF16),
    "k": ((2, 512, 768), BF16),
    "v": ((2, 512, 768), BF16),
    "p": ((2, 12, 512, 128), BF16),
    "c": ((2, 128, 768), BF16),
    "unit_one": ((256, 768), F32),
    "scale_one": ((256, 128), F32),
    "n1": ((256, 768), F32),
    "n1b": ((256, 768), BF16),
    "g": ((256, 3072), BF16),
    "slope": ((256, 3072), BF16),
    "dh2": ((256, 768), F32),
    "df": ((256, 768), BF16),
    "da": ((2, 128, 768), BF16),
    "dc": ((2, 128, 768), BF16),
    "dq": ((2, 128, 768), BF16),
    "dk": ((2, 512, 768), BF16),
    "dv": ((2, 512, 768), BF16),
    "dx_own": ((2, 128, 768), F32),
    "dx_part": ((2, 512, 768), BF16),
    "sums": ((16, 768), F32),
    "ring": ((4, 768, 768), BF16),
}


def kinds(*names):
    return {name: KINDS[name] for name in names}


VECTOR_ROWS = (0, 1, 2, 3, 4, None, 9, 10, 11)
HANDED = ("x", "q", "k", "v", "p", "c", "unit_one", "scale_one", "n1b", "g", "slope", "dh2", "df")

FORWARD_WORK = kinds(
    "place", "small_own", "small", "b_inner", "x", "q", "k", "v", "p", "c", "unit_one", "scale_one", "n1", "n1b", "g",
    "slope", "dh2", "df",
)

def place_vectors(r, shard):
    r.place[...] = jnp.zeros_like(r.place)
    for row, ref in zip(VECTOR_ROWS, r.vectors):
        if row is not None:
            r.place[row : row + 1, 0:ROWS] = ref[...].astype(F32)
    r.place[...] = pltpu.roll(r.place[...], shard * ROWS, 1)
    r.place[pl.ds(5 + shard // 2, 1), column(lax.rem(shard, 2) * 384, 384)] = r.vectors[5][...].astype(F32).reshape(1, 384)
    r.small_own[...] = r.place[...].astype(BF16)


def forward_kernel(*refs):
    own = refs[0:6]
    r = SimpleNamespace(vectors=refs[6:15])
    x_own, r.cot, r.lengths = refs[15:18]
    kept = refs[18:24]
    r.result, r.sums, r.vec = refs[24:27]
    handed = dict(zip(HANDED, refs[27:40]))
    full = refs[40:46]
    rest = list(refs[46:])
    for name in FORWARD_WORK:
        setattr(r, name, rest.pop(0))
    r.w_q, r.w_k, r.w_v, r.w_o, r.w_inner, r.w_outer = full
    small_own, small_full, x_full = r.small_own, r.small, r.x
    send_sem, z_sem, x_sem, y_sem, c_sem, local_sem, own_sem, extra_send, extra_recv, keep_sem = rest
    z, x, y, core = place()
    shard = z * 2 + x
    seq = y * 2 + core
    r.seq = seq
    place_vectors(r, shard)
    r.sums[...] = jnp.zeros_like(r.sums)
    greet(z, x, y, core)
    to_x = device(z, 1 - x, y, core)
    to_y = device(z, x, 1 - y, core)
    to_c = device(z, x, y, 1 - core)
    others = along_z(z)

    def shard_at(back, side):
        return lax.rem(z + 4 - back, 4) * 2 + side

    def kept_rows(n):
        rows = SHARD_ROWS[ITEMS[n][0]]
        return rows, rows // 3

    def block(n, owner, begin, size):
        return full[ITEMS[n][0]].at[owner, at(begin, size), half(ITEMS[n], core)]

    def carried(n, owner):
        rows, third = kept_rows(n)
        return block(n, owner, y * third, rows - third)

    def for_y(n, owner):
        rows, third = kept_rows(n)
        return block(n, owner, y * (rows - third), third)

    mine = x_full.at[:, at(seq * 128, 128), :]
    x_local = pltpu.make_async_copy(x_own, mine, local_sem.at[0])
    x_local.start()
    s_local = pltpu.make_async_copy(small_own, small_full.at[shard], local_sem.at[1])
    s_local.start()

    def start(n):
        rows, third = kept_rows(n)
        src = own[ITEMS[n][0]].at[at(y * third, rows - third), half(ITEMS[n], core)]
        for m in (1, 0):
            send(src, carried(n, shard), send_sem.at[n], z_sem.at[n, m], device(others[m], x, y, core))
        send(src, carried(n, shard), send_sem.at[n], x_sem.at[n, 0], to_x)

    start(0)
    send(x_own, mine, extra_send.at[0], extra_recv.at[0], to_y)
    send(x_own, mine, extra_send.at[0], extra_recv.at[1], to_c)
    for j in (1, 2, 3):
        there = device(lax.rem(z + j, 4), x, y, core)
        send(small_own, small_full.at[shard], extra_send.at[1], extra_recv.at[1 + j], there)
    send(small_own, small_full.at[shard], extra_send.at[1], extra_recv.at[5], to_x)
    for n in range(1, LEAD):
        start(n)
    locals_ = []
    for n, item in enumerate(ITEMS):
        rows = SHARD_ROWS[item[0]]
        copy = pltpu.make_async_copy(own[item[0]].at[:, half(item, core)], block(n, shard, 0, rows), own_sem.at[n])
        copy.start()
        locals_.append(copy)

    def pass_on(n, m):
        owner = others[m] * 2 + x
        got = carried(n, owner)
        await_bytes(got, z_sem.at[n, m])
        if m == 1:
            send(got, got, send_sem.at[n], z_sem.at[n, 2], device(others[0], x, y, core))
        send(got, got, send_sem.at[n], x_sem.at[n, 1 + m], to_x)
        send(for_y(n, owner), for_y(n, owner), send_sem.at[n], y_sem.at[n], to_y)

    def from_z(n):
        pass_on(n, 0)
        pass_on(n, 1)

    def from_far_z(n):
        pass_on(n, 2)

    def from_x(n):
        for j in range(4):
            owner = (z if j == 0 else others[j - 1]) * 2 + 1 - x
            await_bytes(carried(n, owner), x_sem.at[n, j])
            send(for_y(n, owner), for_y(n, owner), send_sem.at[n], y_sem.at[n], to_y)

    def some(n, owners, rows):
        return full[ITEMS[n][0]].at[pl.ds(0, owners), pl.ds(0, rows), half(ITEMS[n], core)]

    def from_y(n):
        rows, third = kept_rows(n)
        await_bytes(some(n, 7, third), y_sem.at[n])
        locals_[n].wait()
        whole = some(n, 8, rows)
        send(whole, whole, send_sem.at[n], c_sem.at[n], to_c)

    def from_c(n):
        await_bytes(some(n, 8, SHARD_ROWS[ITEMS[n][0]]), c_sem.at[n])

    def sent(n):
        rows, third = kept_rows(n)
        await_bytes(some(n, 7, rows - third), send_sem.at[n])
        await_bytes(some(n, 7, third), send_sem.at[n])
        await_bytes(some(n, 8, rows), send_sem.at[n])

    def small_relay():
        for j in (1, 2, 3):
            there = small_full.at[shard_at(j, x)]
            await_bytes(there, extra_recv.at[1 + j])
            send(there, there, extra_send.at[1], extra_recv.at[5 + j], to_x)

    def x_relay():
        theirs = x_full.at[:, at(((1 - y) * 2 + core) * 128, 128), :]
        await_bytes(theirs, extra_recv.at[0])
        send(theirs, theirs, extra_send.at[0], extra_recv.at[1], to_c)

    keeps = []

    def keep(src, dst):
        copy = pltpu.make_async_copy(src, dst, keep_sem.at[len(keeps)])
        copy.start()
        keeps.append(copy)

    def hand(*names):
        for name in names:
            keep(getattr(r, name), handed[name])

    def arrive():
        for j in range(4):
            await_bytes(small_full.at[shard_at(j, 1 - x)], extra_recv.at[5 + j])
        await_bytes(x_full.at[:, pl.ds(0, 256), :], extra_recv.at[1])
        x_local.wait()
        s_local.wait()
        vectors(r)
        hand("x")

    def after(n):
        if n == 0:
            arrive()
            project_one(r, "q")
            hand("q")
        elif n == 1:
            project_one(r, "k")
            hand("k")
        elif n == 2:
            project_one(r, "v")
            hand("v")
        if 2 <= n <= 5:
            attend(r, (n - 2) // 2, (n % 2) * 3, (n % 2) * 3 + 3)
        if n == 5:
            hand("p", "c")
            first_norm(r)
            hand("unit_one", "scale_one", "n1b")
            feed_in(r, 0)
        if n == 6:
            feed_in(r, 1)
            feed_in(r, 2)
        if n == 7:
            feed_in(r, 3)
            hand("g", "slope")
        if n >= 8:
            feed_out(r, n - 8)
        if n in (0, 1, 2, 3, 7, 10):
            which = ITEMS[n][0]
            keep(full[which], kept[which])

    delay = FORWARD_DELAY
    stages = ((0, from_z),) + tuple(zip(delay, (from_far_z, from_x, from_y, from_c)))
    for step in range(len(ITEMS) + delay[-1]):
        if step + LEAD < len(ITEMS):
            start(step + LEAD)
        if step == 1:
            small_relay()
        if step == X_STEP:
            x_relay()
        for depth, stage in stages:
            n = step - depth
            if 0 <= n < len(ITEMS):
                stage(n)
        n = step - delay[-1]
        if 0 <= n < len(ITEMS):
            after(n)

    second_norm(r)
    hand("dh2", "df")
    await_bytes(x_full.at[:, pl.ds(0, 384), :], extra_send.at[0])
    await_bytes(small_full.at[pl.ds(0, 7)], extra_send.at[1])
    for n in range(len(ITEMS)):
        sent(n)
    for copy in keeps:
        copy.wait()


def forward(weights, vectors_in, inputs, cotangent, lengths):
    count = len(ITEMS)
    wholes = [(8,) + w.shape for w in weights]
    outs = [jax.ShapeDtypeStruct(shape, BF16) for shape in wholes]
    outs += [
        jax.ShapeDtypeStruct(cotangent.shape, BF16),
        jax.ShapeDtypeStruct((16, 768), F32),
        jax.ShapeDtypeStruct((16, 768), F32),
    ]
    outs += [jax.ShapeDtypeStruct(*FORWARD_WORK[name]) for name in HANDED]
    vmem, anywhere = pl.BlockSpec(memory_space=pltpu.VMEM), pl.BlockSpec(memory_space=pl.ANY)
    return pl.pallas_call(
        forward_kernel,
        out_shape=outs,
        in_specs=[vmem] * 17 + [pl.BlockSpec(memory_space=pltpu.SMEM)],
        out_specs=[anywhere] * 6 + [vmem] * 3 + [anywhere] * len(HANDED),
        scratch_shapes=[pltpu.VMEM(shape, BF16) for shape in wholes]
        + [pltpu.VMEM(*kind) for kind in FORWARD_WORK.values()]
        + [
            pltpu.SemaphoreType.DMA((count,)),
            pltpu.SemaphoreType.DMA((count, 3)),
            pltpu.SemaphoreType.DMA((count, 4)),
            pltpu.SemaphoreType.DMA((count,)),
            pltpu.SemaphoreType.DMA((count,)),
            pltpu.SemaphoreType.DMA((2,)),
            pltpu.SemaphoreType.DMA((count,)),
            pltpu.SemaphoreType.DMA((2,)),
            pltpu.SemaphoreType.DMA((9,)),
            pltpu.SemaphoreType.DMA((6 + len(HANDED),)),
        ],
        compiler_params=pltpu.CompilerParams(
            collective_id=0, has_side_effects=True, vmem_limit_bytes=60 * 2**20
        ),
        name="forward",
    )(*weights, *vectors_in, inputs, cotangent, lengths)


ORDER = (8, 9, 10, 4, 5, 6, 7, 3, 0, 1, 2)
RING = 4
TAKE_ORDER = ("g", "df", "slope", "n1b", "dh2", "unit_one", "scale_one", "c", "k", "q", "v", "p", "x")
GRAD_SHAPES = [(4, 2, rows, width) for rows, width in zip(SHARD_ROWS, WIDTHS)]

BACKWARD_WORK = kinds(
    "x", "q", "k", "v", "p", "c", "unit_one", "scale_one", "n1b", "g", "slope", "dh2", "df", "da", "dc", "dq", "dk", "dv",
    "dx_own", "dx_part", "sums", "ring",
)

def ring_load(r, j):
    if j < 4:
        src = r.w_outer.at[pl.ds(j * 768, 768), :]
    elif j < 8:
        src = r.w_inner.at[:, pl.ds((j - 4) * 768, 768)]
    else:
        src = (r.w_o, r.w_q, r.w_k, r.w_v)[j - 8]
    copy = pltpu.make_async_copy(src, r.ring.at[j % RING], r.ring_sem.at[j])
    copy.start()
    return copy


def outer_grad(r, i):
    cols = pl.ds(i * 256, 256)
    for c in range(8):
        left = r.g[:, c * 384 : c * 384 + 384]
        r.grads[5][c // 2, c % 2, :, cols] = row_contract(left, r.df[:, cols]).astype(BF16)


def inner_part(r, i, weight):
    @pl.loop(0, 3)
    def _(c):
        cols = column(i * 768 + c * 256, 256)
        low = (times_transposed(r.df[...], weight[at(c * 256, 256), :]) * r.slope[:, cols].astype(F32)).astype(BF16)
        r.slope[:, cols] = low
        r.sums[5 + i : 6 + i, column(c * 256, 256)] = jnp.sum(low.astype(F32), axis=0, keepdims=True)
        r.grads[4][:, :, :, cols] = row_contract(r.n1b[...], low).astype(BF16).reshape(4, 2, ROWS, 256)


def normed_part(r, i, weight):
    r.dh2[...] = r.dh2[...] + times_transposed(r.slope[:, i * 768 : i * 768 + 768], weight[...])


def first_norm_back(r):
    for slot in range(2):
        rows = pl.ds(slot * 128, 128)
        dn1 = r.dh2[rows, :]
        unit = r.unit_one[rows, :]
        back = norm_back(dn1, r.vec[3:4, :], unit, r.scale_one[rows, 0:1])
        low = back.astype(BF16)
        r.da[slot] = low
        tally(r, slot, 3, dn1 * unit)
        tally(r, slot, 4, dn1)
        tally(r, slot, 2, low.astype(F32))
        r.dx_own[slot] = back


def output_back(r, weight):
    for slot in range(2):
        r.dc[slot] = times_transposed(r.da[slot], weight[...]).astype(BF16)


def attend_back(r, slot, first, last):
    masks = head_masks()
    factor = HEAD_DIM**-0.5

    @pl.loop(first, last)
    def _(p):
        cols = column(p * 128, 128)
        k, q, v, dc = r.k[slot, :, cols], r.q[slot, :, cols], r.v[slot, :, cols], r.dc[slot, :, cols]
        dq = dk = dv = None
        for h in range(2):
            low = r.p[slot, p * 2 + h]
            probs = low.astype(F32)
            dch = dc * masks[h]
            dp = times_transposed(v, dch)
            inner = jnp.sum(dp * probs, axis=0, keepdims=True)
            ds = (probs * (dp - inner)).astype(BF16)
            parts = (row_contract(ds, k * masks[h]), product(ds, q * masks[h]), product(low, dch))
            dq, dk, dv = parts if dq is None else (dq + parts[0], dk + parts[1], dv + parts[2])
        dq = (dq * factor).astype(BF16)
        dv = dv.astype(BF16)
        r.dq[slot, :, cols] = dq
        r.dk[slot, :, cols] = (dk * factor).astype(BF16)
        r.dv[slot, :, cols] = dv
        dq_sum = jnp.sum(dq.astype(F32), axis=0, keepdims=True)
        dv_sum = jnp.sum(dv.astype(F32), axis=0, keepdims=True)
        if slot == 0:
            r.sums[0:1, cols] = dq_sum
            r.sums[1:2, cols] = dv_sum
        else:
            r.sums[0:1, cols] = r.sums[0:1, cols] + dq_sum
            r.sums[1:2, cols] = r.sums[1:2, cols] + dv_sum


def square_grad(r, which):
    own = at(r.seq * 128, 128)

    @pl.loop(0, 2)
    def _(c):
        cols = column(c * 384, 384)
        value = None
        for s in range(2):
            left, right = (
                (r.x[s, own, cols], r.dq[s]),
                (r.x[s, :, cols], r.dk[s]),
                (r.x[s, :, cols], r.dv[s]),
                (r.c[s, :, cols], r.da[s]),
            )[which]
            piece = row_contract(left, right)
            value = piece if value is None else value + piece
        r.grads[which][pl.ds(c * 2, 2)] = value.astype(BF16).reshape(2, 2, ROWS, 768)


def input_grads(r, w_q, w_k, w_v):
    for slot in range(2):
        r.dx_own[slot] = r.dx_own[slot] + times_transposed(r.dq[slot], w_q[...])

        @pl.loop(0, 3)
        def _(c):
            rows = at(c * 256, 256)
            r.dx_part[slot, :, column(c * 256, 256)] = (
                times_transposed(r.dk[slot], w_k[rows, :]) + times_transposed(r.dv[slot], w_v[rows, :])
            ).astype(BF16)


def backward_kernel(*refs):
    r = SimpleNamespace()
    r.w_q, r.w_k, r.w_v, r.w_o, r.w_inner, r.w_outer = refs[0:6]
    taken = dict(zip(HANDED, refs[6:19]))
    r.vec, sums_in = refs[19:21]
    out = refs[21:27]
    small_out, dx_out = refs[27:29]
    r.grads = refs[29:35]
    rest = list(refs[35:])
    for name in BACKWARD_WORK:
        setattr(r, name, rest.pop(0))
    count = len(ITEMS)
    from_core, from_y, from_x, from_z, total, back_y = [rest[i * count : i * count + count] for i in range(6)]
    rest = rest[6 * count :]
    (small_c, small_y, small_x, small_z, small_1, small_2, small_3, dx_c, dx_sum, dx_y) = rest[0:10]
    send_sem, c_sem, y_sem, x_sem, z_sem, fy_sem, fc_sem, s_send, s_recv, d_send, d_recv = rest[10:21]
    r.take_sem, r.ring_sem = rest[21:23]
    f32 = F32
    small = r.sums
    z, x, y, core = place()
    seq = y * 2 + core
    r.seq = seq
    takes = {}
    for i, name in enumerate(TAKE_ORDER):
        if name == "slope":
            loads = [ring_load(r, j) for j in range(RING)]
        takes[name] = pltpu.make_async_copy(taken[name], getattr(r, name), r.take_sem.at[i])
        takes[name].start()
    r.sums[...] = sums_in[...]
    greet(z, x, y, core)
    to_x = device(z, 1 - x, y, core)
    to_y = device(z, x, 1 - y, core)
    to_c = device(z, x, y, 1 - core)

    def parts(n):
        rows = SHARD_ROWS[ITEMS[ORDER[n]][0]]
        return rows, rows // THIRDS[n]

    def grad(n, side=core):
        item = ITEMS[ORDER[n]]
        return r.grads[item[0]].at[:, :, :, half(item, side)]

    def to_partner(n):
        send(grad(n, 1 - core), from_core[n], send_sem.at[n], c_sem.at[n], to_c)

    def add(ref, *others):
        value = ref[...].astype(f32)
        for other in others:
            value = value + other[...].astype(f32)
        ref[...] = value.astype(BF16)

    def stage_core(n):
        rows, part = parts(n)
        await_bytes(from_core[n], c_sem.at[n])
        far = at((1 - y) * (rows - part), part)
        add(grad(n).at[:, :, far, :], from_core[n].at[:, :, far, :])
        send(grad(n).at[:, :, far, :], from_y[n], send_sem.at[n], y_sem.at[n], to_y)
        middle = pl.ds(part, rows - 2 * part)
        add(grad(n).at[:, :, middle, :], from_core[n].at[:, :, middle, :])

    def stage_y(n):
        rows, part = parts(n)
        await_bytes(from_y[n], y_sem.at[n])
        near = at(y * (rows - part), part)
        add(grad(n).at[:, :, near, :], from_core[n].at[:, :, near, :], from_y[n])
        carried = at(y * part, rows - part)
        send(grad(n).at[:, 1 - x, carried, :], from_x[n], send_sem.at[n], x_sem.at[n], to_x)

    def stage_x(n):
        rows, part = parts(n)
        await_bytes(from_x[n], x_sem.at[n])
        carried = at(y * part, rows - part)
        add(grad(n).at[:, x, carried, :], from_x[n])
        for j in (2, 1, 3):
            there = lax.rem(z + j, 4)
            send(
                grad(n).at[there, x, carried, :],
                from_z[n].at[j - 1],
                send_sem.at[n],
                z_sem.at[n, j - 1],
                device(there, x, y, core),
            )

    def stage_z(n):
        rows, part = parts(n)
        for j in range(3):
            await_bytes(from_z[n].at[j], z_sem.at[n, j])
        value = grad(n).at[z, x, at(y * part, rows - part), :][...].astype(f32)
        for j in range(3):
            value = value + from_z[n][j].astype(f32)
        total[n][...] = value.astype(BF16)
        send(total[n], back_y[n], send_sem.at[n], fy_sem.at[n], to_y)

    def shares(n):
        item = ITEMS[ORDER[n]]
        return out[item[0]].at[:, half(item, core)]

    def stage_back(n):
        rows, part = parts(n)
        await_bytes(back_y[n], fy_sem.at[n])
        middle = rows - 2 * part
        place_ = shares(n)
        place_[at(y * (rows - part), part), :] = total[n][at(y * middle, part), :]
        place_[at((1 - y) * (rows - part), part), :] = back_y[n][at((1 - y) * middle, part), :]
        place_[pl.ds(part, middle), :] = (
            total[n][at((1 - y) * part, middle), :].astype(f32) + back_y[n][at(y * part, middle), :].astype(f32)
        ).astype(BF16)
        send(place_, place_, send_sem.at[n], fc_sem.at[n], to_c)

    def stage_end(n):
        await_bytes(shares(n), fc_sem.at[n])

    def sent(n):
        for ref in (from_core[n], from_y[n], from_x[n], from_z[n], total[n], shares(n)):
            await_bytes(ref, send_sem.at[n])

    def dx_rows(who):
        return r.dx_part.at[:, at(who * 128, 128), :]

    def dx_0():
        send(dx_rows((1 - y) * 2 + 1 - core), dx_c.at[1], d_send, d_recv.at[0], to_c)
        send(dx_rows(y * 2 + 1 - core), dx_c.at[0], d_send, d_recv.at[0], to_c)

    def dx_1():
        await_bytes(dx_c, d_recv.at[0])
        dx_sum[...] = (dx_rows((1 - y) * 2 + core)[...].astype(f32) + dx_c[1].astype(f32)).astype(BF16)
        send(dx_sum, dx_y, d_send, d_recv.at[1], to_y)

    def dx_end():
        await_bytes(dx_y, d_recv.at[1])
        dx_out[...] = (
            r.dx_own[...] + dx_rows(seq)[...].astype(f32) + dx_c[0].astype(f32) + dx_y[...].astype(f32)
        )

    def small_0():
        send(small, small_c, s_send.at[0], s_recv.at[0], to_c)

    def small_1st():
        await_bytes(small_c, s_recv.at[0])
        small_1[...] = small[...] + small_c[...]
        send(small_1, small_y, s_send.at[1], s_recv.at[1], to_y)

    def small_2nd():
        await_bytes(small_y, s_recv.at[1])
        small_2[...] = small_1[...] + small_y[...]
        send(small_2, small_x, s_send.at[2], s_recv.at[2], to_x)

    def small_3rd():
        await_bytes(small_x, s_recv.at[2])
        small_3[...] = small_2[...] + small_x[...]
        for j in (1, 2, 3):
            send(small_3, small_z.at[z], s_send.at[3], s_recv.at[2 + j], device(lax.rem(z + j, 4), x, y, core))

    def small_4th():
        for j in (1, 2, 3):
            await_bytes(small_z.at[lax.rem(z + 4 - j, 4)], s_recv.at[2 + j])
        await_bytes(small_z.at[pl.ds(0, 3)], s_send.at[3])
        small_z[z] = small_3[...]
        small_out[...] = ((small_z[0] + small_z[1]) + small_z[2]) + small_z[3]

    def block(j):
        loads[j].wait()
        return r.ring.at[j % RING]

    def refill(j):
        loads.append(ring_load(r, j))

    def task(k):
        if k == 0:
            takes["g"].wait()
            takes["df"].wait()
            for i in range(2):
                outer_grad(r, i)
                to_partner(i)
        if k == 1:
            outer_grad(r, 2)
            to_partner(2)
            takes["slope"].wait()
            takes["n1b"].wait()
        for i in ((), (0,), (1,), (2, 3))[k] if k < 4 else ():
            inner_part(r, i, block(i))
            refill(i + RING)
            to_partner(3 + i)
        if k == 4:
            takes["dh2"].wait()
            for i in range(4):
                normed_part(r, i, block(4 + i))
                refill(8 + i)
            for name in ("unit_one", "scale_one", "c"):
                takes[name].wait()
            first_norm_back(r)
            square_grad(r, 3)
            to_partner(7)
        if k == 5:
            output_back(r, block(8))
            for name in ("k", "q", "v", "p"):
                takes[name].wait()
        for i in {5: (0,), 6: (1,), 7: (2, 3)}.get(k, ()):
            attend_back(r, i // 2, (i % 2) * 3, (i % 2) * 3 + 3)
        if k == 8:
            takes["x"].wait()
            small_0()
            for i in range(3):
                square_grad(r, i)
                to_partner(8 + i)
        if k == 9:
            input_grads(r, block(9), block(10), block(11))
            dx_0()

    extra = {9: small_1st, 10: small_2nd, 11: small_3rd, 13: small_4th}
    depths = BACKWARD_DELAY
    stages = tuple(zip(depths, (stage_core, stage_y, stage_x, stage_z, stage_back, stage_end)))
    for step in range(count + depths[-1]):
        task(step)
        for depth, stage in stages:
            n = step - depth
            if 0 <= n < count:
                stage(n)
        if step in extra:
            extra[step]()
        if step == 10:
            dx_1()
        if step == count + depths[-1] - 2:
            dx_end()

    for n in range(count):
        sent(n)
    for j in range(3):
        await_bytes(small, s_send.at[j])
    await_bytes(dx_c, d_send)
    await_bytes(dx_sum, d_send)


def reduce_shapes():
    stages = [[] for _ in range(6)]
    for n, number in enumerate(ORDER):
        which, _, width = ITEMS[number]
        rows = SHARD_ROWS[which]
        part, width = rows // THIRDS[n], width // 2
        left = rows - part
        shapes = ((4, 2, rows, width), (4, 2, part, width), (4, left, width), (3, left, width), (left, width), (left, width))
        for stage, shape in zip(stages, shapes):
            stage.append(shape)
    return stages


def backward(weights, handed, vec, sums, dx_like):
    count = len(ITEMS)
    outs = [jax.ShapeDtypeStruct(s[2:], BF16) for s in GRAD_SHAPES]
    outs += [jax.ShapeDtypeStruct((16, 768), F32), jax.ShapeDtypeStruct(dx_like.shape, F32)]
    vmem, anywhere = pl.BlockSpec(memory_space=pltpu.VMEM), pl.BlockSpec(memory_space=pl.ANY)
    shape = (16, 768)
    return pl.pallas_call(
        backward_kernel,
        out_shape=outs,
        in_specs=[anywhere] * (6 + len(HANDED)) + [vmem] * 2,
        out_specs=[vmem] * 8,
        scratch_shapes=[pltpu.VMEM(s, BF16) for s in GRAD_SHAPES]
        + [pltpu.VMEM(*kind) for kind in BACKWARD_WORK.values()]
        + [pltpu.VMEM(shape_, BF16) for stage in reduce_shapes() for shape_ in stage]
        + [pltpu.VMEM(shape, F32)] * 3
        + [pltpu.VMEM((4,) + shape, F32)]
        + [pltpu.VMEM(shape, F32)] * 3
        + [
            pltpu.VMEM((2,) + dx_like.shape, BF16),
            pltpu.VMEM(dx_like.shape, BF16),
            pltpu.VMEM(dx_like.shape, BF16),
            pltpu.SemaphoreType.DMA((count,)),
            pltpu.SemaphoreType.DMA((count,)),
            pltpu.SemaphoreType.DMA((count,)),
            pltpu.SemaphoreType.DMA((count,)),
            pltpu.SemaphoreType.DMA((count, 3)),
            pltpu.SemaphoreType.DMA((count,)),
            pltpu.SemaphoreType.DMA((count,)),
            pltpu.SemaphoreType.DMA((4,)),
            pltpu.SemaphoreType.DMA((6,)),
            pltpu.SemaphoreType.DMA,
            pltpu.SemaphoreType.DMA((2,)),
            pltpu.SemaphoreType.DMA((len(HANDED),)),
            pltpu.SemaphoreType.DMA((12,)),
        ],
        compiler_params=pltpu.CompilerParams(
            collective_id=1, has_side_effects=True, vmem_limit_bytes=67043328
        ),
        name="backward",
    )(*weights, *handed, vec, sums)


def finish_kernel(*refs):
    shares, totals, dx, result = refs[0:6], refs[6], refs[7], refs[8]
    outs = refs[9:15]
    vectors_out = refs[15:24]
    dx_out, result_out, turned = refs[24:27]
    shard = lax.axis_index("shard")
    for share, out in zip(shares, outs):
        out[...] = share[...].astype(F32)
    dx_out[...] = dx[...]
    result_out[...] = result[...]
    turned[...] = pltpu.roll(totals[...], lax.rem(8 - shard, 8) * ROWS, 1)
    for row, out in zip(VECTOR_ROWS, vectors_out):
        if row is not None:
            out[...] = turned[row : row + 1, 0:ROWS]
    vectors_out[5][...] = totals[pl.ds(5 + shard // 2, 1), column(lax.rem(shard, 2) * 384, 384)].reshape(384)


def finish(shares, totals, dx, result):
    outs = [jax.ShapeDtypeStruct(s.shape, F32) for s in shares]
    outs += [jax.ShapeDtypeStruct((384,) if row is None else (1, ROWS), F32) for row in VECTOR_ROWS]
    outs += [jax.ShapeDtypeStruct(dx.shape, F32), jax.ShapeDtypeStruct(result.shape, BF16)]
    vmem = pl.BlockSpec(memory_space=pltpu.VMEM)
    return pl.pallas_call(
        finish_kernel,
        out_shape=outs,
        in_specs=[vmem] * 9,
        out_specs=[vmem] * len(outs),
        scratch_shapes=[pltpu.VMEM((16, 768), F32)],
        compiler_params=pltpu.CompilerParams(vmem_limit_bytes=67043328),
        name="finish",
    )(*shares, totals, dx, result)


def per_device(
    inputs,
    lengths,
    w_query,
    b_query,
    w_key,
    w_value,
    b_value,
    w_output,
    b_output,
    gain_one,
    shift_one,
    w_inner,
    b_inner,
    w_outer,
    b_outer,
    gain_two,
    shift_two,
    cotangent,
):
    vectors_in = (b_query, b_value, b_output, gain_one, shift_one, b_inner, b_outer, gain_two, shift_two)
    weights = (w_query, w_key, w_value, w_output, w_inner, w_outer)
    first = forward(weights, [v if v is b_inner else v.reshape(1, -1) for v in vectors_in], inputs, cotangent, lengths)
    wholes = [w.reshape(-1, w.shape[2]) for w in first[0:6]]
    (result, sums, vec), handed = first[6:9], first[9:]
    *shares, totals, dx = backward(wholes, handed, vec, sums, inputs)
    done = finish(shares, totals, dx, result)
    g_q, g_k, g_v, g_o, g_inner, g_outer = done[0:6]
    g_bq, g_bv, g_bo, g_g1, g_s1, g_bi, g_bouter, g_g2, g_s2 = [v.reshape(-1) for v in done[6:15]]
    return (
        done[16],
        done[15],
        g_q,
        g_bq,
        g_k,
        g_v,
        g_bv,
        g_o,
        g_bo,
        g_g1,
        g_s1,
        g_inner,
        g_bi,
        g_outer,
        g_bouter,
        g_g2,
        g_s2,
    )


def head_logits(query_seq, key_seq, length, factor):
    scores = (
        jnp.einsum("qhd,khd->hqk", query_seq, key_seq, preferred_element_type=jnp.float32) * factor
    )
    visible = jnp.arange(key_seq.shape[0]) < length
    return jnp.where(visible[None, None, :], scores, -1000000000.0)


def per_device_plain(
    inputs,
    lengths,
    w_query,
    b_query,
    w_key,
    w_value,
    b_value,
    w_output,
    b_output,
    gain_one,
    shift_one,
    w_inner,
    b_inner,
    w_outer,
    b_outer,
    gain_two,
    shift_two,
    cotangent,
):
    local_seqs, tok_dev, model_width = inputs.shape
    groups = lax.axis_size("seq")
    head_width = model_width // groups
    local_heads = head_width // HEAD_DIM
    factor = HEAD_DIM ** (-0.5)
    gathered = (
        lax.all_gather(w_query, "shard", axis=0, tiled=True),
        lax.all_gather(b_query, "shard", axis=0, tiled=True),
        lax.all_gather(w_key, "shard", axis=0, tiled=True),
        lax.all_gather(w_value, "shard", axis=0, tiled=True),
        lax.all_gather(b_value, "shard", axis=0, tiled=True),
        lax.all_gather(w_output, "shard", axis=0, tiled=True),
        lax.all_gather(b_output, "shard", axis=0, tiled=True),
        lax.all_gather(gain_one, "shard", axis=0, tiled=True),
        lax.all_gather(shift_one, "shard", axis=0, tiled=True),
        lax.all_gather(w_inner, "shard", axis=0, tiled=True),
        lax.all_gather(b_inner, "shard", axis=0, tiled=True),
        lax.all_gather(w_outer, "shard", axis=0, tiled=True),
        lax.all_gather(b_outer, "shard", axis=0, tiled=True),
        lax.all_gather(gain_two, "shard", axis=0, tiled=True),
        lax.all_gather(shift_two, "shard", axis=0, tiled=True),
    )
    (
        query_w,
        query_b,
        key_w,
        value_w,
        value_b,
        output_w,
        output_b,
        gain_a,
        shift_a,
        inner_w,
        inner_b,
        outer_w,
        outer_b,
        gain_b,
        shift_b,
    ) = gathered
    gain_first = gain_a.astype(jnp.float32)
    shift_first = shift_a.astype(jnp.float32)
    gain_second = gain_b.astype(jnp.float32)
    shift_second = shift_b.astype(jnp.float32)
    flat_rows = inputs.reshape(local_seqs * tok_dev, model_width)
    queries = (product(flat_rows, query_w) + query_b.astype(jnp.float32)).astype(jnp.bfloat16)
    key_rows = product(flat_rows, key_w).astype(jnp.bfloat16)
    values = (product(flat_rows, value_w) + value_b.astype(jnp.float32)).astype(jnp.bfloat16)
    shape_seq = (local_seqs, tok_dev, model_width)
    head_q, head_k, head_v = (
        lax.all_to_all(queries.reshape(shape_seq), "seq", split_axis=2, concat_axis=1, tiled=True),
        lax.all_to_all(key_rows.reshape(shape_seq), "seq", split_axis=2, concat_axis=1, tiled=True),
        lax.all_to_all(values.reshape(shape_seq), "seq", split_axis=2, concat_axis=1, tiled=True),
    )
    seq_len = head_q.shape[1]
    split = (local_seqs, seq_len, local_heads, HEAD_DIM)
    head_q = head_q.reshape(split)
    head_k = head_k.reshape(split)
    head_v = head_v.reshape(split)

    def attend(packed):
        query_seq, key_seq, value_seq, length = packed
        logits = head_logits(query_seq, key_seq, length, factor)
        row_max = jnp.max(logits, axis=-1, keepdims=True)
        shifted = jnp.exp(logits - row_max)
        row_total = jnp.sum(shifted, axis=-1, keepdims=True)
        weights = (shifted / row_total).astype(jnp.bfloat16)
        context = jnp.einsum("hqk,khd->qhd", weights, value_seq, preferred_element_type=jnp.float32)
        return (context.astype(jnp.bfloat16), (row_max + jnp.log(row_total))[..., 0])

    head_context, log_total = lax.map(attend, (head_q, head_k, head_v, lengths))
    back_shape = (local_seqs, seq_len, head_width)
    context = lax.all_to_all(
        head_context.reshape(back_shape), "seq", split_axis=1, concat_axis=2, tiled=True
    ).reshape(-1, model_width)
    branch = product(context, output_w) + output_b.astype(jnp.float32)
    summed = flat_rows.astype(jnp.float32) + branch
    normed = layer_norm(summed, gain_first, shift_first)
    normed_low = normed.astype(jnp.bfloat16)
    pre_inner = product(normed_low, inner_w) + inner_b.astype(jnp.float32)
    activated = jax.nn.gelu(pre_inner, approximate=False).astype(jnp.bfloat16)
    final_sum = normed + product(activated, outer_w) + outer_b.astype(jnp.float32)
    result = layer_norm(final_sum, gain_second, shift_second)
    grad_out = cotangent.reshape(-1, model_width).astype(jnp.float32)
    second_back = jax.vjp(layer_norm, final_sum, gain_second, shift_second)[1]
    grad_final, grad_gain_two, grad_shift_two = second_back(grad_out)
    grad_ffn = grad_final.astype(jnp.bfloat16)
    grad_w_outer = row_contract(activated, grad_ffn)
    grad_b_outer = column_sum(grad_ffn)
    grad_active = times_transposed(grad_ffn, outer_w)
    gelu_back = jax.vjp(partial(jax.nn.gelu, approximate=False), pre_inner)[1]
    grad_pre = gelu_back(grad_active)[0].astype(jnp.bfloat16)
    grad_w_inner = row_contract(normed_low, grad_pre)
    grad_b_inner = column_sum(grad_pre)
    grad_normed = grad_final + times_transposed(grad_pre, inner_w)
    first_back = jax.vjp(layer_norm, summed, gain_first, shift_first)[1]
    grad_summed, grad_gain_one, grad_shift_one = first_back(grad_normed)
    grad_branch = grad_summed.astype(jnp.bfloat16)
    grad_w_output = row_contract(context, grad_branch)
    grad_b_output = column_sum(grad_branch)
    grad_context = times_transposed(grad_branch, output_w).astype(jnp.bfloat16)
    grad_head_context = lax.all_to_all(
        grad_context.reshape(shape_seq), "seq", split_axis=2, concat_axis=1, tiled=True
    ).reshape(split)

    def attend_back(packed):
        query_seq, key_seq, value_seq, log_sum, grad_seq, length = packed
        logits = head_logits(query_seq, key_seq, length, factor)
        attn_probs = jnp.exp(logits - log_sum[..., None])
        weights = attn_probs.astype(jnp.bfloat16)
        grad_value = jnp.einsum(
            "hqk,qhd->khd", weights, grad_seq, preferred_element_type=jnp.float32
        )
        grad_probs = jnp.einsum(
            "qhd,khd->hqk", grad_seq, value_seq, preferred_element_type=jnp.float32
        )
        inner_sum = jnp.sum(grad_probs * attn_probs, axis=-1, keepdims=True)
        grad_scores = (attn_probs * (grad_probs - inner_sum)).astype(jnp.bfloat16)
        grad_query = (
            jnp.einsum("hqk,khd->qhd", grad_scores, key_seq, preferred_element_type=jnp.float32)
            * factor
        )
        grad_key = (
            jnp.einsum("hqk,qhd->khd", grad_scores, query_seq, preferred_element_type=jnp.float32)
            * factor
        )
        return (
            grad_query.astype(jnp.bfloat16),
            grad_key.astype(jnp.bfloat16),
            grad_value.astype(jnp.bfloat16),
        )

    head_gq, head_gk, head_gv = lax.map(
        attend_back, (head_q, head_k, head_v, log_total, grad_head_context, lengths)
    )
    tok_gq, tok_gk, tok_gv = (
        lax.all_to_all(head_gq.reshape(back_shape), "seq", split_axis=1, concat_axis=2, tiled=True),
        lax.all_to_all(head_gk.reshape(back_shape), "seq", split_axis=1, concat_axis=2, tiled=True),
        lax.all_to_all(head_gv.reshape(back_shape), "seq", split_axis=1, concat_axis=2, tiled=True),
    )
    grad_query = tok_gq.reshape(-1, model_width)
    grad_key = tok_gk.reshape(-1, model_width)
    grad_value = tok_gv.reshape(-1, model_width)
    grad_w_query = row_contract(flat_rows, grad_query)
    grad_b_query = column_sum(grad_query)
    grad_w_key = row_contract(flat_rows, grad_key)
    grad_w_value = row_contract(flat_rows, grad_value)
    grad_b_value = column_sum(grad_value)
    grad_rows = (
        grad_summed
        + times_transposed(grad_query, query_w)
        + times_transposed(grad_key, key_w)
        + times_transposed(grad_value, value_w)
    )
    local_grads = (
        grad_w_query,
        grad_b_query,
        grad_w_key,
        grad_w_value,
        grad_b_value,
        grad_w_output,
        grad_b_output,
        grad_gain_one,
        grad_shift_one,
        grad_w_inner,
        grad_b_inner,
        grad_w_outer,
        grad_b_outer,
        grad_gain_two,
        grad_shift_two,
    )
    shares = (
        lax.psum_scatter(local_grads[0], "shard", scatter_dimension=0, tiled=True),
        lax.psum_scatter(local_grads[1], "shard", scatter_dimension=0, tiled=True),
        lax.psum_scatter(local_grads[2], "shard", scatter_dimension=0, tiled=True),
        lax.psum_scatter(local_grads[3], "shard", scatter_dimension=0, tiled=True),
        lax.psum_scatter(local_grads[4], "shard", scatter_dimension=0, tiled=True),
        lax.psum_scatter(local_grads[5], "shard", scatter_dimension=0, tiled=True),
        lax.psum_scatter(local_grads[6], "shard", scatter_dimension=0, tiled=True),
        lax.psum_scatter(local_grads[7], "shard", scatter_dimension=0, tiled=True),
        lax.psum_scatter(local_grads[8], "shard", scatter_dimension=0, tiled=True),
        lax.psum_scatter(local_grads[9], "shard", scatter_dimension=0, tiled=True),
        lax.psum_scatter(local_grads[10], "shard", scatter_dimension=0, tiled=True),
        lax.psum_scatter(local_grads[11], "shard", scatter_dimension=0, tiled=True),
        lax.psum_scatter(local_grads[12], "shard", scatter_dimension=0, tiled=True),
        lax.psum_scatter(local_grads[13], "shard", scatter_dimension=0, tiled=True),
        lax.psum_scatter(local_grads[14], "shard", scatter_dimension=0, tiled=True),
    )
    summed_grads = (
        lax.psum(shares[0].astype(jnp.bfloat16), "seq").astype(jnp.float32),
        lax.psum(shares[1].astype(jnp.bfloat16), "seq").astype(jnp.float32),
        lax.psum(shares[2].astype(jnp.bfloat16), "seq").astype(jnp.float32),
        lax.psum(shares[3].astype(jnp.bfloat16), "seq").astype(jnp.float32),
        lax.psum(shares[4].astype(jnp.bfloat16), "seq").astype(jnp.float32),
        lax.psum(shares[5].astype(jnp.bfloat16), "seq").astype(jnp.float32),
        lax.psum(shares[6].astype(jnp.bfloat16), "seq").astype(jnp.float32),
        lax.psum(shares[7].astype(jnp.bfloat16), "seq").astype(jnp.float32),
        lax.psum(shares[8].astype(jnp.bfloat16), "seq").astype(jnp.float32),
        lax.psum(shares[9].astype(jnp.bfloat16), "seq").astype(jnp.float32),
        lax.psum(shares[10].astype(jnp.bfloat16), "seq").astype(jnp.float32),
        lax.psum(shares[11].astype(jnp.bfloat16), "seq").astype(jnp.float32),
        lax.psum(shares[12].astype(jnp.bfloat16), "seq").astype(jnp.float32),
        lax.psum(shares[13].astype(jnp.bfloat16), "seq").astype(jnp.float32),
        lax.psum(shares[14].astype(jnp.bfloat16), "seq").astype(jnp.float32),
    )
    return (
        result.astype(jnp.bfloat16).reshape(shape_seq),
        grad_rows.reshape(shape_seq),
        summed_grads[0],
        summed_grads[1],
        summed_grads[2],
        summed_grads[3],
        summed_grads[4],
        summed_grads[5],
        summed_grads[6],
        summed_grads[7],
        summed_grads[8],
        summed_grads[9],
        summed_grads[10],
        summed_grads[11],
        summed_grads[12],
        summed_grads[13],
        summed_grads[14],
    )


def solution(mesh):
    tuned = (mesh.shape["shard"], mesh.shape["seq"]) == (8, 4)
    return jax.shard_map(
        per_device if tuned else per_device_plain,
        mesh=mesh,
        in_specs=(
            P("shard", "seq", None),
            P("shard"),
            P("shard", None),
            P("shard"),
            P("shard", None),
            P("shard", None),
            P("shard"),
            P("shard", None),
            P("shard"),
            P("shard"),
            P("shard"),
            P("shard", None),
            P("shard"),
            P("shard", None),
            P("shard"),
            P("shard"),
            P("shard"),
            P("shard", "seq", None),
        ),
        out_specs=(
            P("shard", "seq", None),
            P("shard", "seq", None),
            P("shard", None),
            P("shard"),
            P("shard", None),
            P("shard", None),
            P("shard"),
            P("shard", None),
            P("shard"),
            P("shard"),
            P("shard"),
            P("shard", None),
            P("shard"),
            P("shard", None),
            P("shard"),
            P("shard"),
            P("shard"),
        ),
        check_vma=False,
    )
```
